128 devices in a mesh: dx: 8 (over z, core), dy: 16 (over x, y).
Axes of the slice: x: 4, y: 4, z: 4, core: 2. Of those that a mesh axis runs over, the one named last changes fastest.
Arguments:
- orbitals: bfloat16 [112, 224, 13, 256], P('dx', 'dy'), may hold values from -6 to 6
- elem_mats: bfloat16 [16, 32, 2, 512, 512], P('dx', 'dy'), as said below
- conn: int32 [16, 32, 2, 512], P('dx', 'dy'), may hold values from 0 to 3374, as said below
Outputs:
- filtered: float32 [112, 224, 13, 256], P('dx', 'dy')
The draws below stay inside these ranges and needn't reach their ends.
Inputs may be any that keep to these rules, and one draw needn't show every extreme that they name: conn[e1, e2, e3, k] is ((7 (e1 mod 2) + a) (15) + 7 (e2 mod 2) + b) * 15 + 7 e3 + c for a node (a, b, c) of the element, 0 <= a, b, c <= 7, and each of the element's 512 nodes appears exactly once. `elem_mats`: each element's matrix is symmetric.
All inputs are finite; a program needn't handle non-finite values.
Results may differ from the reference program's by a relative error of at most 0.0059.
Values may be sent and summed in bfloat16 or wider, within the bound.
A program may use at most 128 MiB of HBM per device.

```python
import math
import jax
import jax.numpy as jnp
from jax import lax

BANDS = 256
DEG = 7
ESIDE = 2
EZ = 2
NPE = 512
NZO = 13
NZE = 15
NEX = 16
NEY = 32
NX = 112
NY = 224
N_DX = 8
N_DY = 16


def draw_conn(key, part):
    count = NEX * NEY * EZ
    keys = jax.random.split(jax.random.fold_in(key, 11), count)
    orders = jax.vmap(lambda single: jax.random.permutation(single, NPE))(keys).reshape(NEX, NEY, EZ, NPE)
    side = DEG + 1
    node_ids = jnp.arange(NPE, dtype=jnp.int32)
    first = node_ids // (side * side)
    second = node_ids // side % side
    third = node_ids % side
    along_x = (jnp.arange(NEX, dtype=jnp.int32) % ESIDE)[:, None, None, None]
    along_y = (jnp.arange(NEY, dtype=jnp.int32) % ESIDE)[None, :, None, None]
    along_z = jnp.arange(EZ, dtype=jnp.int32)[None, None, :, None]
    width = ESIDE * DEG + 1
    base = ((DEG * along_x + first) * width + DEG * along_y + second) * NZE + DEG * along_z + third
    base = jnp.broadcast_to(base, (NEX, NEY, EZ, NPE))
    return jnp.take_along_axis(base, orders.astype(jnp.int32), axis=3).astype(jnp.int32)


def draw_elem_mats(key, part):
    keys = jax.random.split(jax.random.fold_in(key, 5), NEX)

    def slab(single):
        noise_key, diag_key = jax.random.split(single, 2)
        noise = jax.random.normal(noise_key, (NEY, EZ, NPE, NPE), jnp.float32)
        matrix = (noise + jnp.swapaxes(noise, 2, 3)) * (1.0 / math.sqrt(2.0 * NPE))
        diagonal = jax.random.uniform(diag_key, (NEY, EZ, NPE), jnp.float32, 0.5, 2.5)
        matrix = matrix + diagonal[..., None] * jnp.eye(NPE, dtype=jnp.float32)
        return matrix.astype(jnp.bfloat16)
    return lax.map(slab, keys)


def steps_of(stream_key, dims, pieces, smallest, high):
    def one(axis_at, blocks):
        draws = jax.random.uniform(jax.random.fold_in(jax.random.fold_in(stream_key, 6), axis_at), (blocks,), jnp.float32, smallest / len(pieces), high / len(pieces))
        return jnp.repeat(jnp.exp(draws), dims[axis_at] // blocks).reshape((-1,) + (1,) * (len(dims) - axis_at - 1))

    gain = one(*pieces[0])
    for cut in pieces[1:]:
        gain = gain * one(*cut)
    return gain


def gaussian(key, shape, spread, most, cuts=(), kind=jnp.bfloat16):
    result = jax.random.normal(key, shape, jnp.float32) * spread
    if len(cuts) > 0:
        result = steps_of(key, shape, cuts, -0.22, 0.18) * result
    return jnp.clip(result, min=-most, max=most).astype(kind)


def setup_inputs(seed: int = 0) -> dict:
    streams_of = jax.random.split(jax.random.key(seed), 4)
    orbitals = gaussian(streams_of[0], (NX, NY, NZO, BANDS), 1.0, 6.0, ((0, 8), (1, 16)))
    elem_mats = draw_elem_mats(jax.random.fold_in(streams_of[3], 71), 0)
    conn = draw_conn(jax.random.fold_in(streams_of[3], 71), 0)
    return {"orbitals": orbitals, "elem_mats": elem_mats, "conn": conn}


filter_center = 1.5
filter_half = 4.0

def local_apply(block, mats_dev, conn_dev):
    rows = block[conn_dev]
    product = jnp.einsum('eij,ejb->eib', mats_dev.astype(jnp.float32), rows.astype(jnp.float32))
    summed = jnp.zeros((block.shape[0], block.shape[1]), jnp.float32)
    return summed.at[conn_dev.reshape(-1)].add(product.reshape(-1, block.shape[1]))

def apply_operator(field, elem_mats, conn):
    edge = ESIDE * DEG
    width = edge + 1
    padded = jnp.pad(field, ((1, 0), (1, 0), (1, 1), (0, 0)))
    start_sum = jnp.zeros(padded.shape, jnp.float32)

    def visit(index, summed):
        row = (index // N_DY).astype(jnp.int32)
        col = (index % N_DY).astype(jnp.int32)
        zero = jnp.zeros((), jnp.int32)
        start = (row * edge, col * edge, zero, zero)
        block = lax.dynamic_slice(padded, start, (width, width, NZE, BANDS)).reshape(-1, BANDS)
        mats_dev = lax.dynamic_slice(elem_mats, (row * ESIDE, col * ESIDE, zero, zero, zero), (ESIDE, ESIDE, EZ, NPE, NPE)).reshape(-1, NPE, NPE)
        conn_dev = lax.dynamic_slice(conn, (row * ESIDE, col * ESIDE, zero, zero), (ESIDE, ESIDE, EZ, NPE)).reshape(-1, NPE).astype(jnp.int32)
        piece = local_apply(block, mats_dev, conn_dev).reshape(width, width, NZE, BANDS)
        current = lax.dynamic_slice(summed, start, (width, width, NZE, BANDS))
        return lax.dynamic_update_slice(summed, current + piece, start)
    summed = lax.fori_loop(0, N_DX * N_DY, visit, start_sum)
    return summed[1:, 1:, 1:-1]

def reference(orbitals, elem_mats, conn):
    previous = orbitals.astype(jnp.float32)
    image = apply_operator(orbitals, elem_mats, conn)
    current = (image - filter_center * previous) / filter_half
    for turn in range(2):
        field = lax.optimization_barrier(current.astype(jnp.bfloat16))
        image = apply_operator(field, elem_mats, conn)
        following = 2.0 * (image - filter_center * current) / filter_half - previous
        previous, current = (current, following)
    matrix = current.reshape(-1, BANDS)
    basis, upper = jnp.linalg.qr(matrix)
    basis = basis * jnp.sign(jnp.diagonal(upper))[None, :]
    scale = math.sqrt(matrix.shape[0])
    return (basis * scale).reshape(current.shape)
```

```python
import math

import jax
import jax.numpy as jnp
from jax import lax
from jax.experimental import pallas as pl
from jax.experimental.pallas import tpu as pltpu
from jax.sharding import PartitionSpec as P

MESH = pl.DeviceIdType.MESH
F32 = jnp.float32
BF16 = jnp.bfloat16
NB = 256
HI = lax.Precision.HIGHEST


def dot_nn(a, b, precision=None):
    return lax.dot_general(
        a, b, (((1,), (0,)), ((), ())), precision=precision, preferred_element_type=F32
    )


def dot_nt(a, b, precision=None):
    return lax.dot_general(
        a, b, (((1,), (1,)), ((), ())), precision=precision, preferred_element_type=F32
    )


def dot_tn(a, b, precision=None):
    return lax.dot_general(
        a, b, (((0,), (0,)), ((), ())), precision=precision, preferred_element_type=F32
    )


def filter_kernel(
    ndx, ndy,
    orb, mats, conn,
    yout, gout,
    abuf, ap, rmap, st, tt, ya, yb, acc,
    hx, hy, hc, sxl, sxh, syl, syh, rxl, rxh, ryl, ryh, rcs,
    gl, ra, sb, rb, gb, gf,
    msem, ysem, hss, hrs, ess, ers, as_, ar_, bs_, br_, cs_, cr_, ds_, dr_,
):
    dx = lax.axis_index("dx")
    dy = lax.axis_index("dy")
    xp, xm = lax.rem(dx + 1, ndx), lax.rem(dx + ndx - 1, ndx)
    yp, ym = lax.rem(dy + 1, ndy), lax.rem(dy + ndy - 1, ndy)

    barrier = pltpu.get_barrier_semaphore()
    partners = [(lax.rem(dx + d, ndx), dy) for d in range(1, ndx)]
    partners += [(dx, lax.rem(dy + d, ndy)) for d in range(1, ndy)]
    partners += [(xp, yp), (xp, ym), (xm, yp), (xm, ym)]
    for partner in partners:
        pl.semaphore_signal(barrier, inc=1, device_id=partner, device_id_type=MESH)

    loads = []
    for e in range(8):
        copy = pltpu.make_async_copy(mats.at[e // 4, e // 2 % 2, e % 2], abuf.at[e], msem.at[e])
        copy.start()
        loads.append(copy)

    m = lax.broadcasted_iota(jnp.int32, (512, 128), 0)
    a_of, b_of, s_of = m // 64, m // 8 % 8, m % 8
    plane = a_of * 225 + b_of * 15
    rmap[0] = jnp.where(s_of < 7, plane + s_of + 1, -1)
    rmap[1] = jnp.where(s_of < 5, plane + s_of + 2, jnp.where(s_of > 5, plane + s_of - 6, -1))

    ya[...] = jnp.zeros_like(ya)

    def fill(i, carry):
        ya[i + 1, 1:15, 0:13, :] = orb[i].astype(F32)
        return carry

    lax.fori_loop(0, 14, fill, 0)

    def fold(c):
        ex, ey = c // 2, c % 2
        links = conn[ex, ey]
        for ez in range(2):
            e = c * 2 + ez
            loads[e].wait()
            row = links[ez : ez + 1] - ((7 * ex * 15 + 7 * ey) * 15 + 7 * ez)
            for q in range(4):
                part = row[:, 128 * q : 128 * q + 128]
                st[:, 128 * q : 128 * q + 128] = jnp.where(rmap[ez] == part, 1.0, 0.0).astype(BF16)
            tt[...] = dot_nt(abuf[e], st[...]).astype(BF16)
            ap[e] = dot_nn(st[...], tt[...]).astype(BF16)

    def remote(src, dst, ssem, rsem, where):
        copy = pltpu.make_async_remote_copy(
            src_ref=src, dst_ref=dst, send_sem=ssem, recv_sem=rsem, device_id=where, device_id_type=MESH
        )
        copy.start()
        return copy

    fold(0)
    pl.semaphore_wait(barrier, len(partners))
    halo = [
        remote(orb.at[13], hx, hss.at[0], hrs.at[0], (xp, dy)),
        remote(orb.at[:, 13], hy, hss.at[1], hrs.at[1], (dx, yp)),
        remote(orb.at[13, 13], hc, hss.at[2], hrs.at[2], (xp, yp)),
    ]
    for c in range(1, 4):
        fold(c)
    for copy in halo:
        copy.wait()
    x_low, x_high, y_low, y_high = dx > 0, dx < ndx - 1, dy > 0, dy < ndy - 1
    ya[0, 1:15, 0:13, :] = jnp.where(x_low, hx[...].astype(F32), 0.0)
    ya[1:15, 0, 0:13, :] = jnp.where(y_low, hy[...].astype(F32), 0.0)
    ya[0, 0, 0:13, :] = jnp.where(jnp.logical_and(x_low, y_low), hc[...].astype(F32), 0.0)

    sub = lax.broadcasted_iota(jnp.int32, (8, 8, 8, NB), 2)
    first = sub < 6

    def apply(src):
        acc[...] = jnp.zeros_like(acc)
        for c in range(4):
            i0, j0 = 7 * (c // 2), 7 * (c % 2)
            t0 = src[i0 : i0 + 8, j0 : j0 + 8, 0:8, :]
            t1 = jnp.where(first, src[i0 : i0 + 8, j0 : j0 + 8, 8:16, :], t0)
            p0 = dot_nn(ap[2 * c], t0.reshape(512, NB).astype(BF16)).reshape(8, 8, 8, NB)
            p1 = dot_nn(ap[2 * c + 1], t1.reshape(512, NB).astype(BF16)).reshape(8, 8, 8, NB)
            acc[i0 : i0 + 8, j0 : j0 + 8, 0:8, :] += p0 + jnp.where(first, 0.0, p1)
            acc[i0 : i0 + 8, j0 : j0 + 8, 8:16, :] += jnp.where(first, p1, 0.0)

    def exchange(t):
        copies = []
        sxl[t] = acc[0].astype(BF16)
        copies.append(remote(sxl.at[t], rxh.at[t], ess.at[t, 0], ers.at[t, 0], (xm, dy)))
        syl[t] = acc[:, 0].astype(BF16)
        copies.append(remote(syl.at[t], ryh.at[t], ess.at[t, 1], ers.at[t, 1], (dx, ym)))
        copies.append(remote(sxl.at[t, 0], rcs.at[t, 0], ess.at[t, 2], ers.at[t, 2], (xm, ym)))
        if t < 2:
            sxh[t] = acc[14].astype(BF16)
            copies.append(remote(sxh.at[t], rxl.at[t], ess.at[t, 3], ers.at[t, 3], (xp, dy)))
            syh[t] = acc[:, 14].astype(BF16)
            copies.append(remote(syh.at[t], ryl.at[t], ess.at[t, 4], ers.at[t, 4], (dx, yp)))
            copies.append(remote(sxh.at[t, 14], rcs.at[t, 1], ess.at[t, 5], ers.at[t, 5], (xp, yp)))
            copies.append(remote(sxl.at[t, 14], rcs.at[t, 2], ess.at[t, 6], ers.at[t, 6], (xm, yp)))
            copies.append(remote(sxh.at[t, 0], rcs.at[t, 3], ess.at[t, 7], ers.at[t, 7], (xp, ym)))
        return copies

    def gated(flag, ref, coef):
        return jnp.where(flag, ref.astype(F32), 0.0) * coef

    def faces(t, y, coef):
        y[14] += gated(x_high, rxh[t], coef)
        y[:, 14] += gated(y_high, ryh[t], coef)
        y[14, 14] += gated(jnp.logical_and(x_high, y_high), rcs[t, 0], coef)
        if t < 2:
            y[0] += rxl[t].astype(F32) * coef
            y[:, 0] += ryl[t].astype(F32) * coef
            y[0, 0] += rcs[t, 1].astype(F32) * coef
            y[14, 0] += gated(x_high, rcs[t, 2], coef)
            y[0, 14] += gated(y_high, rcs[t, 3], coef)
            y[0] = jnp.where(x_low, y[0], 0.0)
            y[:, 0] = jnp.where(y_low, y[:, 0], 0.0)

    apply(ya)
    copies = exchange(0)
    yb[...] = 0.25 * acc[...] - 0.375 * ya[...]
    for copy in copies:
        copy.wait()
    faces(0, yb, 0.25)

    apply(yb)
    copies = exchange(1)
    ya[...] = 0.5 * acc[...] - 0.75 * yb[...] - ya[...]
    for copy in copies:
        copy.wait()
    faces(1, ya, 0.5)

    apply(ya)
    copies = exchange(2)
    yb[...] = 0.5 * acc[...] - 0.75 * ya[...] - yb[...]
    for copy in copies:
        copy.wait()
    faces(2, yb, 0.5)

    keep = pltpu.make_async_copy(yb.at[1:15, 1:15], yout, ysem)
    keep.start()

    for h in range(2):
        total = None
        for i in range(7):
            y = yb[1 + 2 * i : 3 + 2 * i, 1:15].reshape(448, NB)
            top = y.astype(BF16)
            low = (y - top.astype(F32)).astype(BF16)
            term = dot_tn(top, low if h else top)
            total = term if total is None else total + term
        if h == 0:
            gl[...] = total.reshape(8, 32, NB)
        else:
            gl[...] += (total + total.T).reshape(8, 32, NB)

    copies = []
    for d in range(1, ndx):
        peer = lax.rem(dx + d, ndx)
        copies.append(remote(gl.at[peer], ra.at[dx], as_.at[d], ar_.at[d], (peer, dy)))
    for copy in copies:
        copy.wait()
    chunk = gl[dx]
    for d in range(1, ndx):
        chunk += ra[lax.rem(dx + d, ndx)]
    for p in range(16):
        sb[p] = chunk[p // 2 * 4 : p // 2 * 4 + 4, p % 2 * 128 : p % 2 * 128 + 128]
    copies = []
    for d in range(1, ndy):
        peer = lax.rem(dy + d, ndy)
        copies.append(remote(sb.at[peer], rb.at[dy], bs_.at[d], br_.at[d], (dx, peer)))
    for copy in copies:
        copy.wait()
    piece = sb[dy]
    for d in range(1, ndy):
        piece += rb[lax.rem(dy + d, ndy)]
    gb[dy] = piece
    copies = []
    for d in range(1, ndy):
        peer = lax.rem(dy + d, ndy)
        copies.append(remote(gb.at[dy], gb.at[dy], cs_.at[d], cr_.at[d], (dx, peer)))
    for copy in copies:
        copy.wait()
    for p in range(16):
        gf[dx, p // 2 * 4 : p // 2 * 4 + 4, p % 2 * 128 : p % 2 * 128 + 128] = gb[p]
    copies = []
    for d in range(1, ndx):
        peer = lax.rem(dx + d, ndx)
        copies.append(remote(gf.at[dx], gf.at[dx], ds_.at[d], dr_.at[d], (peer, dy)))
    for copy in copies:
        copy.wait()
    gout[...] = gf[...].reshape(NB, NB)
    keep.wait()


def eliminate(tiles, n):
    count = n // 8
    rows = lax.broadcasted_iota(jnp.int32, (8, n), 0)
    lanes = lax.broadcasted_iota(jnp.int32, (8, n), 1)
    inverse = [jnp.where(lanes == rows + 8 * r, 1.0, 0.0) for r in range(count)]
    pivots = [jnp.ones((8, n), F32) for _ in range(count)]
    for k in range(n):
        r, j = k // 8, k % 8
        row = jnp.broadcast_to(tiles[r][j : j + 1, :], (8, n))
        pivot = jnp.broadcast_to(row[:, k : k + 1], (8, n))
        pivots[r] = jnp.where(rows == j, pivot, pivots[r])
        factor = 1.0 / pivot
        row = row * factor
        back = jnp.broadcast_to(inverse[r][j : j + 1, :], (8, n)) * factor
        for q in range(r, count):
            if q == r and j == 7:
                continue
            column = jnp.broadcast_to(tiles[q][:, k : k + 1], (8, n))
            if q == r:
                column = jnp.where(rows > j, column, 0.0)
            tiles[q] = tiles[q] - column * row
            inverse[q] = inverse[q] - column * back
    return jnp.concatenate([w * lax.rsqrt(p) for w, p in zip(inverse, pivots)], axis=0)


def basis_kernel(scale, y, g, out, ybuf, stage, whi, wlo, yin, osem):
    load = pltpu.make_async_copy(y, ybuf, yin)
    load.start()
    h = 128
    w1 = eliminate([g[8 * r : 8 * r + 8, 0:h] for r in range(16)], h)
    l21 = dot_nt(g[h:, 0:h], w1, HI)
    schur = g[h:, h:] - dot_nt(l21, l21, HI)
    mid = dot_nn(l21, w1, HI)
    w2 = eliminate([schur[8 * r : 8 * r + 8] for r in range(16)], h)
    w21 = -dot_nn(w2, mid, HI)

    def split(block, rows, cols):
        block = block * scale
        top = block.astype(BF16)
        whi[rows, cols] = top
        wlo[rows, cols] = (block - top.astype(F32)).astype(BF16)

    split(w1, slice(0, h), slice(0, h))
    split(jnp.zeros((h, h), F32), slice(0, h), slice(h, NB))
    split(w21, slice(h, NB), slice(0, h))
    split(w2, slice(h, NB), slice(h, NB))
    load.wait()
    copies = []
    for i in range(14):
        rows = ybuf[i].reshape(224, NB)
        top = rows.astype(BF16)
        low = (rows - top.astype(F32)).astype(BF16)
        q = dot_nt(top, whi[...]) + (dot_nt(top, wlo[...]) + dot_nt(low, whi[...]))
        stage[i] = q.reshape(14, 16, NB)[:, 0:13, :]
        copy = pltpu.make_async_copy(stage.at[i], out.at[i], osem.at[i])
        copy.start()
        copies.append(copy)
    for copy in copies:
        copy.wait()


def solution(mesh):
    ndx, ndy = mesh.shape["dx"], mesh.shape["dy"]
    vmem = pl.BlockSpec(memory_space=pltpu.VMEM)
    anywhere = pl.BlockSpec(memory_space=pl.ANY)
    scale = math.sqrt(14 * 14 * 13 * ndx * ndy)

    def shards(orbitals, elem_mats, conn):
        dma = pltpu.SemaphoreType.DMA
        y, g = pl.pallas_call(
            lambda *refs: filter_kernel(ndx, ndy, *refs),
            out_shape=(
                jax.ShapeDtypeStruct((14, 14, 16, NB), F32),
                jax.ShapeDtypeStruct((NB, NB), F32),
            ),
            in_specs=[vmem, anywhere, vmem],
            out_specs=(anywhere, vmem),
            scratch_shapes=[
                pltpu.VMEM((8, 512, 512), BF16),
                pltpu.VMEM((8, 512, 512), BF16),
                pltpu.VMEM((2, 512, 128), jnp.int32),
                pltpu.VMEM((512, 512), BF16),
                pltpu.VMEM((512, 512), BF16),
                pltpu.VMEM((15, 15, 16, NB), F32),
                pltpu.VMEM((15, 15, 16, NB), F32),
                pltpu.VMEM((15, 15, 16, NB), F32),
                pltpu.VMEM((14, 13, NB), BF16),
                pltpu.VMEM((14, 13, NB), BF16),
                pltpu.VMEM((13, NB), BF16),
                pltpu.VMEM((3, 15, 16, NB), BF16),
                pltpu.VMEM((2, 15, 16, NB), BF16),
                pltpu.VMEM((3, 15, 16, NB), BF16),
                pltpu.VMEM((2, 15, 16, NB), BF16),
                pltpu.VMEM((2, 15, 16, NB), BF16),
                pltpu.VMEM((3, 15, 16, NB), BF16),
                pltpu.VMEM((2, 15, 16, NB), BF16),
                pltpu.VMEM((3, 15, 16, NB), BF16),
                pltpu.VMEM((3, 4, 16, NB), BF16),
                pltpu.VMEM((8, 32, NB), F32),
                pltpu.VMEM((8, 32, NB), F32),
                pltpu.VMEM((16, 4, 128), F32),
                pltpu.VMEM((16, 4, 128), F32),
                pltpu.VMEM((16, 4, 128), F32),
                pltpu.VMEM((8, 32, NB), F32),
                dma((8,)),
                dma,
                dma((3,)),
                dma((3,)),
                dma((3, 8)),
                dma((3, 8)),
                dma((8,)),
                dma((8,)),
                dma((16,)),
                dma((16,)),
                dma((16,)),
                dma((16,)),
                dma((8,)),
                dma((8,)),
            ],
            compiler_params=pltpu.CompilerParams(collective_id=0, has_side_effects=True),
            name="filter",
        )(orbitals, elem_mats, conn)
        return pl.pallas_call(
            lambda *refs: basis_kernel(scale, *refs),
            out_shape=jax.ShapeDtypeStruct((14, 14, 13, NB), F32),
            in_specs=[anywhere, vmem],
            out_specs=anywhere,
            scratch_shapes=[
                pltpu.VMEM((14, 14, 16, NB), F32),
                pltpu.VMEM((14, 14, 13, NB), F32),
                pltpu.VMEM((NB, NB), BF16),
                pltpu.VMEM((NB, NB), BF16),
                dma,
                dma((14,)),
            ],
            name="basis",
        )(y, g)

    in_specs = (
        P("dx", "dy", None, None),
        P("dx", "dy", None, None, None),
        P("dx", "dy", None, None),
    )
    out_specs = P("dx", "dy", None, None)
    return jax.shard_map(shards, mesh=mesh, in_specs=in_specs, out_specs=out_specs, check_vma=False)
```

```python
import math

import jax
import jax.numpy as jnp
from jax import lax
from jax.experimental import pallas as pl
from jax.experimental.pallas import tpu as pltpu
from jax.sharding import PartitionSpec as P

MESH = pl.DeviceIdType.MESH
F32 = jnp.float32
BF16 = jnp.bfloat16
NB = 256


def dot_nn(a, b, precision=None):
    return lax.dot_general(
        a, b, (((1,), (0,)), ((), ())), precision=precision, preferred_element_type=F32
    )


def dot_nt(a, b, precision=None):
    return lax.dot_general(
        a, b, (((1,), (1,)), ((), ())), precision=precision, preferred_element_type=F32
    )


def dot_tn(a, b, precision=None):
    return lax.dot_general(
        a, b, (((0,), (0,)), ((), ())), precision=precision, preferred_element_type=F32
    )


def filter_kernel(
    ndx, ndy,
    orb, mats, conn,
    yout, gout,
    abuf, ap, rmap, st, tt, ya2, yb2, acc2, both,
    hx, hy, hc, shy, shc, sxl, sxh, syl, syh, scs, rxl, rxh, ryl, ryh, rcs,
    gl, ra, sb, rb, gb, gf,
    msem, ysem, hss, hrs, ess, ers, as_, ar_, bs_, br_, cs_, cr_, ds_, dr_,
):
    dx = lax.axis_index("dx")
    dy = lax.axis_index("dy")
    xp, xm = lax.rem(dx + 1, ndx), lax.rem(dx + ndx - 1, ndx)
    yp, ym = lax.rem(dy + 1, ndy), lax.rem(dy + ndy - 1, ndy)
    ya, yb, acc = (ref.reshape(2, 15, 13, 16, 128) for ref in (ya2, yb2, acc2))

    barrier = pltpu.get_barrier_semaphore()
    partners = [(lax.rem(dx + d, ndx), dy) for d in range(1, ndx)]
    partners += [(dx, lax.rem(dy + d, ndy)) for d in range(1, ndy)]
    partners += [(xp, yp), (xp, ym), (xm, yp), (xm, ym)]
    for partner in partners:
        pl.semaphore_signal(barrier, inc=1, device_id=partner, device_id_type=MESH)

    loads = []
    for e in range(8):
        copy = pltpu.make_async_copy(mats.at[e // 4, e // 2 % 2, e % 2], abuf.at[e], msem.at[e])
        copy.start()
        loads.append(copy)

    grid = (8, 7, 8, 128)
    a_of, l_of, s_of = (lax.broadcasted_iota(jnp.int32, grid, d) for d in range(3))
    for ey in range(2):
        b_of = jnp.where(s_of < 7 - ey, s_of + 1 + ey, s_of - 7 + ey)
        rmap[ey] = (a_of * 225 + b_of * 15 + l_of).reshape(448, 128)

    ya2[...] = jnp.zeros_like(ya2)

    def fill(i, carry):
        plane = orb[i].astype(F32)
        for h in range(2):
            ya[h, i + 1, :, 0:14, :] = plane[:, :, 128 * h : 128 * h + 128]
        return carry

    lax.fori_loop(0, 14, fill, 0)

    def line(i, slot, count):
        return pl.ds(i * 208 + slot, 13 * count, stride=16)

    for h in range(2):
        shy[h] = ya2[h, line(1, 13, 14), :].astype(BF16)
        shc[h] = ya2[h, line(14, 13, 1), :].astype(BF16)

    def fold(c):
        ex, ey = c // 2, c % 2
        links = conn[ex, ey]
        for ez in range(2):
            e = c * 2 + ez
            loads[e].wait()
            row = links[ez : ez + 1] - ((7 * ex * 15 + 7 * ey) * 15 + 7 * ez + 1 - ez)
            for q in range(4):
                part = row[:, 128 * q : 128 * q + 128]
                st[:, 128 * q : 128 * q + 128] = jnp.where(rmap[ey] == part, 1.0, 0.0).astype(BF16)
            tt[...] = dot_nt(abuf[e], st[...]).astype(BF16)
            ap[e] = dot_nn(st[...], tt[...]).astype(BF16)

    def remote(src, dst, ssem, rsem, where):
        copy = pltpu.make_async_remote_copy(
            src_ref=src, dst_ref=dst, send_sem=ssem, recv_sem=rsem, device_id=where, device_id_type=MESH
        )
        copy.start()
        return copy

    fold(0)
    pl.semaphore_wait(barrier, len(partners))
    halo = [
        remote(orb.at[13], hx, hss.at[0], hrs.at[0], (xp, dy)),
        remote(shy, hy, hss.at[1], hrs.at[1], (dx, yp)),
        remote(shc, hc, hss.at[2], hrs.at[2], (xp, yp)),
    ]
    for c in range(1, 4):
        fold(c)
    for copy in halo:
        copy.wait()
    x_low, x_high, y_low, y_high = dx > 0, dx < ndx - 1, dy > 0, dy < ndy - 1
    plane = jnp.where(x_low, hx[...].astype(F32), 0.0)
    for h in range(2):
        ya[h, 0, :, 0:14, :] = plane[:, :, 128 * h : 128 * h + 128]
        ya2[h, line(1, 15, 14), :] = jnp.where(y_low, hy[h].astype(F32), 0.0)
        ya2[h, line(0, 15, 1), :] = jnp.where(
            jnp.logical_and(x_low, y_low), hc[h].astype(F32), 0.0
        )

    sub = lax.broadcasted_iota(jnp.int32, (8, 7, 8, 128), 2)

    def apply(src):
        acc2[...] = jnp.zeros_like(acc2)
        for ex in range(2):
            for ez in range(2):
                box = (slice(7 * ex, 7 * ex + 8), slice(6 * ez, 6 * ez + 7))
                t0, t1 = [], []
                for h in range(2):
                    n0 = src[(h, *box, slice(0, 8))]
                    n1 = src[(h, *box, slice(8, 16))]
                    t0.append(jnp.where(sub < 7, n0, n1).reshape(448, 128).astype(BF16))
                    t1.append(jnp.where(sub < 6, n1, n0).reshape(448, 128).astype(BF16))
                q0 = dot_nn(ap[4 * ex + ez], jnp.concatenate(t0, axis=1))
                q1 = dot_nn(ap[4 * ex + 2 + ez], jnp.concatenate(t1, axis=1))
                for h in range(2):
                    p0, p1 = (
                        q[:, 128 * h : 128 * h + 128].reshape(8, 7, 8, 128) for q in (q0, q1)
                    )
                    acc[(h, *box, slice(0, 8))] += jnp.where(sub < 7, p0, 0.0) + jnp.where(
                        sub < 6, 0.0, p1
                    )
                    acc[(h, *box, slice(8, 16))] += jnp.where(sub < 6, p1, 0.0) + jnp.where(
                        sub < 7, 0.0, p0
                    )

    def exchange(t):
        copies = []
        for h in range(2):
            syl[t, h] = acc2[h, line(0, 15, 15), :].astype(BF16)
        copies.append(remote(syl.at[t], ryh.at[t], ess.at[t, 1], ers.at[t, 1], (dx, ym)))
        if t < 2:
            for h in range(2):
                syh[t, h] = acc2[h, line(0, 13, 15), :].astype(BF16)
            copies.append(remote(syh.at[t], ryl.at[t], ess.at[t, 4], ers.at[t, 4], (dx, yp)))
        sxl[t] = acc[:, 0].astype(BF16)
        copies.append(remote(sxl.at[t], rxh.at[t], ess.at[t, 0], ers.at[t, 0], (xm, dy)))
        if t < 2:
            sxh[t] = acc[:, 14].astype(BF16)
            copies.append(remote(sxh.at[t], rxl.at[t], ess.at[t, 3], ers.at[t, 3], (xp, dy)))
        corners = [(0, 15, (xm, ym)), (14, 13, (xp, yp)), (0, 13, (xm, yp)), (14, 15, (xp, ym))]
        for n, (i, slot, where) in enumerate(corners[: 4 if t < 2 else 1]):
            for h in range(2):
                scs[t, n, h] = acc2[h, line(i, slot, 1), :].astype(BF16)
            copies.append(remote(scs.at[t, n], rcs.at[t, n], ess.at[t, 5 + n], ers.at[t, 5 + n], where))
        return copies

    def gated(flag, value, coef):
        return jnp.where(flag, value.astype(F32), 0.0) * coef

    def faces(t, y, y2, coef):
        def bump(i, slot, count, value):
            for h in range(2):
                y2[h, line(i, slot, count), :] += value[h]

        y[:, 14] += gated(x_high, rxh[t], coef)
        bump(0, 13, 15, gated(y_high, ryh[t], coef))
        bump(14, 13, 1, gated(jnp.logical_and(x_high, y_high), rcs[t, 0], coef))
        if t < 2:
            y[:, 0] += rxl[t].astype(F32) * coef
            bump(0, 15, 15, ryl[t].astype(F32) * coef)
            bump(0, 15, 1, rcs[t, 1].astype(F32) * coef)
            bump(14, 15, 1, gated(x_high, rcs[t, 2], coef))
            bump(0, 13, 1, gated(y_high, rcs[t, 3], coef))
            y[:, 0] = jnp.where(x_low, y[:, 0], 0.0)
            for h in range(2):
                edge = y2[h, line(0, 15, 15), :]
                y2[h, line(0, 15, 15), :] = jnp.where(y_low, edge, 0.0)

    apply(ya)
    copies = exchange(0)
    yb2[...] = 0.25 * acc2[...] - 0.375 * ya2[...]
    for copy in copies:
        copy.wait()
    faces(0, yb, yb2, 0.25)

    apply(yb)
    copies = exchange(1)
    ya2[...] = 0.5 * acc2[...] - 0.75 * yb2[...] - ya2[...]
    for copy in copies:
        copy.wait()
    faces(1, ya, ya2, 0.5)

    apply(ya)
    copies = exchange(2)
    yb2[...] = 0.5 * acc2[...] - 0.75 * ya2[...] - yb2[...]
    for copy in copies:
        copy.wait()
    faces(2, yb, yb2, 0.5)
    for h in range(2):
        yb2[h, line(0, 15, 15), :] = jnp.zeros((195, 128), F32)

    for h in range(2):
        y = yb2[h, 208:3120, :]
        top = y.astype(BF16)
        both[:, 128 * h : 128 * h + 128] = top
        both[:, NB + 128 * h : NB + 128 * h + 128] = (y - top.astype(F32)).astype(BF16)
    keep = pltpu.make_async_copy(both, yout, ysem)
    keep.start()
    total = dot_tn(both[:, 0:NB], both[...])
    cross = total[:, NB:]
    gl[...] = (total[:, 0:NB] + (cross + cross.T)).reshape(8, 32, NB)

    copies = []
    for d in range(1, ndx):
        peer = lax.rem(dx + d, ndx)
        copies.append(remote(gl.at[peer], ra.at[dx], as_.at[d], ar_.at[d], (peer, dy)))
    for copy in copies:
        copy.wait()
    chunk = gl[dx]
    for d in range(1, ndx):
        chunk += ra[lax.rem(dx + d, ndx)]
    for p in range(16):
        sb[p] = chunk[p // 2 * 4 : p // 2 * 4 + 4, p % 2 * 128 : p % 2 * 128 + 128]
    copies = []
    for d in range(1, ndy):
        peer = lax.rem(dy + d, ndy)
        copies.append(remote(sb.at[peer], rb.at[dy], bs_.at[d], br_.at[d], (dx, peer)))
    for copy in copies:
        copy.wait()
    piece = sb[dy]
    for d in range(1, ndy):
        piece += rb[lax.rem(dy + d, ndy)]
    gb[dy] = piece
    copies = []
    for d in range(1, ndy):
        peer = lax.rem(dy + d, ndy)
        copies.append(remote(gb.at[dy], gb.at[dy], cs_.at[d], cr_.at[d], (dx, peer)))
    for copy in copies:
        copy.wait()
    for p in range(16):
        gf[dx, p // 2 * 4 : p // 2 * 4 + 4, p % 2 * 128 : p % 2 * 128 + 128] = gb[p]
    copies = []
    for d in range(1, ndx):
        peer = lax.rem(dx + d, ndx)
        copies.append(remote(gf.at[dx], gf.at[dx], ds_.at[d], dr_.at[d], (peer, dy)))
    for copy in copies:
        copy.wait()
    gout[...] = gf[...].reshape(NB, NB)
    keep.wait()


def split3(x):
    a = x.astype(BF16)
    rest = x - a.astype(F32)
    b = rest.astype(BF16)
    return a, b, (rest - b.astype(F32)).astype(BF16)


def factor_inverse(g, work):
    rows = lax.broadcasted_iota(jnp.int32, (8, 128), 0)
    lanes = lax.broadcasted_iota(jnp.int32, (8, 128), 1)
    scales = []
    for o in range(8):
        base = 32 * o
        source = g if o == 0 else work
        tiles = [
            [source[base + 8 * t : base + 8 * t + 8, 128 * h : 128 * h + 128] for h in range(2)]
            for t in range(4)
        ]
        factors = []
        half = base // 128
        for s in range(4):
            first = base + 8 * s - 128 * half
            inside = jnp.logical_and(lanes >= first, lanes < first + 8)
            columns = []
            for q in range(s, 4):
                tile = tiles[q][half]
                columns.append(
                    [jnp.broadcast_to(tile[:, first + j : first + j + 1], (8, 128)) for j in range(8)]
                )
                fresh = jnp.where(lanes == rows + first, 1.0, 0.0) if q == s else 0.0
                tiles[q][half] = jnp.where(inside, fresh, tile)
            scale = jnp.ones((8, 128), F32)
            factor = jnp.ones((8, 128), F32)
            for k in range(8):
                lead = [jnp.broadcast_to(columns[0][j][k : k + 1, :], (8, 128)) for j in range(k, 8)]
                inv = 1.0 / lead[0]
                scale = jnp.where(rows == k, lead[0], scale)
                factor = jnp.where(rows == k, inv, factor)
                pivot = [jnp.broadcast_to(tiles[s][h][k : k + 1, :], (8, 128)) * inv for h in range(2)]
                lead = [v * inv for v in lead]
                for q in range(s, 4):
                    if q == s and k == 7:
                        continue
                    column = columns[q - s][k]
                    if q == s:
                        column = jnp.where(rows > k, column, 0.0)
                    for j in range(k + 1, 8):
                        columns[q - s][j] = columns[q - s][j] - column * lead[j - k]
                    for h in range(2):
                        tiles[q][h] = tiles[q][h] - column * pivot[h]
            scales.append(lax.rsqrt(scale))
            factors.append(factor)
        for t in range(4):
            for h in range(2):
                work[base + 8 * t : base + 8 * t + 8, 128 * h : 128 * h + 128] = tiles[t][h]
        if o < 7:
            u = jnp.concatenate([jnp.concatenate(tiles[t], axis=1) for t in range(4)], axis=0)
            f = jnp.concatenate([jnp.concatenate([v, v], axis=1) for v in factors], axis=0)
            r = lax.broadcasted_iota(jnp.int32, (32, NB), 0) + base
            c = lax.broadcasted_iota(jnp.int32, (32, NB), 1)
            v = jnp.where(jnp.logical_and(c > r, c < base + 32), 0.0, u * f)
            start = 128 * ((base + 32) // 128)
            u1, u2, u3 = split3(u[:, start:])
            v1, v2, v3 = split3(v)
            left = jnp.concatenate([u1, u1, u1, u2, u2, u3], axis=0)
            right = jnp.concatenate([v1, v2, v3, v1, v2, v1], axis=0)
            change = lax.dot_general(
                left, right, (((0,), (0,)), ((), ())), preferred_element_type=F32
            )
            rest = slice(base + 32, NB)
            old = (g if o == 0 else work)[rest, :]
            cc = lax.broadcasted_iota(jnp.int32, old.shape, 1)
            old = jnp.where(jnp.logical_and(cc >= base, cc < base + 32), 0.0, old)
            work[rest, :] = old - change[base + 32 - start :, :]
    for t in range(32):
        for h in range(2):
            tile = work[8 * t : 8 * t + 8, 128 * h : 128 * h + 128] * scales[t]
            work[8 * t : 8 * t + 8, 128 * h : 128 * h + 128] = jnp.where(
                lanes + 128 * h <= rows + 8 * t, tile, 0.0
            )


def basis_kernel(scale, y, g, out, ybuf, stage, work, whh, wlo, yin, osem):
    load = pltpu.make_async_copy(y, ybuf, yin)
    load.start()
    factor_inverse(g, work)
    w = work[...] * scale
    top = w.astype(BF16)
    whh[:, 0:NB] = top
    whh[:, NB:] = top
    wlo[...] = (w - top.astype(F32)).astype(BF16)
    load.wait()
    copies = []
    for i in range(14):
        rows = slice(208 * i, 208 * i + 208)
        q = dot_nt(ybuf[rows, :], whh[...]) + dot_nt(ybuf[rows, 0:NB], wlo[...])
        stage[i] = q.reshape(13, 16, NB)[:, 0:14, :]
        copy = pltpu.make_async_copy(stage.at[i], out.at[i], osem.at[i])
        copy.start()
        copies.append(copy)
    for copy in copies:
        copy.wait()


def solution(mesh):
    ndx, ndy = mesh.shape["dx"], mesh.shape["dy"]
    vmem = pl.BlockSpec(memory_space=pltpu.VMEM)
    anywhere = pl.BlockSpec(memory_space=pl.ANY)
    scale = math.sqrt(14 * 14 * 13 * ndx * ndy)

    def shards(orbitals, elem_mats, conn):
        dma = pltpu.SemaphoreType.DMA
        y, g = pl.pallas_call(
            lambda *refs: filter_kernel(ndx, ndy, *refs),
            out_shape=(
                jax.ShapeDtypeStruct((2912, 2 * NB), BF16),
                jax.ShapeDtypeStruct((NB, NB), F32),
            ),
            in_specs=[vmem, anywhere, vmem],
            out_specs=(anywhere, vmem),
            scratch_shapes=[
                pltpu.VMEM((8, 512, 512), BF16),
                pltpu.VMEM((8, 448, 448), BF16),
                pltpu.VMEM((2, 448, 128), jnp.int32),
                pltpu.VMEM((448, 512), BF16),
                pltpu.VMEM((512, 448), BF16),
                pltpu.VMEM((2, 3120, 128), F32),
                pltpu.VMEM((2, 3120, 128), F32),
                pltpu.VMEM((2, 3120, 128), F32),
                pltpu.VMEM((2912, 2 * NB), BF16),
                pltpu.VMEM((13, 14, NB), BF16),
                pltpu.VMEM((2, 182, 128), BF16),
                pltpu.VMEM((2, 13, 128), BF16),
                pltpu.VMEM((2, 182, 128), BF16),
                pltpu.VMEM((2, 13, 128), BF16),
                pltpu.VMEM((3, 2, 13, 16, 128), BF16),
                pltpu.VMEM((2, 2, 13, 16, 128), BF16),
                pltpu.VMEM((3, 2, 195, 128), BF16),
                pltpu.VMEM((2, 2, 195, 128), BF16),
                pltpu.VMEM((3, 4, 2, 13, 128), BF16),
                pltpu.VMEM((2, 2, 13, 16, 128), BF16),
                pltpu.VMEM((3, 2, 13, 16, 128), BF16),
                pltpu.VMEM((2, 2, 195, 128), BF16),
                pltpu.VMEM((3, 2, 195, 128), BF16),
                pltpu.VMEM((3, 4, 2, 13, 128), BF16),
                pltpu.VMEM((8, 32, NB), F32),
                pltpu.VMEM((8, 32, NB), F32),
                pltpu.VMEM((16, 4, 128), F32),
                pltpu.VMEM((16, 4, 128), F32),
                pltpu.VMEM((16, 4, 128), F32),
                pltpu.VMEM((8, 32, NB), F32),
                dma((8,)),
                dma,
                dma((3,)),
                dma((3,)),
                dma((3, 9)),
                dma((3, 9)),
                dma((8,)),
                dma((8,)),
                dma((16,)),
                dma((16,)),
                dma((16,)),
                dma((16,)),
                dma((8,)),
                dma((8,)),
            ],
            compiler_params=pltpu.CompilerParams(collective_id=0, has_side_effects=True),
            name="filter",
        )(jnp.swapaxes(orbitals, 1, 2), elem_mats, conn)
        filtered = pl.pallas_call(
            lambda *refs: basis_kernel(scale, *refs),
            out_shape=jax.ShapeDtypeStruct((14, 13, 14, NB), F32),
            in_specs=[anywhere, vmem],
            out_specs=anywhere,
            scratch_shapes=[
                pltpu.VMEM((2912, 2 * NB), BF16),
                pltpu.VMEM((14, 13, 14, NB), F32),
                pltpu.VMEM((NB, NB), F32),
                pltpu.VMEM((NB, 2 * NB), BF16),
                pltpu.VMEM((NB, NB), BF16),
                dma,
                dma((14,)),
            ],
            name="basis",
        )(y, g)
        return jnp.swapaxes(filtered, 1, 2)

    in_specs = (
        P("dx", "dy", None, None),
        P("dx", "dy", None, None, None),
        P("dx", "dy", None, None),
    )
    out_specs = P("dx", "dy", None, None)
    return jax.shard_map(shards, mesh=mesh, in_specs=in_specs, out_specs=out_specs, check_vma=False)
```

```python
import math

import jax
import jax.numpy as jnp
from jax import lax
from jax.experimental import pallas as pl
from jax.experimental.pallas import tpu as pltpu
from jax.sharding import PartitionSpec as P

MESH = pl.DeviceIdType.MESH
F32 = jnp.float32
BF16 = jnp.bfloat16
NB = 256


def dot_nn(a, b, precision=None):
    return lax.dot_general(
        a, b, (((1,), (0,)), ((), ())), precision=precision, preferred_element_type=F32
    )


def dot_nt(a, b, precision=None):
    return lax.dot_general(
        a, b, (((1,), (1,)), ((), ())), precision=precision, preferred_element_type=F32
    )


def dot_tn(a, b, precision=None):
    return lax.dot_general(
        a, b, (((0,), (0,)), ((), ())), precision=precision, preferred_element_type=F32
    )


def filter_kernel(
    ndx, ndy,
    orb, mats, conn,
    yout, gout,
    abuf, ap, rmap, st, tt, ya2, yb2, acc2, both,
    hx, hy, hc, shy, shc, sxl, sxh, syl, syh, scs, rxl, rxh, ryl, ryh, rcs,
    gl, ra, sb, rb, gb, gf,
    msem, ysem, hss, hrs, ess, ers, as_, ar_, bs_, br_, cs_, cr_, ds_, dr_,
):
    dx = lax.axis_index("dx")
    dy = lax.axis_index("dy")
    xp, xm = lax.rem(dx + 1, ndx), lax.rem(dx + ndx - 1, ndx)
    yp, ym = lax.rem(dy + 1, ndy), lax.rem(dy + ndy - 1, ndy)
    ya, yb, acc = (ref.reshape(2, 15, 13, 16, 128) for ref in (ya2, yb2, acc2))

    barrier = pltpu.get_barrier_semaphore()
    partners = [(lax.rem(dx + d, ndx), dy) for d in range(1, ndx)]
    partners += [(dx, lax.rem(dy + d, ndy)) for d in range(1, ndy)]
    partners += [(xp, yp), (xp, ym), (xm, yp), (xm, ym)]
    for partner in partners:
        pl.semaphore_signal(barrier, inc=1, device_id=partner, device_id_type=MESH)

    loads = []
    for e in range(8):
        copy = pltpu.make_async_copy(mats.at[e // 4, e // 2 % 2, e % 2], abuf.at[e], msem.at[e])
        copy.start()
        loads.append(copy)

    grid = (8, 7, 8, 128)
    a_of, l_of, s_of = (lax.broadcasted_iota(jnp.int32, grid, d) for d in range(3))
    for ey in range(2):
        b_of = jnp.where(s_of < 7 - ey, s_of + 1 + ey, s_of - 7 + ey)
        rmap[ey] = (a_of * 225 + b_of * 15 + l_of).reshape(448, 128)

    ya2[...] = jnp.zeros_like(ya2)

    def fill(i, carry):
        plane = orb[i].astype(F32)
        for h in range(2):
            ya[h, i + 1, :, 0:14, :] = plane[:, :, 128 * h : 128 * h + 128]
        return carry

    lax.fori_loop(0, 14, fill, 0)

    def line(i, slot, count):
        return pl.ds(i * 208 + slot, 13 * count, stride=16)

    for h in range(2):
        shy[h] = ya2[h, line(1, 13, 14), :].astype(BF16)
        shc[h] = ya2[h, line(14, 13, 1), :].astype(BF16)

    def fold(c):
        ex, ey = c // 2, c % 2
        links = conn[ex, ey]
        for ez in range(2):
            e = c * 2 + ez
            loads[e].wait()
            row = links[ez : ez + 1] - ((7 * ex * 15 + 7 * ey) * 15 + 7 * ez + 1 - ez)
            for q in range(4):
                part = row[:, 128 * q : 128 * q + 128]
                st[:, 128 * q : 128 * q + 128] = jnp.where(rmap[ey] == part, 1.0, 0.0).astype(BF16)
            tt[...] = dot_nt(abuf[e], st[...]).astype(BF16)
            ap[e] = dot_nn(st[...], tt[...]).astype(BF16)

    def remote(src, dst, ssem, rsem, where):
        copy = pltpu.make_async_remote_copy(
            src_ref=src, dst_ref=dst, send_sem=ssem, recv_sem=rsem, device_id=where, device_id_type=MESH
        )
        copy.start()
        return copy

    fold(0)
    pl.semaphore_wait(barrier, len(partners))
    halo = []
    for h in range(2):
        half = orb.at[13, :, :, 128 * h : 128 * h + 128]
        halo.append(
            [
                remote(shy.at[h], hy.at[h], hss.at[h, 1], hrs.at[h, 1], (dx, yp)),
                remote(half, hx.at[h], hss.at[h, 0], hrs.at[h, 0], (xp, dy)),
                remote(shc.at[h], hc.at[h], hss.at[h, 2], hrs.at[h, 2], (xp, yp)),
            ]
        )
    for c in range(1, 4):
        fold(c)
    x_low, x_high, y_low, y_high = dx > 0, dx < ndx - 1, dy > 0, dy < ndy - 1

    sub = lax.broadcasted_iota(jnp.int32, (8, 7, 8, 128), 2)

    def apply(src, h):
        for ex in range(2):
            for ez in range(2):
                i0, l0 = 7 * ex, 6 * ez
                rows, layers = slice(i0, i0 + 8), slice(l0, l0 + 7)
                n0 = src[h, rows, layers, 0:8]
                n1 = src[h, rows, layers, 8:16]
                t0 = jnp.where(sub < 7, n0, n1).reshape(448, 128).astype(BF16)
                t1 = jnp.where(sub < 6, n1, n0).reshape(448, 128).astype(BF16)
                p0 = dot_nn(ap[4 * ex + ez], t0).reshape(8, 7, 8, 128)
                p1 = dot_nn(ap[4 * ex + 2 + ez], t1).reshape(8, 7, 8, 128)
                m0 = jnp.where(sub < 7, p0, 0.0) + jnp.where(sub < 6, 0.0, p1)
                m1 = jnp.where(sub < 6, p1, 0.0) + jnp.where(sub < 7, 0.0, p0)
                for part, tile in ((m0, slice(0, 8)), (m1, slice(8, 16))):
                    if ex:
                        first = part[:1, ez:] + acc[h, 7:8, l0 + ez : l0 + 7, tile]
                        rest = jnp.concatenate([first, part[1:, ez:]], axis=0)
                    else:
                        rest = part[:, ez:]
                    if ez:
                        joint = part[:, :1] + acc[h, rows, l0 : l0 + 1, tile]
                        rest = jnp.concatenate([joint, rest], axis=1)
                    acc[h, rows, layers, tile] = rest

    def exchange(t, h):
        copies = []

        def send(n, src, dst, where):
            copies.append(remote(src, dst, ess.at[t, h, n], ers.at[t, h, n], where))

        syl[t, h] = acc2[h, line(0, 15, 15), :].astype(BF16)
        send(0, syl.at[t, h], ryh.at[t, h], (dx, ym))
        if t < 2:
            syh[t, h] = acc2[h, line(0, 13, 15), :].astype(BF16)
            send(1, syh.at[t, h], ryl.at[t, h], (dx, yp))
        sxl[t, h] = acc[h, 0].astype(BF16)
        send(2, sxl.at[t, h], rxh.at[t, h], (xm, dy))
        if t < 2:
            sxh[t, h] = acc[h, 14].astype(BF16)
            send(3, sxh.at[t, h], rxl.at[t, h], (xp, dy))
        corners = [(0, 15, (xm, ym)), (14, 13, (xp, yp)), (0, 13, (xm, yp)), (14, 15, (xp, ym))]
        for n, (i, slot, where) in enumerate(corners[: 4 if t < 2 else 1]):
            scs[t, n, h] = acc2[h, line(i, slot, 1), :].astype(BF16)
            send(4 + n, scs.at[t, n, h], rcs.at[t, n, h], where)
        return copies

    def gated(flag, value, coef):
        return jnp.where(flag, value.astype(F32), 0.0) * coef

    def faces(t, h, y, y2, coef):
        def bump(i, slot, count, value):
            y2[h, line(i, slot, count), :] += value

        y[h, 14] += gated(x_high, rxh[t, h], coef)
        bump(0, 13, 15, gated(y_high, ryh[t, h], coef))
        bump(14, 13, 1, gated(jnp.logical_and(x_high, y_high), rcs[t, 0, h], coef))
        if t < 2:
            y[h, 0] += rxl[t, h].astype(F32) * coef
            bump(0, 15, 15, ryl[t, h].astype(F32) * coef)
            bump(0, 15, 1, rcs[t, 1, h].astype(F32) * coef)
            bump(14, 15, 1, gated(x_high, rcs[t, 2, h], coef))
            bump(0, 13, 1, gated(y_high, rcs[t, 3, h], coef))
            y[h, 0] = jnp.where(x_low, y[h, 0], 0.0)
            edge = y2[h, line(0, 15, 15), :]
            y2[h, line(0, 15, 15), :] = jnp.where(y_low, edge, 0.0)

    def wait(copies):
        for copy in copies:
            copy.wait()

    stages = []
    for h in range(2):
        wait(halo[h])
        ya[h, 0, :, 0:14, :] = jnp.where(x_low, hx[h].astype(F32), 0.0)
        ya2[h, line(1, 15, 14), :] = jnp.where(y_low, hy[h].astype(F32), 0.0)
        ya2[h, line(0, 15, 1), :] = jnp.where(
            jnp.logical_and(x_low, y_low), hc[h].astype(F32), 0.0
        )
        apply(ya, h)
        stages.append(exchange(0, h))
    for h in range(2):
        yb2[h] = 0.25 * acc2[h] - 0.375 * ya2[h]
    for h in range(2):
        wait(stages[h])
        faces(0, h, yb, yb2, 0.25)
        apply(yb, h)
        stages[h] = exchange(1, h)
    for h in range(2):
        ya2[h] = 0.5 * acc2[h] - 0.75 * yb2[h] - ya2[h]
    for h in range(2):
        wait(stages[h])
        faces(1, h, ya, ya2, 0.5)
        apply(ya, h)
        stages[h] = exchange(2, h)
    for h in range(2):
        yb2[h] = 0.5 * acc2[h] - 0.75 * ya2[h] - yb2[h]

    def pair(h):
        high = both[:, 128 * h : 128 * h + 128]
        low = both[:, NB + 128 * h : NB + 128 * h + 128]
        return high, low, jnp.concatenate([high, low], axis=1)

    def diagonal(h):
        high, _, pairs = pair(h)
        total = dot_tn(high, pairs)
        cross = total[:, 128:]
        return total[:, 0:128] + (cross + cross.T)

    for h in range(2):
        wait(stages[h])
        faces(2, h, yb, yb2, 0.5)
        yb2[h, line(0, 15, 15), :] = jnp.zeros((195, 128), F32)
        y = yb2[h, 208:3120, :]
        top = y.astype(BF16)
        both[:, 128 * h : 128 * h + 128] = top
        both[:, NB + 128 * h : NB + 128 * h + 128] = (y - top.astype(F32)).astype(BF16)
        block = diagonal(h)
        if h == 0:
            grams = [block]
        else:
            total = dot_tn(both[:, 0:128], pair(1)[2])
            cross = dot_tn(both[:, NB : NB + 128], both[:, 128:NB])
            grams += [total[:, 0:128] + (total[:, 128:] + cross), block]
    keep = pltpu.make_async_copy(both, yout, ysem)
    keep.start()
    gl[...] = jnp.concatenate(grams, axis=0).reshape(8, 48, 128)

    copies = []
    for d in range(1, ndx):
        peer = lax.rem(dx + d, ndx)
        copies.append(remote(gl.at[peer], ra.at[dx], as_.at[d], ar_.at[d], (peer, dy)))
    for copy in copies:
        copy.wait()
    chunk = gl[dx]
    for d in range(1, ndx):
        chunk += ra[lax.rem(dx + d, ndx)]
    for p in range(16):
        sb[p] = chunk[3 * p : 3 * p + 3]
    copies = []
    for d in range(1, ndy):
        peer = lax.rem(dy + d, ndy)
        copies.append(remote(sb.at[peer], rb.at[dy], bs_.at[d], br_.at[d], (dx, peer)))
    for copy in copies:
        copy.wait()
    piece = sb[dy]
    for d in range(1, ndy):
        piece += rb[lax.rem(dy + d, ndy)]
    gb[dy] = piece
    copies = []
    for d in range(1, ndy):
        peer = lax.rem(dy + d, ndy)
        copies.append(remote(gb.at[dy], gb.at[dy], cs_.at[d], cr_.at[d], (dx, peer)))
    for copy in copies:
        copy.wait()
    for p in range(16):
        gf[dx, 3 * p : 3 * p + 3] = gb[p]
    copies = []
    for d in range(1, ndx):
        peer = lax.rem(dx + d, ndx)
        copies.append(remote(gf.at[dx], gf.at[dx], ds_.at[d], dr_.at[d], (peer, dy)))
    for copy in copies:
        copy.wait()
    grams = gf[...].reshape(384, 128)
    gout[0:128, 0:128] = grams[0:128]
    gout[0:128, 128:NB] = grams[128:NB]
    gout[128:NB, 0:128] = jnp.zeros((128, 128), F32)
    gout[128:NB, 128:NB] = grams[NB:384]
    keep.wait()


def split3(x):
    a = x.astype(BF16)
    rest = x - a.astype(F32)
    b = rest.astype(BF16)
    return a, b, (rest - b.astype(F32)).astype(BF16)


def factor_inverse(g, work):
    rows = lax.broadcasted_iota(jnp.int32, (8, 128), 0)
    lanes = lax.broadcasted_iota(jnp.int32, (8, 128), 1)
    scales = []
    for o in range(8):
        base = 32 * o
        source = g if o == 0 else work
        tiles = [
            [source[base + 8 * t : base + 8 * t + 8, 128 * h : 128 * h + 128] for h in range(2)]
            for t in range(4)
        ]
        factors = []
        half = base // 128
        for s in range(4):
            first = base + 8 * s - 128 * half
            inside = jnp.logical_and(lanes >= first, lanes < first + 8)
            columns = []
            for q in range(s, 4):
                tile = tiles[q][half]
                columns.append(
                    [jnp.broadcast_to(tile[:, first + j : first + j + 1], (8, 128)) for j in range(8)]
                )
                fresh = jnp.where(lanes == rows + first, 1.0, 0.0) if q == s else 0.0
                tiles[q][half] = jnp.where(inside, fresh, tile)
            scale = jnp.ones((8, 128), F32)
            factor = jnp.ones((8, 128), F32)
            for k in range(8):
                lead = [jnp.broadcast_to(columns[0][j][k : k + 1, :], (8, 128)) for j in range(k, 8)]
                inv = 1.0 / lead[0]
                scale = jnp.where(rows == k, lead[0], scale)
                factor = jnp.where(rows == k, inv, factor)
                pivot = [jnp.broadcast_to(tiles[s][h][k : k + 1, :], (8, 128)) * inv for h in range(2)]
                lead = [v * inv for v in lead]
                for q in range(s, 4):
                    if q == s and k == 7:
                        continue
                    column = columns[q - s][k]
                    if q == s:
                        column = jnp.where(rows > k, column, 0.0)
                    for j in range(k + 1, 8):
                        columns[q - s][j] = columns[q - s][j] - column * lead[j - k]
                    for h in range(2):
                        tiles[q][h] = tiles[q][h] - column * pivot[h]
            scales.append(lax.rsqrt(scale))
            factors.append(factor)
        for t in range(4):
            for h in range(2):
                work[base + 8 * t : base + 8 * t + 8, 128 * h : 128 * h + 128] = tiles[t][h]
        if o < 7:
            u = jnp.concatenate([jnp.concatenate(tiles[t], axis=1) for t in range(4)], axis=0)
            f = jnp.concatenate([jnp.concatenate([v, v], axis=1) for v in factors], axis=0)
            r = lax.broadcasted_iota(jnp.int32, (32, NB), 0) + base
            c = lax.broadcasted_iota(jnp.int32, (32, NB), 1)
            v = jnp.where(jnp.logical_and(c > r, c < base + 32), 0.0, u * f)
            start = 128 * ((base + 32) // 128)
            u1, u2, u3 = split3(u[:, start:])
            v1, v2, v3 = split3(v)
            left = jnp.concatenate([u1, u1, u1, u2, u2, u3], axis=0)
            right = jnp.concatenate([v1, v2, v3, v1, v2, v1], axis=0)
            change = lax.dot_general(
                left, right, (((0,), (0,)), ((), ())), preferred_element_type=F32
            )
            rest = slice(base + 32, NB)
            old = (g if o == 0 else work)[rest, :]
            cc = lax.broadcasted_iota(jnp.int32, old.shape, 1)
            old = jnp.where(jnp.logical_and(cc >= base, cc < base + 32), 0.0, old)
            work[rest, :] = old - change[base + 32 - start :, :]
    for t in range(32):
        for h in range(2):
            tile = work[8 * t : 8 * t + 8, 128 * h : 128 * h + 128] * scales[t]
            work[8 * t : 8 * t + 8, 128 * h : 128 * h + 128] = jnp.where(
                lanes + 128 * h <= rows + 8 * t, tile, 0.0
            )


def basis_kernel(scale, y, g, out, ybuf, stage, work, whh, wlo, yin, osem):
    load = pltpu.make_async_copy(y, ybuf, yin)
    load.start()
    factor_inverse(g, work)
    w = work[...] * scale
    top = w.astype(BF16)
    whh[:, 0:NB] = top
    whh[:, NB:] = top
    wlo[...] = (w - top.astype(F32)).astype(BF16)
    load.wait()
    copies = []
    for i in range(14):
        rows = slice(208 * i, 208 * i + 208)
        q = dot_nt(ybuf[rows, :], whh[...]) + dot_nt(ybuf[rows, 0:NB], wlo[...])
        stage[i] = q.reshape(13, 16, NB)[:, 0:14, :]
        copy = pltpu.make_async_copy(stage.at[i], out.at[i], osem.at[i])
        copy.start()
        copies.append(copy)
    for copy in copies:
        copy.wait()


def solution(mesh):
    ndx, ndy = mesh.shape["dx"], mesh.shape["dy"]
    vmem = pl.BlockSpec(memory_space=pltpu.VMEM)
    anywhere = pl.BlockSpec(memory_space=pl.ANY)
    scale = math.sqrt(14 * 14 * 13 * ndx * ndy)

    def shards(orbitals, elem_mats, conn):
        dma = pltpu.SemaphoreType.DMA
        y, g = pl.pallas_call(
            lambda *refs: filter_kernel(ndx, ndy, *refs),
            out_shape=(
                jax.ShapeDtypeStruct((2912, 2 * NB), BF16),
                jax.ShapeDtypeStruct((NB, NB), F32),
            ),
            in_specs=[vmem, anywhere, vmem],
            out_specs=(anywhere, vmem),
            scratch_shapes=[
                pltpu.VMEM((8, 512, 512), BF16),
                pltpu.VMEM((8, 448, 448), BF16),
                pltpu.VMEM((2, 448, 128), jnp.int32),
                pltpu.VMEM((448, 512), BF16),
                pltpu.VMEM((512, 448), BF16),
                pltpu.VMEM((2, 3120, 128), F32),
                pltpu.VMEM((2, 3120, 128), F32),
                pltpu.VMEM((2, 3120, 128), F32),
                pltpu.VMEM((2912, 2 * NB), BF16),
                pltpu.VMEM((2, 13, 14, 128), BF16),
                pltpu.VMEM((2, 182, 128), BF16),
                pltpu.VMEM((2, 13, 128), BF16),
                pltpu.VMEM((2, 182, 128), BF16),
                pltpu.VMEM((2, 13, 128), BF16),
                pltpu.VMEM((3, 2, 13, 16, 128), BF16),
                pltpu.VMEM((2, 2, 13, 16, 128), BF16),
                pltpu.VMEM((3, 2, 195, 128), BF16),
                pltpu.VMEM((2, 2, 195, 128), BF16),
                pltpu.VMEM((3, 4, 2, 13, 128), BF16),
                pltpu.VMEM((2, 2, 13, 16, 128), BF16),
                pltpu.VMEM((3, 2, 13, 16, 128), BF16),
                pltpu.VMEM((2, 2, 195, 128), BF16),
                pltpu.VMEM((3, 2, 195, 128), BF16),
                pltpu.VMEM((3, 4, 2, 13, 128), BF16),
                pltpu.VMEM((8, 48, 128), F32),
                pltpu.VMEM((8, 48, 128), F32),
                pltpu.VMEM((16, 3, 128), F32),
                pltpu.VMEM((16, 3, 128), F32),
                pltpu.VMEM((16, 3, 128), F32),
                pltpu.VMEM((8, 48, 128), F32),
                dma((8,)),
                dma,
                dma((2, 3)),
                dma((2, 3)),
                dma((3, 2, 8)),
                dma((3, 2, 8)),
                dma((8,)),
                dma((8,)),
                dma((16,)),
                dma((16,)),
                dma((16,)),
                dma((16,)),
                dma((8,)),
                dma((8,)),
            ],
            compiler_params=pltpu.CompilerParams(collective_id=0, has_side_effects=True),
            name="filter",
        )(jnp.swapaxes(orbitals, 1, 2), elem_mats, conn)
        filtered = pl.pallas_call(
            lambda *refs: basis_kernel(scale, *refs),
            out_shape=jax.ShapeDtypeStruct((14, 13, 14, NB), F32),
            in_specs=[anywhere, vmem],
            out_specs=anywhere,
            scratch_shapes=[
                pltpu.VMEM((2912, 2 * NB), BF16),
                pltpu.VMEM((14, 13, 14, NB), F32),
                pltpu.VMEM((NB, NB), F32),
                pltpu.VMEM((NB, 2 * NB), BF16),
                pltpu.VMEM((NB, NB), BF16),
                dma,
                dma((14,)),
            ],
            name="basis",
        )(y, g)
        return jnp.swapaxes(filtered, 1, 2)

    in_specs = (
        P("dx", "dy", None, None),
        P("dx", "dy", None, None, None),
        P("dx", "dy", None, None),
    )
    out_specs = P("dx", "dy", None, None)
    return jax.shard_map(shards, mesh=mesh, in_specs=in_specs, out_specs=out_specs, check_vma=False)
```

```python
import math

import jax
import jax.numpy as jnp
from jax import lax
from jax.experimental import pallas as pl
from jax.experimental.pallas import tpu as pltpu
from jax.sharding import PartitionSpec as P

MESH = pl.DeviceIdType.MESH
F32 = jnp.float32
BF16 = jnp.bfloat16
NB = 256


def dot_nn(a, b, precision=None):
    return lax.dot_general(
        a, b, (((1,), (0,)), ((), ())), precision=precision, preferred_element_type=F32
    )


def dot_nt(a, b, precision=None):
    return lax.dot_general(
        a, b, (((1,), (1,)), ((), ())), precision=precision, preferred_element_type=F32
    )


def dot_tn(a, b, precision=None):
    return lax.dot_general(
        a, b, (((0,), (0,)), ((), ())), precision=precision, preferred_element_type=F32
    )


def filter_kernel(
    ndx, ndy,
    orb, mats, conn,
    yout, gout,
    obuf, abuf, ap, rmap, st, tt, ya2, yb2, acc2, both,
    hx, hy, hc, shy, shc, sxl, sxh, syl, syh, scs, rxl, rxh, ryl, ryh, rcs,
    gl, ra, sb, rb, gb, gf,
    osem, msem, ysem, hss, hrs, ess, ers, as_, ar_, bs_, br_, cs_, cr_, ds_, dr_,
):
    dx = lax.axis_index("dx")
    dy = lax.axis_index("dy")
    xp, xm = lax.rem(dx + 1, ndx), lax.rem(dx + ndx - 1, ndx)
    yp, ym = lax.rem(dy + 1, ndy), lax.rem(dy + ndy - 1, ndy)
    ya, yb, acc = (ref.reshape(2, 15, 13, 16, 128) for ref in (ya2, yb2, acc2))

    barrier = pltpu.get_barrier_semaphore()
    partners = [(lax.rem(dx + d, ndx), dy) for d in range(1, ndx)]
    partners += [(dx, lax.rem(dy + d, ndy)) for d in range(1, ndy)]
    partners += [(xp, yp), (xp, ym), (xm, yp), (xm, ym)]
    for partner in partners:
        pl.semaphore_signal(barrier, inc=1, device_id=partner, device_id_type=MESH)

    first_load = pltpu.make_async_copy(orb, obuf, osem)
    first_load.start()
    loads = []
    for e in range(8):
        copy = pltpu.make_async_copy(mats.at[e // 4, e // 2 % 2, e % 2], abuf.at[e], msem.at[e])
        copy.start()
        loads.append(copy)

    grid = (8, 7, 8, 128)
    a_of, l_of, s_of = (lax.broadcasted_iota(jnp.int32, grid, d) for d in range(3))
    for ey in range(2):
        b_of = jnp.where(s_of < 7 - ey, s_of + 1 + ey, s_of - 7 + ey)
        rmap[ey] = (a_of * 225 + b_of * 15 + l_of).reshape(448, 128)

    def line(i, slot, count):
        return pl.ds(i * 208 + slot, 13 * count, stride=16)

    for h in range(2):
        ya2[h, 0:208, :] = jnp.zeros((208, 128), F32)
        ya2[h, line(1, 14, 14), :] = jnp.zeros((182, 128), F32)
        ya2[h, line(1, 15, 14), :] = jnp.zeros((182, 128), F32)
    first_load.wait()

    def fill(i, carry):
        plane = obuf[i].astype(F32)
        for h in range(2):
            ya[h, i + 1, :, 0:14, :] = plane[:, :, 128 * h : 128 * h + 128]
        return carry

    lax.fori_loop(0, 14, fill, 0)

    for h in range(2):
        shy[h] = ya2[h, line(1, 13, 14), :].astype(BF16)
        shc[h] = ya2[h, line(14, 13, 1), :].astype(BF16)

    def fold(c):
        ex, ey = c // 2, c % 2
        links = conn[ex, ey]
        for ez in range(2):
            e = c * 2 + ez
            loads[e].wait()
            row = links[ez : ez + 1] - ((7 * ex * 15 + 7 * ey) * 15 + 7 * ez + 1 - ez)
            for q in range(4):
                part = row[:, 128 * q : 128 * q + 128]
                st[:, 128 * q : 128 * q + 128] = jnp.where(rmap[ey] == part, 1.0, 0.0).astype(BF16)
            tt[...] = dot_nt(abuf[e], st[...]).astype(BF16)
            ap[e] = dot_nn(st[...], tt[...]).astype(BF16)

    def remote(src, dst, ssem, rsem, where):
        copy = pltpu.make_async_remote_copy(
            src_ref=src, dst_ref=dst, send_sem=ssem, recv_sem=rsem, device_id=where, device_id_type=MESH
        )
        copy.start()
        return copy

    x_low, x_high, y_low, y_high = dx > 0, dx < ndx - 1, dy > 0, dy < ndy - 1

    def toward(src, dst, ssem, rsem, sx, sy):
        where = (dx + sx, dy + sy)
        copy = pltpu.make_async_remote_copy(
            src_ref=src, dst_ref=dst, send_sem=ssem, recv_sem=rsem, device_id=where, device_id_type=MESH
        )
        ahead = [f for f in ({1: x_high, -1: x_low}.get(sx), {1: y_high, -1: y_low}.get(sy)) if f is not None]
        behind = [f for f in ({1: x_low, -1: x_high}.get(sx), {1: y_low, -1: y_high}.get(sy)) if f is not None]
        ahead = ahead[0] if len(ahead) == 1 else jnp.logical_and(*ahead)
        behind = behind[0] if len(behind) == 1 else jnp.logical_and(*behind)

        @pl.when(ahead)
        def _():
            copy.start()

        return copy, ahead, behind

    def wait(copies):
        for copy, ahead, behind in copies:

            @pl.when(behind)
            def _():
                copy.wait_recv()

            @pl.when(ahead)
            def _():
                copy.wait_send()

    pl.semaphore_wait(barrier, len(partners))
    halo = []
    for h in range(2):
        half = obuf.at[13, :, :, 128 * h : 128 * h + 128]
        halo.append(
            [
                toward(shc.at[h], hc.at[h], hss.at[h, 2], hrs.at[h, 2], 1, 1),
                toward(shy.at[h], hy.at[h], hss.at[h, 1], hrs.at[h, 1], 0, 1),
                toward(half, hx.at[h], hss.at[h, 0], hrs.at[h, 0], 1, 0),
            ]
        )
    for c in range(4):
        fold(c)

    sub = lax.broadcasted_iota(jnp.int32, (8, 7, 8, 128), 2)

    def apply(src, h):
        for ex in range(2):
            for ez in range(2):
                i0, l0 = 7 * ex, 6 * ez
                rows, layers = slice(i0, i0 + 8), slice(l0, l0 + 7)
                n0 = src[h, rows, layers, 0:8]
                n1 = src[h, rows, layers, 8:16]
                t0 = jnp.where(sub < 7, n0, n1).reshape(448, 128).astype(BF16)
                t1 = jnp.where(sub < 6, n1, n0).reshape(448, 128).astype(BF16)
                p0 = dot_nn(ap[4 * ex + ez], t0).reshape(8, 7, 8, 128)
                p1 = dot_nn(ap[4 * ex + 2 + ez], t1).reshape(8, 7, 8, 128)
                m0 = jnp.where(sub < 7, p0, 0.0) + jnp.where(sub < 6, 0.0, p1)
                m1 = jnp.where(sub < 6, p1, 0.0) + jnp.where(sub < 7, 0.0, p0)
                for part, tile in ((m0, slice(0, 8)), (m1, slice(8, 16))):
                    if ex:
                        first = part[:1, ez:] + acc[h, 7:8, l0 + ez : l0 + 7, tile]
                        rest = jnp.concatenate([first, part[1:, ez:]], axis=0)
                    else:
                        rest = part[:, ez:]
                    if ez:
                        joint = part[:, :1] + acc[h, rows, l0 : l0 + 1, tile]
                        rest = jnp.concatenate([joint, rest], axis=1)
                    acc[h, rows, layers, tile] = rest

    def exchange(t, h):
        copies = []

        def send(n, src, dst, sx, sy):
            copies.append(toward(src, dst, ess.at[t, h, n], ers.at[t, h, n], sx, sy))

        corners = [(0, 15, -1, -1), (14, 13, 1, 1), (0, 13, -1, 1), (14, 15, 1, -1)]
        count = 4 if t < 2 else 1
        for n, (i, slot, _, _) in enumerate(corners[:count]):
            scs[t, n, h] = acc2[h, line(i, slot, 1), :].astype(BF16)
        syl[t, h] = acc2[h, line(0, 15, 15), :].astype(BF16)
        if t < 2:
            syh[t, h] = acc2[h, line(0, 13, 15), :].astype(BF16)
        sxl[t, h] = acc[h, 0].astype(BF16)
        if t < 2:
            sxh[t, h] = acc[h, 14].astype(BF16)
        for n, (_, _, sx, sy) in enumerate(corners[:count]):
            send(4 + n, scs.at[t, n, h], rcs.at[t, n, h], sx, sy)
        send(0, syl.at[t, h], ryh.at[t, h], 0, -1)
        if t < 2:
            send(1, syh.at[t, h], ryl.at[t, h], 0, 1)
        send(2, sxl.at[t, h], rxh.at[t, h], -1, 0)
        if t < 2:
            send(3, sxh.at[t, h], rxl.at[t, h], 1, 0)
        return copies

    def gated(flag, value, coef):
        return jnp.where(flag, value.astype(F32), 0.0) * coef

    def faces(t, h, y, y2, coef):
        def bump(i, slot, count, value):
            y2[h, line(i, slot, count), :] += value

        y[h, 14] += gated(x_high, rxh[t, h], coef)
        bump(0, 13, 15, gated(y_high, ryh[t, h], coef))
        bump(14, 13, 1, gated(jnp.logical_and(x_high, y_high), rcs[t, 0, h], coef))
        if t < 2:
            y[h, 0] += rxl[t, h].astype(F32) * coef
            bump(0, 15, 15, ryl[t, h].astype(F32) * coef)
            bump(0, 15, 1, rcs[t, 1, h].astype(F32) * coef)
            bump(14, 15, 1, gated(x_high, rcs[t, 2, h], coef))
            bump(0, 13, 1, gated(y_high, rcs[t, 3, h], coef))
            y[h, 0] = jnp.where(x_low, y[h, 0], 0.0)
            edge = y2[h, line(0, 15, 15), :]
            y2[h, line(0, 15, 15), :] = jnp.where(y_low, edge, 0.0)

    stages = []
    for h in range(2):
        wait(halo[h])
        ya[h, 0, :, 0:14, :] = jnp.where(x_low, hx[h].astype(F32), 0.0)
        ya2[h, line(1, 15, 14), :] = jnp.where(y_low, hy[h].astype(F32), 0.0)
        ya2[h, line(0, 15, 1), :] = jnp.where(
            jnp.logical_and(x_low, y_low), hc[h].astype(F32), 0.0
        )
        apply(ya, h)
        stages.append(exchange(0, h))
    for h in range(2):
        yb2[h] = 0.25 * acc2[h] - 0.375 * ya2[h]
    for h in range(2):
        wait(stages[h])
        faces(0, h, yb, yb2, 0.25)
        apply(yb, h)
        stages[h] = exchange(1, h)
    for h in range(2):
        ya2[h] = 0.5 * acc2[h] - 0.75 * yb2[h] - ya2[h]
    for h in range(2):
        wait(stages[h])
        faces(1, h, ya, ya2, 0.5)
        apply(ya, h)
        stages[h] = exchange(2, h)
    for h in range(2):
        yb2[h] = 0.5 * acc2[h] - 0.75 * ya2[h] - yb2[h]

    def pair(h):
        high = both[:, 128 * h : 128 * h + 128]
        low = both[:, NB + 128 * h : NB + 128 * h + 128]
        return high, low, jnp.concatenate([high, low], axis=1)

    def diagonal(h):
        high, _, pairs = pair(h)
        total = dot_tn(high, pairs)
        cross = total[:, 128:]
        return total[:, 0:128] + (cross + cross.T)

    for h in range(2):
        wait(stages[h])
        faces(2, h, yb, yb2, 0.5)
        yb2[h, line(0, 15, 15), :] = jnp.zeros((195, 128), F32)
        y = yb2[h, 208:3120, :]
        top = y.astype(BF16)
        both[:, 128 * h : 128 * h + 128] = top
        both[:, NB + 128 * h : NB + 128 * h + 128] = (y - top.astype(F32)).astype(BF16)
        block = diagonal(h)
        if h == 0:
            grams = [block]
        else:
            total = dot_tn(both[:, 0:128], pair(1)[2])
            cross = dot_tn(both[:, NB : NB + 128], both[:, 128:NB])
            grams += [total[:, 0:128] + (total[:, 128:] + cross), block]
    keep = pltpu.make_async_copy(both, yout, ysem)
    keep.start()
    gl[...] = jnp.concatenate(grams, axis=0).reshape(8, 48, 128)

    copies = []
    for d in range(1, ndx):
        peer = lax.rem(dx + d, ndx)
        copies.append(remote(gl.at[peer], ra.at[dx], as_.at[d], ar_.at[d], (peer, dy)))
    for copy in copies:
        copy.wait()
    chunk = gl[dx]
    for d in range(1, ndx):
        chunk += ra[lax.rem(dx + d, ndx)]
    for p in range(16):
        sb[p] = chunk[3 * p : 3 * p + 3]
    copies = []
    for d in range(1, ndy):
        peer = lax.rem(dy + d, ndy)
        copies.append(remote(sb.at[peer], rb.at[dy], bs_.at[d], br_.at[d], (dx, peer)))
    for copy in copies:
        copy.wait()
    piece = sb[dy]
    for d in range(1, ndy):
        piece += rb[lax.rem(dy + d, ndy)]
    gb[dy] = piece
    copies = []
    for d in range(1, ndy):
        peer = lax.rem(dy + d, ndy)
        copies.append(remote(gb.at[dy], gb.at[dy], cs_.at[d], cr_.at[d], (dx, peer)))
    for copy in copies:
        copy.wait()
    for p in range(16):
        gf[dx, 3 * p : 3 * p + 3] = gb[p]
    copies = []
    for d in range(1, ndx):
        peer = lax.rem(dx + d, ndx)
        copies.append(remote(gf.at[dx], gf.at[dx], ds_.at[d], dr_.at[d], (peer, dy)))
    for copy in copies:
        copy.wait()
    grams = gf[...].reshape(384, 128)
    gout[0:128, 0:128] = grams[0:128]
    gout[0:128, 128:NB] = grams[128:NB]
    gout[128:NB, 0:128] = jnp.zeros((128, 128), F32)
    gout[128:NB, 128:NB] = grams[NB:384]
    keep.wait()


def split3(x):
    a = x.astype(BF16)
    rest = x - a.astype(F32)
    b = rest.astype(BF16)
    return a, b, (rest - b.astype(F32)).astype(BF16)


def factor_inverse(g, work):
    rows = lax.broadcasted_iota(jnp.int32, (8, 128), 0)
    lanes = lax.broadcasted_iota(jnp.int32, (8, 128), 1)
    scales = []
    for o in range(8):
        base = 32 * o
        source = g if o == 0 else work
        tiles = [
            [source[base + 8 * t : base + 8 * t + 8, 128 * h : 128 * h + 128] for h in range(2)]
            for t in range(4)
        ]
        factors = []
        half = base // 128
        for s in range(4):
            first = base + 8 * s - 128 * half
            inside = jnp.logical_and(lanes >= first, lanes < first + 8)
            columns = []
            for q in range(s, 4):
                tile = tiles[q][half]
                columns.append(
                    [jnp.broadcast_to(tile[:, first + j : first + j + 1], (8, 128)) for j in range(8)]
                )
                fresh = jnp.where(lanes == rows + first, 1.0, 0.0) if q == s else 0.0
                tiles[q][half] = jnp.where(inside, fresh, tile)
            scale = jnp.ones((8, 128), F32)
            factor = jnp.ones((8, 128), F32)
            for k in range(8):
                lead = [jnp.broadcast_to(columns[0][j][k : k + 1, :], (8, 128)) for j in range(k, 8)]
                inv = 1.0 / lead[0]
                scale = jnp.where(rows == k, lead[0], scale)
                factor = jnp.where(rows == k, inv, factor)
                pivot = [jnp.broadcast_to(tiles[s][h][k : k + 1, :], (8, 128)) * inv for h in range(2)]
                lead = [v * inv for v in lead]
                for q in range(s, 4):
                    if q == s and k == 7:
                        continue
                    column = columns[q - s][k]
                    if q == s:
                        column = jnp.where(rows > k, column, 0.0)
                    for j in range(k + 1, 8):
                        columns[q - s][j] = columns[q - s][j] - column * lead[j - k]
                    for h in range(2):
                        tiles[q][h] = tiles[q][h] - column * pivot[h]
            scales.append(lax.rsqrt(scale))
            factors.append(factor)
        for t in range(4):
            for h in range(2):
                work[base + 8 * t : base + 8 * t + 8, 128 * h : 128 * h + 128] = tiles[t][h]
        if o < 7:
            u = jnp.concatenate([jnp.concatenate(tiles[t], axis=1) for t in range(4)], axis=0)
            f = jnp.concatenate([jnp.concatenate([v, v], axis=1) for v in factors], axis=0)
            r = lax.broadcasted_iota(jnp.int32, (32, NB), 0) + base
            c = lax.broadcasted_iota(jnp.int32, (32, NB), 1)
            v = jnp.where(jnp.logical_and(c > r, c < base + 32), 0.0, u * f)
            start = 128 * ((base + 32) // 128)
            u1, u2, u3 = split3(u[:, start:])
            v1, v2, v3 = split3(v)
            left = jnp.concatenate([u1, u1, u1, u2, u2, u3], axis=0)
            right = jnp.concatenate([v1, v2, v3, v1, v2, v1], axis=0)
            change = lax.dot_general(
                left, right, (((0,), (0,)), ((), ())), preferred_element_type=F32
            )
            rest = slice(base + 32, NB)
            old = (g if o == 0 else work)[rest, :]
            cc = lax.broadcasted_iota(jnp.int32, old.shape, 1)
            old = jnp.where(jnp.logical_and(cc >= base, cc < base + 32), 0.0, old)
            work[rest, :] = old - change[base + 32 - start :, :]
    for t in range(32):
        for h in range(2):
            tile = work[8 * t : 8 * t + 8, 128 * h : 128 * h + 128] * scales[t]
            work[8 * t : 8 * t + 8, 128 * h : 128 * h + 128] = jnp.where(
                lanes + 128 * h <= rows + 8 * t, tile, 0.0
            )


def basis_kernel(scale, y, g, out, ybuf, stage, work, whh, wlo, yin, osem):
    load = pltpu.make_async_copy(y, ybuf, yin)
    load.start()
    factor_inverse(g, work)
    w = work[...] * scale
    top = w.astype(BF16)
    whh[:, 0:NB] = top
    whh[:, NB:] = top
    wlo[...] = (w - top.astype(F32)).astype(BF16)
    load.wait()
    copies = []
    for i in range(14):
        rows = slice(208 * i, 208 * i + 208)
        q = dot_nt(ybuf[rows, :], whh[...]) + dot_nt(ybuf[rows, 0:NB], wlo[...])
        stage[i] = q.reshape(13, 16, NB)[:, 0:14, :]
        copy = pltpu.make_async_copy(stage.at[i], out.at[i], osem.at[i])
        copy.start()
        copies.append(copy)
    for copy in copies:
        copy.wait()


def solution(mesh):
    ndx, ndy = mesh.shape["dx"], mesh.shape["dy"]
    vmem = pl.BlockSpec(memory_space=pltpu.VMEM)
    anywhere = pl.BlockSpec(memory_space=pl.ANY)
    scale = math.sqrt(14 * 14 * 13 * ndx * ndy)

    def shards(orbitals, elem_mats, conn):
        dma = pltpu.SemaphoreType.DMA
        y, g = pl.pallas_call(
            lambda *refs: filter_kernel(ndx, ndy, *refs),
            out_shape=(
                jax.ShapeDtypeStruct((2912, 2 * NB), BF16),
                jax.ShapeDtypeStruct((NB, NB), F32),
            ),
            in_specs=[anywhere, anywhere, vmem],
            out_specs=(anywhere, vmem),
            scratch_shapes=[
                pltpu.VMEM((14, 13, 14, NB), BF16),
                pltpu.VMEM((8, 512, 512), BF16),
                pltpu.VMEM((8, 448, 448), BF16),
                pltpu.VMEM((2, 448, 128), jnp.int32),
                pltpu.VMEM((448, 512), BF16),
                pltpu.VMEM((512, 448), BF16),
                pltpu.VMEM((2, 3120, 128), F32),
                pltpu.VMEM((2, 3120, 128), F32),
                pltpu.VMEM((2, 3120, 128), F32),
                pltpu.VMEM((2912, 2 * NB), BF16),
                pltpu.VMEM((2, 13, 14, 128), BF16),
                pltpu.VMEM((2, 182, 128), BF16),
                pltpu.VMEM((2, 13, 128), BF16),
                pltpu.VMEM((2, 182, 128), BF16),
                pltpu.VMEM((2, 13, 128), BF16),
                pltpu.VMEM((3, 2, 13, 16, 128), BF16),
                pltpu.VMEM((2, 2, 13, 16, 128), BF16),
                pltpu.VMEM((3, 2, 195, 128), BF16),
                pltpu.VMEM((2, 2, 195, 128), BF16),
                pltpu.VMEM((3, 4, 2, 13, 128), BF16),
                pltpu.VMEM((2, 2, 13, 16, 128), BF16),
                pltpu.VMEM((3, 2, 13, 16, 128), BF16),
                pltpu.VMEM((2, 2, 195, 128), BF16),
                pltpu.VMEM((3, 2, 195, 128), BF16),
                pltpu.VMEM((3, 4, 2, 13, 128), BF16),
                pltpu.VMEM((8, 48, 128), F32),
                pltpu.VMEM((8, 48, 128), F32),
                pltpu.VMEM((16, 3, 128), F32),
                pltpu.VMEM((16, 3, 128), F32),
                pltpu.VMEM((16, 3, 128), F32),
                pltpu.VMEM((8, 48, 128), F32),
                dma,
                dma((8,)),
                dma,
                dma((2, 3)),
                dma((2, 3)),
                dma((3, 2, 8)),
                dma((3, 2, 8)),
                dma((8,)),
                dma((8,)),
                dma((16,)),
                dma((16,)),
                dma((16,)),
                dma((16,)),
                dma((8,)),
                dma((8,)),
            ],
            compiler_params=pltpu.CompilerParams(collective_id=0, has_side_effects=True),
            name="filter",
        )(jnp.swapaxes(orbitals, 1, 2), elem_mats, conn)
        filtered = pl.pallas_call(
            lambda *refs: basis_kernel(scale, *refs),
            out_shape=jax.ShapeDtypeStruct((14, 13, 14, NB), F32),
            in_specs=[anywhere, vmem],
            out_specs=anywhere,
            scratch_shapes=[
                pltpu.VMEM((2912, 2 * NB), BF16),
                pltpu.VMEM((14, 13, 14, NB), F32),
                pltpu.VMEM((NB, NB), F32),
                pltpu.VMEM((NB, 2 * NB), BF16),
                pltpu.VMEM((NB, NB), BF16),
                dma,
                dma((14,)),
            ],
            name="basis",
        )(y, g)
        return jnp.swapaxes(filtered, 1, 2)

    in_specs = (
        P("dx", "dy", None, None),
        P("dx", "dy", None, None, None),
        P("dx", "dy", None, None),
    )
    out_specs = P("dx", "dy", None, None)
    return jax.shard_map(shards, mesh=mesh, in_specs=in_specs, out_specs=out_specs, check_vma=False)
```

```python
import math

import jax
import jax.numpy as jnp
from jax import lax
from jax.experimental import pallas as pl
from jax.experimental.pallas import tpu as pltpu
from jax.sharding import PartitionSpec as P

MESH = pl.DeviceIdType.MESH
F32 = jnp.float32
BF16 = jnp.bfloat16
NB = 256


def dot_nn(a, b, precision=None):
    return lax.dot_general(
        a, b, (((1,), (0,)), ((), ())), precision=precision, preferred_element_type=F32
    )


def dot_nt(a, b, precision=None):
    return lax.dot_general(
        a, b, (((1,), (1,)), ((), ())), precision=precision, preferred_element_type=F32
    )


def dot_tn(a, b, precision=None):
    return lax.dot_general(
        a, b, (((0,), (0,)), ((), ())), precision=precision, preferred_element_type=F32
    )


def filter_kernel(
    ndx, ndy, scale,
    orb, mats, conn,
    yout, wout,
    obuf, abuf, ap, rmap, st, tt, ya2, yb2, acc2, both,
    hx, hy, hc, shy, shc, sxl, sxh, syl, syh, scs, rxl, rxh, ryl, ryh, rcs,
    gl0, ra0, gf0, gl1, ra1, gf1, sb0, rb0, gb0, sb1, rb1, gb1, work, pivots,
    osem, msem, ysem, hss, hrs, ess, ers, as_, ar_, bs_, br_, cs_, cr_, ds_, dr_,
):
    dx = lax.axis_index("dx")
    dy = lax.axis_index("dy")
    xp, xm = lax.rem(dx + 1, ndx), lax.rem(dx + ndx - 1, ndx)
    yp, ym = lax.rem(dy + 1, ndy), lax.rem(dy + ndy - 1, ndy)
    ya, yb, acc = (ref.reshape(2, 15, 13, 16, 128) for ref in (ya2, yb2, acc2))

    barrier = pltpu.get_barrier_semaphore()
    partners = [(lax.rem(dx + d, ndx), dy) for d in range(1, ndx)]
    partners += [(dx, lax.rem(dy + d, ndy)) for d in range(1, ndy)]
    partners += [(xp, yp), (xp, ym), (xm, yp), (xm, ym)]
    for partner in partners:
        pl.semaphore_signal(barrier, inc=1, device_id=partner, device_id_type=MESH)

    first_load = pltpu.make_async_copy(orb, obuf, osem)
    first_load.start()
    loads = []
    for e in range(8):
        copy = pltpu.make_async_copy(mats.at[e // 4, e // 2 % 2, e % 2], abuf.at[e], msem.at[e])
        copy.start()
        loads.append(copy)

    grid = (8, 7, 8, 128)
    a_of, l_of, s_of = (lax.broadcasted_iota(jnp.int32, grid, d) for d in range(3))
    for ey in range(2):
        b_of = jnp.where(s_of < 7 - ey, s_of + 1 + ey, s_of - 7 + ey)
        rmap[ey] = (a_of * 225 + b_of * 15 + l_of).reshape(448, 128)

    def line(i, slot, count):
        return pl.ds(i * 208 + slot, 13 * count, stride=16)

    for h in range(2):
        ya2[h, 0:208, :] = jnp.zeros((208, 128), F32)
        ya2[h, line(1, 14, 14), :] = jnp.zeros((182, 128), F32)
        ya2[h, line(1, 15, 14), :] = jnp.zeros((182, 128), F32)
    first_load.wait()

    def fill(i, carry):
        plane = obuf[i].astype(F32)
        for h in range(2):
            ya[h, i + 1, :, 0:14, :] = plane[:, :, 128 * h : 128 * h + 128]
        return carry

    lax.fori_loop(0, 14, fill, 0)

    for h in range(2):
        shy[h] = ya2[h, line(1, 13, 14), :].astype(BF16)
        shc[h] = ya2[h, line(14, 13, 1), :].astype(BF16)

    def fold(c):
        ex, ey = c // 2, c % 2
        links = conn[ex, ey]
        for ez in range(2):
            e = c * 2 + ez
            loads[e].wait()
            row = links[ez : ez + 1] - ((7 * ex * 15 + 7 * ey) * 15 + 7 * ez + 1 - ez)
            for q in range(4):
                part = row[:, 128 * q : 128 * q + 128]
                st[:, 128 * q : 128 * q + 128] = jnp.where(rmap[ey] == part, 1.0, 0.0).astype(BF16)
            tt[...] = dot_nt(abuf[e], st[...]).astype(BF16)
            ap[e] = dot_nn(st[...], tt[...]).astype(BF16)

    def remote(src, dst, ssem, rsem, where):
        copy = pltpu.make_async_remote_copy(
            src_ref=src, dst_ref=dst, send_sem=ssem, recv_sem=rsem, device_id=where, device_id_type=MESH
        )
        copy.start()
        return copy

    x_low, x_high, y_low, y_high = dx > 0, dx < ndx - 1, dy > 0, dy < ndy - 1

    def toward(src, dst, ssem, rsem, sx, sy):
        where = (dx + sx, dy + sy)
        copy = pltpu.make_async_remote_copy(
            src_ref=src, dst_ref=dst, send_sem=ssem, recv_sem=rsem, device_id=where, device_id_type=MESH
        )
        ahead = [f for f in ({1: x_high, -1: x_low}.get(sx), {1: y_high, -1: y_low}.get(sy)) if f is not None]
        behind = [f for f in ({1: x_low, -1: x_high}.get(sx), {1: y_low, -1: y_high}.get(sy)) if f is not None]
        ahead = ahead[0] if len(ahead) == 1 else jnp.logical_and(*ahead)
        behind = behind[0] if len(behind) == 1 else jnp.logical_and(*behind)

        @pl.when(ahead)
        def _():
            copy.start()

        return copy, ahead, behind

    def wait(copies):
        for copy, ahead, behind in copies:

            @pl.when(behind)
            def _():
                copy.wait_recv()

            @pl.when(ahead)
            def _():
                copy.wait_send()

    fold(0)
    pl.semaphore_wait(barrier, len(partners))
    halo = []
    for h in range(2):
        half = obuf.at[13, :, :, 128 * h : 128 * h + 128]
        halo.append(
            [
                toward(shc.at[h], hc.at[h], hss.at[h, 2], hrs.at[h, 2], 1, 1),
                toward(shy.at[h], hy.at[h], hss.at[h, 1], hrs.at[h, 1], 0, 1),
                toward(half, hx.at[h], hss.at[h, 0], hrs.at[h, 0], 1, 0),
            ]
        )
    for c in range(1, 4):
        fold(c)

    sub = lax.broadcasted_iota(jnp.int32, (8, 7, 8, 128), 2)

    def apply(src, h):
        for ex in range(2):
            for ez in range(2):
                i0, l0 = 7 * ex, 6 * ez
                rows, layers = slice(i0, i0 + 8), slice(l0, l0 + 7)
                n0 = src[h, rows, layers, 0:8]
                n1 = src[h, rows, layers, 8:16]
                t0 = jnp.where(sub < 7, n0, n1).reshape(448, 128).astype(BF16)
                t1 = jnp.where(sub < 6, n1, n0).reshape(448, 128).astype(BF16)
                p0 = dot_nn(ap[4 * ex + ez], t0).reshape(8, 7, 8, 128)
                p1 = dot_nn(ap[4 * ex + 2 + ez], t1).reshape(8, 7, 8, 128)
                m0 = jnp.where(sub < 7, p0, 0.0) + jnp.where(sub < 6, 0.0, p1)
                m1 = jnp.where(sub < 6, p1, 0.0) + jnp.where(sub < 7, 0.0, p0)
                for part, tile in ((m0, slice(0, 8)), (m1, slice(8, 16))):
                    if ex:
                        first = part[:1, ez:] + acc[h, 7:8, l0 + ez : l0 + 7, tile]
                        rest = jnp.concatenate([first, part[1:, ez:]], axis=0)
                    else:
                        rest = part[:, ez:]
                    if ez:
                        joint = part[:, :1] + acc[h, rows, l0 : l0 + 1, tile]
                        rest = jnp.concatenate([joint, rest], axis=1)
                    acc[h, rows, layers, tile] = rest

    def exchange(t, h):
        copies = []

        def send(n, src, dst, sx, sy):
            copies.append(toward(src, dst, ess.at[t, h, n], ers.at[t, h, n], sx, sy))

        corners = [(0, 15, -1, -1), (14, 13, 1, 1), (0, 13, -1, 1), (14, 15, 1, -1)]
        count = 4 if t < 2 else 1
        for n, (i, slot, _, _) in enumerate(corners[:count]):
            scs[t, n, h] = acc2[h, line(i, slot, 1), :].astype(BF16)
        syl[t, h] = acc2[h, line(0, 15, 15), :].astype(BF16)
        if t < 2:
            syh[t, h] = acc2[h, line(0, 13, 15), :].astype(BF16)
        sxl[t, h] = acc[h, 0].astype(BF16)
        if t < 2:
            sxh[t, h] = acc[h, 14].astype(BF16)
        for n, (_, _, sx, sy) in enumerate(corners[:count]):
            send(4 + n, scs.at[t, n, h], rcs.at[t, n, h], sx, sy)
        send(0, syl.at[t, h], ryh.at[t, h], 0, -1)
        if t < 2:
            send(1, syh.at[t, h], ryl.at[t, h], 0, 1)
        send(2, sxl.at[t, h], rxh.at[t, h], -1, 0)
        if t < 2:
            send(3, sxh.at[t, h], rxl.at[t, h], 1, 0)
        return copies

    def gated(flag, value, coef):
        return jnp.where(flag, value.astype(F32), 0.0) * coef

    def faces(t, h, y, y2, coef):
        def bump(i, slot, count, value):
            y2[h, line(i, slot, count), :] += value

        y[h, 14] += gated(x_high, rxh[t, h], coef)
        bump(0, 13, 15, gated(y_high, ryh[t, h], coef))
        bump(14, 13, 1, gated(jnp.logical_and(x_high, y_high), rcs[t, 0, h], coef))
        if t < 2:
            y[h, 0] += rxl[t, h].astype(F32) * coef
            bump(0, 15, 15, ryl[t, h].astype(F32) * coef)
            bump(0, 15, 1, rcs[t, 1, h].astype(F32) * coef)
            bump(14, 15, 1, gated(x_high, rcs[t, 2, h], coef))
            bump(0, 13, 1, gated(y_high, rcs[t, 3, h], coef))
            y[h, 0] = jnp.where(x_low, y[h, 0], 0.0)
            edge = y2[h, line(0, 15, 15), :]
            y2[h, line(0, 15, 15), :] = jnp.where(y_low, edge, 0.0)

    stages = []
    for h in range(2):
        wait(halo[h])
        ya[h, 0, :, 0:14, :] = jnp.where(x_low, hx[h].astype(F32), 0.0)
        ya2[h, line(1, 15, 14), :] = jnp.where(y_low, hy[h].astype(F32), 0.0)
        ya2[h, line(0, 15, 1), :] = jnp.where(
            jnp.logical_and(x_low, y_low), hc[h].astype(F32), 0.0
        )
        apply(ya, h)
        stages.append(exchange(0, h))
    for h in range(2):
        yb2[h] = 0.25 * acc2[h] - 0.375 * ya2[h]
    for h in range(2):
        wait(stages[h])
        faces(0, h, yb, yb2, 0.25)
        apply(yb, h)
        stages[h] = exchange(1, h)
    for h in range(2):
        ya2[h] = 0.5 * acc2[h] - 0.75 * yb2[h] - ya2[h]
    for h in range(2):
        wait(stages[h])
        faces(1, h, ya, ya2, 0.5)
        apply(ya, h)
        stages[h] = exchange(2, h)
    for h in range(2):
        yb2[h] = 0.5 * acc2[h] - 0.75 * ya2[h] - yb2[h]

    def pair(h):
        high = both[:, 128 * h : 128 * h + 128]
        low = both[:, NB + 128 * h : NB + 128 * h + 128]
        return high, low, jnp.concatenate([high, low], axis=1)

    def diagonal(h):
        high, _, pairs = pair(h)
        total = dot_tn(high, pairs)
        cross = total[:, 128:]
        return total[:, 0:128] + (cross + cross.T)

    def finish(h):
        wait(stages[h])
        faces(2, h, yb, yb2, 0.5)
        yb2[h, line(0, 15, 15), :] = jnp.zeros((195, 128), F32)
        y = yb2[h, 208:3120, :]
        top = y.astype(BF16)
        both[:, 128 * h : 128 * h + 128] = top
        both[:, NB + 128 * h : NB + 128 * h + 128] = (y - top.astype(F32)).astype(BF16)

    def members(me, count):
        return [(d, lax.rem(me + d, count)) for d in range(1, count)]

    def settle(copies):
        for copy in copies:
            copy.wait()

    def scatter_x(gl, ra, n):
        return [
            remote(gl.at[p], ra.at[dx], as_.at[n, d], ar_.at[n, d], (p, dy)) for d, p in members(dx, ndx)
        ]

    def scatter_y(gl, ra, sb, rb, n):
        chunk = gl[dx]
        for _, p in members(dx, ndx):
            chunk += ra[p]
        for p in range(16):
            sb[p] = chunk[(n + 1) * p : (n + 1) * p + n + 1]
        return [
            remote(sb.at[p], rb.at[dy], bs_.at[n, d], br_.at[n, d], (dx, p)) for d, p in members(dy, ndy)
        ]

    def gather_y(sb, rb, gb, n):
        piece = sb[dy]
        for _, p in members(dy, ndy):
            piece += rb[p]
        gb[dy] = piece
        return [
            remote(gb.at[dy], gb.at[dy], cs_.at[n, d], cr_.at[n, d], (dx, p)) for d, p in members(dy, ndy)
        ]

    def gather_x(gb, gf, n):
        for p in range(16):
            gf[dx, (n + 1) * p : (n + 1) * p + n + 1] = gb[p]
        return [
            remote(gf.at[dx], gf.at[dx], ds_.at[n, d], dr_.at[n, d], (p, dy)) for d, p in members(dx, ndx)
        ]

    finish(0)
    gl0[...] = diagonal(0).reshape(8, 16, 128)
    round0 = scatter_x(gl0, ra0, 0)
    finish(1)
    keep = pltpu.make_async_copy(both, yout, ysem)
    keep.start()
    total = dot_tn(both[:, 0:128], pair(1)[2])
    cross = dot_tn(both[:, NB : NB + 128], both[:, 128:NB])
    gl1[0:4] = (total[:, 0:128] + (total[:, 128:] + cross)).reshape(4, 32, 128)
    gl1[4:8] = diagonal(1).reshape(4, 32, 128)
    round1 = scatter_x(gl1, ra1, 1)
    settle(round0)
    round0 = scatter_y(gl0, ra0, sb0, rb0, 0)
    settle(round1)
    round1 = scatter_y(gl1, ra1, sb1, rb1, 1)
    settle(round0)
    round0 = gather_y(sb0, rb0, gb0, 0)
    settle(round1)
    round1 = gather_y(sb1, rb1, gb1, 1)
    settle(round0)
    round0 = gather_x(gb0, gf0, 0)
    settle(round1)
    round1 = gather_x(gb1, gf1, 1)

    def put(block, rows, cols):
        block = block * scale
        top = block.astype(BF16)
        low = (block - top.astype(F32)).astype(BF16)
        for start, value in ((0, top), (NB, top), (2 * NB, low)):
            wout[rows, start + cols : start + cols + 128] = value

    settle(round0)
    work[...] = gf0[...].reshape(128, 128)
    w1 = factor_inverse(work, pivots)
    put(w1, slice(0, 128), 0)
    put(jnp.zeros((128, 128), F32), slice(0, 128), 128)
    settle(round1)
    rows01 = gf1[0:4].reshape(128, 128)
    upper = exact(w1, rows01, 1)
    work[...] = gf1[4:8].reshape(128, 128) - exact(upper, upper, 0)
    mid = exact(upper, w1, 0)
    w2 = factor_inverse(work, pivots)
    put(w2, slice(128, NB), 128)
    put(-exact(w2, mid, 1), slice(128, NB), 0)
    keep.wait()


def split3(x):
    a = x.astype(BF16)
    rest = x - a.astype(F32)
    b = rest.astype(BF16)
    return a, b, (rest - b.astype(F32)).astype(BF16)


def exact(left, right, dim):
    l1, l2, l3 = split3(left)
    r1, r2, r3 = split3(right)
    left = jnp.concatenate([l1, l1, l1, l2, l2, l3], axis=dim)
    right = jnp.concatenate([r1, r2, r3, r1, r2, r1], axis=0)
    return lax.dot_general(left, right, (((dim,), (0,)), ((), ())), preferred_element_type=F32)


def factor_inverse(work, pivots):
    rows = lax.broadcasted_iota(jnp.int32, (8, 128), 0)
    lanes = lax.broadcasted_iota(jnp.int32, (8, 128), 1)

    def step(o, carry):
        tiles = [work[8 * t : 8 * t + 8, :] for t in range(4)]
        factors = []
        for s in range(4):
            first = 8 * s
            inside = jnp.logical_and(lanes >= first, lanes < first + 8)
            columns = []
            for q in range(s, 4):
                tile = tiles[q]
                columns.append(
                    [jnp.broadcast_to(tile[:, first + j : first + j + 1], (8, 128)) for j in range(8)]
                )
                fresh = jnp.where(lanes == rows + first, 1.0, 0.0) if q == s else 0.0
                tiles[q] = jnp.where(inside, fresh, tile)
            scale = jnp.ones((8, 128), F32)
            factor = jnp.ones((8, 128), F32)
            for k in range(8):
                lead = [jnp.broadcast_to(columns[0][j][k : k + 1, :], (8, 128)) for j in range(k, 8)]
                inv = 1.0 / lead[0]
                scale = jnp.where(rows == k, lead[0], scale)
                factor = jnp.where(rows == k, inv, factor)
                pivot = jnp.broadcast_to(tiles[s][k : k + 1, :], (8, 128)) * inv
                lead = [v * inv for v in lead]
                for q in range(s, 4):
                    if q == s and k == 7:
                        continue
                    column = columns[q - s][k]
                    if q == s:
                        column = jnp.where(rows > k, column, 0.0)
                    for j in range(k + 1, 8):
                        columns[q - s][j] = columns[q - s][j] - column * lead[j - k]
                    tiles[q] = tiles[q] - column * pivot
            pivots[pl.ds(32 * o + 8 * s, 8), :] = lax.rsqrt(scale)
            factors.append(factor)
        u = jnp.concatenate(tiles, axis=0)
        r = lax.broadcasted_iota(jnp.int32, (32, 128), 0)
        c = lax.broadcasted_iota(jnp.int32, (32, 128), 1)
        v = jnp.where(jnp.logical_and(c > r, c < 32), 0.0, u * jnp.concatenate(factors, axis=0))
        change = exact(u, v, 0)
        old = work[32:128, :]
        r = lax.broadcasted_iota(jnp.int32, (96, 128), 0)
        c = lax.broadcasted_iota(jnp.int32, (96, 128), 1)
        fresh = jnp.where(c < 32, 0.0, old) - change[32:128, :]
        work[0:96, :] = pltpu.roll(jnp.where(r < 96 - 32 * o, fresh, old), 96, 1)
        work[96:128, :] = pltpu.roll(u, 96, 1)
        return carry

    lax.fori_loop(0, 4, step, 0)
    r = lax.broadcasted_iota(jnp.int32, (128, 128), 0)
    c = lax.broadcasted_iota(jnp.int32, (128, 128), 1)
    return jnp.where(c <= r, work[...] * pivots[...], 0.0)


def basis_kernel(y, w, out, ybuf, stage, yin, osem):
    loads = []
    for i in range(14):
        rows = pl.ds(208 * i, 208)
        load = pltpu.make_async_copy(y.at[rows], ybuf.at[rows], yin.at[i])
        load.start()
        loads.append(load)
    copies = []
    for i in range(14):
        loads[i].wait()
        rows = slice(208 * i, 208 * i + 208)
        q = dot_nt(ybuf[rows, :], w[:, 0 : 2 * NB]) + dot_nt(ybuf[rows, 0:NB], w[:, 2 * NB :])
        stage[i] = q.reshape(13, 16, NB)[:, 0:14, :]
        copy = pltpu.make_async_copy(stage.at[i], out.at[i], osem.at[i])
        copy.start()
        copies.append(copy)
    for copy in copies:
        copy.wait()


def solution(mesh):
    ndx, ndy = mesh.shape["dx"], mesh.shape["dy"]
    vmem = pl.BlockSpec(memory_space=pltpu.VMEM)
    anywhere = pl.BlockSpec(memory_space=pl.ANY)
    scale = math.sqrt(14 * 14 * 13 * ndx * ndy)

    def shards(orbitals, elem_mats, conn):
        dma = pltpu.SemaphoreType.DMA
        y, w = pl.pallas_call(
            lambda *refs: filter_kernel(ndx, ndy, scale, *refs),
            out_shape=(
                jax.ShapeDtypeStruct((2912, 2 * NB), BF16),
                jax.ShapeDtypeStruct((NB, 3 * NB), BF16),
            ),
            in_specs=[anywhere, anywhere, vmem],
            out_specs=(anywhere, vmem),
            scratch_shapes=[
                pltpu.VMEM((14, 13, 14, NB), BF16),
                pltpu.VMEM((8, 512, 512), BF16),
                pltpu.VMEM((8, 448, 448), BF16),
                pltpu.VMEM((2, 448, 128), jnp.int32),
                pltpu.VMEM((448, 512), BF16),
                pltpu.VMEM((512, 448), BF16),
                pltpu.VMEM((2, 3120, 128), F32),
                pltpu.VMEM((2, 3120, 128), F32),
                pltpu.VMEM((2, 3120, 128), F32),
                pltpu.VMEM((2912, 2 * NB), BF16),
                pltpu.VMEM((2, 13, 14, 128), BF16),
                pltpu.VMEM((2, 182, 128), BF16),
                pltpu.VMEM((2, 13, 128), BF16),
                pltpu.VMEM((2, 182, 128), BF16),
                pltpu.VMEM((2, 13, 128), BF16),
                pltpu.VMEM((3, 2, 13, 16, 128), BF16),
                pltpu.VMEM((2, 2, 13, 16, 128), BF16),
                pltpu.VMEM((3, 2, 195, 128), BF16),
                pltpu.VMEM((2, 2, 195, 128), BF16),
                pltpu.VMEM((3, 4, 2, 13, 128), BF16),
                pltpu.VMEM((2, 2, 13, 16, 128), BF16),
                pltpu.VMEM((3, 2, 13, 16, 128), BF16),
                pltpu.VMEM((2, 2, 195, 128), BF16),
                pltpu.VMEM((3, 2, 195, 128), BF16),
                pltpu.VMEM((3, 4, 2, 13, 128), BF16),
                pltpu.VMEM((8, 16, 128), F32),
                pltpu.VMEM((8, 16, 128), F32),
                pltpu.VMEM((8, 16, 128), F32),
                pltpu.VMEM((8, 32, 128), F32),
                pltpu.VMEM((8, 32, 128), F32),
                pltpu.VMEM((8, 32, 128), F32),
                pltpu.VMEM((16, 1, 128), F32),
                pltpu.VMEM((16, 1, 128), F32),
                pltpu.VMEM((16, 1, 128), F32),
                pltpu.VMEM((16, 2, 128), F32),
                pltpu.VMEM((16, 2, 128), F32),
                pltpu.VMEM((16, 2, 128), F32),
                pltpu.VMEM((128, 128), F32),
                pltpu.VMEM((128, 128), F32),
                dma,
                dma((8,)),
                dma,
                dma((2, 3)),
                dma((2, 3)),
                dma((3, 2, 8)),
                dma((3, 2, 8)),
                dma((2, 8)),
                dma((2, 8)),
                dma((2, 16)),
                dma((2, 16)),
                dma((2, 16)),
                dma((2, 16)),
                dma((2, 8)),
                dma((2, 8)),
            ],
            compiler_params=pltpu.CompilerParams(collective_id=0, has_side_effects=True),
            name="filter",
        )(jnp.swapaxes(orbitals, 1, 2), elem_mats, conn)
        filtered = pl.pallas_call(
            basis_kernel,
            out_shape=jax.ShapeDtypeStruct((14, 13, 14, NB), F32),
            in_specs=[anywhere, vmem],
            out_specs=anywhere,
            scratch_shapes=[
                pltpu.VMEM((2912, 2 * NB), BF16),
                pltpu.VMEM((14, 13, 14, NB), F32),
                dma((14,)),
                dma((14,)),
            ],
            name="basis",
        )(y, w)
        return jnp.swapaxes(filtered, 1, 2)

    in_specs = (
        P("dx", "dy", None, None),
        P("dx", "dy", None, None, None),
        P("dx", "dy", None, None),
    )
    out_specs = P("dx", "dy", None, None)
    return jax.shard_map(shards, mesh=mesh, in_specs=in_specs, out_specs=out_specs, check_vma=False)
```

```python
import math

import jax
import jax.numpy as jnp
from jax import lax
from jax.experimental import pallas as pl
from jax.experimental.pallas import tpu as pltpu
from jax.sharding import PartitionSpec as P

MESH = pl.DeviceIdType.MESH
F32 = jnp.float32
BF16 = jnp.bfloat16
NB = 256


def dot_nn(a, b, precision=None):
    return lax.dot_general(
        a, b, (((1,), (0,)), ((), ())), precision=precision, preferred_element_type=F32
    )


def dot_nt(a, b, precision=None):
    return lax.dot_general(
        a, b, (((1,), (1,)), ((), ())), precision=precision, preferred_element_type=F32
    )


def dot_tn(a, b, precision=None):
    return lax.dot_general(
        a, b, (((0,), (0,)), ((), ())), precision=precision, preferred_element_type=F32
    )


def filter_kernel(
    ndx, ndy,
    orb, mats, conn,
    yout, gout,
    obuf, abuf, ap, rmap, st, tt, ya2, yb2, acc2, both,
    hx, hy, hc, shy, shc, sxl, sxh, syl, syh, scs, rxl, rxh, ryl, ryh, rcs,
    gl, ra, sb, rb, gb, gf,
    osem, msem, ysem, hss, hrs, ess, ers, as_, ar_, bs_, br_, cs_, cr_, ds_, dr_,
):
    dx = lax.axis_index("dx")
    dy = lax.axis_index("dy")
    xp, xm = lax.rem(dx + 1, ndx), lax.rem(dx + ndx - 1, ndx)
    yp, ym = lax.rem(dy + 1, ndy), lax.rem(dy + ndy - 1, ndy)
    ya, yb, acc = (ref.reshape(2, 15, 13, 16, 128) for ref in (ya2, yb2, acc2))

    barrier = pltpu.get_barrier_semaphore()
    partners = [(lax.rem(dx + d, ndx), dy) for d in range(1, ndx)]
    partners += [(dx, lax.rem(dy + d, ndy)) for d in range(1, ndy)]
    partners += [(xp, yp), (xp, ym), (xm, yp), (xm, ym)]
    for partner in partners:
        pl.semaphore_signal(barrier, inc=1, device_id=partner, device_id_type=MESH)

    first_load = pltpu.make_async_copy(orb, obuf, osem)
    first_load.start()
    loads = []
    for e in range(8):
        copy = pltpu.make_async_copy(mats.at[e // 4, e // 2 % 2, e % 2], abuf.at[e], msem.at[e])
        copy.start()
        loads.append(copy)

    grid = (8, 7, 8, 128)
    a_of, l_of, s_of = (lax.broadcasted_iota(jnp.int32, grid, d) for d in range(3))
    for ey in range(2):
        b_of = jnp.where(s_of < 7 - ey, s_of + 1 + ey, s_of - 7 + ey)
        rmap[ey] = (a_of * 225 + b_of * 15 + l_of).reshape(448, 128)

    def line(i, slot, count):
        return pl.ds(i * 208 + slot, 13 * count, stride=16)

    for h in range(2):
        ya2[h, 0:208, :] = jnp.zeros((208, 128), F32)
        ya2[h, line(1, 14, 14), :] = jnp.zeros((182, 128), F32)
        ya2[h, line(1, 15, 14), :] = jnp.zeros((182, 128), F32)
    first_load.wait()

    def fill(i, carry):
        plane = obuf[i].astype(F32)
        for h in range(2):
            ya[h, i + 1, :, 0:14, :] = plane[:, :, 128 * h : 128 * h + 128]
        return carry

    lax.fori_loop(0, 14, fill, 0)

    for h in range(2):
        shy[h] = ya2[h, line(1, 13, 14), :].astype(BF16)
        shc[h] = ya2[h, line(14, 13, 1), :].astype(BF16)

    def fold(c):
        ex, ey = c // 2, c % 2
        links = conn[ex, ey]
        for ez in range(2):
            e = c * 2 + ez
            loads[e].wait()
            row = links[ez : ez + 1] - ((7 * ex * 15 + 7 * ey) * 15 + 7 * ez + 1 - ez)
            for q in range(4):
                part = row[:, 128 * q : 128 * q + 128]
                st[:, 128 * q : 128 * q + 128] = jnp.where(rmap[ey] == part, 1.0, 0.0).astype(BF16)
            tt[...] = dot_nt(abuf[e], st[...]).astype(BF16)
            ap[e] = dot_nn(st[...], tt[...]).astype(BF16)

    def remote(src, dst, ssem, rsem, where):
        copy = pltpu.make_async_remote_copy(
            src_ref=src, dst_ref=dst, send_sem=ssem, recv_sem=rsem, device_id=where, device_id_type=MESH
        )
        copy.start()
        return copy

    x_low, x_high, y_low, y_high = dx > 0, dx < ndx - 1, dy > 0, dy < ndy - 1

    def toward(src, dst, ssem, rsem, sx, sy):
        where = (dx + sx, dy + sy)
        copy = pltpu.make_async_remote_copy(
            src_ref=src, dst_ref=dst, send_sem=ssem, recv_sem=rsem, device_id=where, device_id_type=MESH
        )
        ahead = [f for f in ({1: x_high, -1: x_low}.get(sx), {1: y_high, -1: y_low}.get(sy)) if f is not None]
        behind = [f for f in ({1: x_low, -1: x_high}.get(sx), {1: y_low, -1: y_high}.get(sy)) if f is not None]
        ahead = ahead[0] if len(ahead) == 1 else jnp.logical_and(*ahead)
        behind = behind[0] if len(behind) == 1 else jnp.logical_and(*behind)

        @pl.when(ahead)
        def _():
            copy.start()

        return copy, ahead, behind

    def wait(copies):
        for copy, ahead, behind in copies:

            @pl.when(behind)
            def _():
                copy.wait_recv()

            @pl.when(ahead)
            def _():
                copy.wait_send()

    fold(0)
    pl.semaphore_wait(barrier, len(partners))
    halo = []
    for h in range(2):
        half = obuf.at[13, :, :, 128 * h : 128 * h + 128]
        halo.append(
            [
                toward(shc.at[h], hc.at[h], hss.at[h, 2], hrs.at[h, 2], 1, 1),
                toward(shy.at[h], hy.at[h], hss.at[h, 1], hrs.at[h, 1], 0, 1),
                toward(half, hx.at[h], hss.at[h, 0], hrs.at[h, 0], 1, 0),
            ]
        )
    for c in range(1, 4):
        fold(c)

    sub = lax.broadcasted_iota(jnp.int32, (8, 7, 8, 128), 2)

    def apply(src, h):
        for ex in range(2):
            for ez in range(2):
                i0, l0 = 7 * ex, 6 * ez
                rows, layers = slice(i0, i0 + 8), slice(l0, l0 + 7)
                n0 = src[h, rows, layers, 0:8]
                n1 = src[h, rows, layers, 8:16]
                t0 = jnp.where(sub < 7, n0, n1).reshape(448, 128).astype(BF16)
                t1 = jnp.where(sub < 6, n1, n0).reshape(448, 128).astype(BF16)
                p0 = dot_nn(ap[4 * ex + ez], t0).reshape(8, 7, 8, 128)
                p1 = dot_nn(ap[4 * ex + 2 + ez], t1).reshape(8, 7, 8, 128)
                m0 = jnp.where(sub < 7, p0, 0.0) + jnp.where(sub < 6, 0.0, p1)
                m1 = jnp.where(sub < 6, p1, 0.0) + jnp.where(sub < 7, 0.0, p0)
                for part, tile in ((m0, slice(0, 8)), (m1, slice(8, 16))):
                    if ex:
                        first = part[:1, ez:] + acc[h, 7:8, l0 + ez : l0 + 7, tile]
                        rest = jnp.concatenate([first, part[1:, ez:]], axis=0)
                    else:
                        rest = part[:, ez:]
                    if ez:
                        joint = part[:, :1] + acc[h, rows, l0 : l0 + 1, tile]
                        rest = jnp.concatenate([joint, rest], axis=1)
                    acc[h, rows, layers, tile] = rest

    def exchange(t, h):
        copies = []

        def send(n, src, dst, sx, sy):
            copies.append(toward(src, dst, ess.at[t, h, n], ers.at[t, h, n], sx, sy))

        corners = [(0, 15, -1, -1), (14, 13, 1, 1), (0, 13, -1, 1), (14, 15, 1, -1)]
        count = 4 if t < 2 else 1
        for n, (i, slot, _, _) in enumerate(corners[:count]):
            scs[t, n, h] = acc2[h, line(i, slot, 1), :].astype(BF16)
        syl[t, h] = acc2[h, line(0, 15, 15), :].astype(BF16)
        if t < 2:
            syh[t, h] = acc2[h, line(0, 13, 15), :].astype(BF16)
        sxl[t, h] = acc[h, 0].astype(BF16)
        if t < 2:
            sxh[t, h] = acc[h, 14].astype(BF16)
        for n, (_, _, sx, sy) in enumerate(corners[:count]):
            send(4 + n, scs.at[t, n, h], rcs.at[t, n, h], sx, sy)
        send(0, syl.at[t, h], ryh.at[t, h], 0, -1)
        if t < 2:
            send(1, syh.at[t, h], ryl.at[t, h], 0, 1)
        send(2, sxl.at[t, h], rxh.at[t, h], -1, 0)
        if t < 2:
            send(3, sxh.at[t, h], rxl.at[t, h], 1, 0)
        return copies

    def gated(flag, value, coef):
        return jnp.where(flag, value.astype(F32), 0.0) * coef

    def faces(t, h, y, y2, coef):
        def bump(i, slot, count, value):
            y2[h, line(i, slot, count), :] += value

        y[h, 14] += gated(x_high, rxh[t, h], coef)
        bump(0, 13, 15, gated(y_high, ryh[t, h], coef))
        bump(14, 13, 1, gated(jnp.logical_and(x_high, y_high), rcs[t, 0, h], coef))
        if t < 2:
            y[h, 0] += rxl[t, h].astype(F32) * coef
            bump(0, 15, 15, ryl[t, h].astype(F32) * coef)
            bump(0, 15, 1, rcs[t, 1, h].astype(F32) * coef)
            bump(14, 15, 1, gated(x_high, rcs[t, 2, h], coef))
            bump(0, 13, 1, gated(y_high, rcs[t, 3, h], coef))
            y[h, 0] = jnp.where(x_low, y[h, 0], 0.0)
            edge = y2[h, line(0, 15, 15), :]
            y2[h, line(0, 15, 15), :] = jnp.where(y_low, edge, 0.0)

    stages = []
    for h in range(2):
        wait(halo[h])
        ya[h, 0, :, 0:14, :] = jnp.where(x_low, hx[h].astype(F32), 0.0)
        ya2[h, line(1, 15, 14), :] = jnp.where(y_low, hy[h].astype(F32), 0.0)
        ya2[h, line(0, 15, 1), :] = jnp.where(
            jnp.logical_and(x_low, y_low), hc[h].astype(F32), 0.0
        )
        apply(ya, h)
        stages.append(exchange(0, h))
    for h in range(2):
        yb2[h] = 0.25 * acc2[h] - 0.375 * ya2[h]
    for h in range(2):
        wait(stages[h])
        faces(0, h, yb, yb2, 0.25)
        apply(yb, h)
        stages[h] = exchange(1, h)
    for h in range(2):
        ya2[h] = 0.5 * acc2[h] - 0.75 * yb2[h] - ya2[h]
    for h in range(2):
        wait(stages[h])
        faces(1, h, ya, ya2, 0.5)
        apply(ya, h)
        stages[h] = exchange(2, h)
    for h in range(2):
        yb2[h] = 0.5 * acc2[h] - 0.75 * ya2[h] - yb2[h]

    def pair(h):
        high = both[:, 128 * h : 128 * h + 128]
        low = both[:, NB + 128 * h : NB + 128 * h + 128]
        return high, low, jnp.concatenate([high, low], axis=1)

    def diagonal(h):
        high, _, pairs = pair(h)
        total = dot_tn(high, pairs)
        cross = total[:, 128:]
        return total[:, 0:128] + (cross + cross.T)

    for h in range(2):
        wait(stages[h])
        faces(2, h, yb, yb2, 0.5)
        yb2[h, line(0, 15, 15), :] = jnp.zeros((195, 128), F32)
        y = yb2[h, 208:3120, :]
        top = y.astype(BF16)
        both[:, 128 * h : 128 * h + 128] = top
        both[:, NB + 128 * h : NB + 128 * h + 128] = (y - top.astype(F32)).astype(BF16)
        block = diagonal(h)
        if h == 0:
            grams = [block]
        else:
            total = dot_tn(both[:, 0:128], pair(1)[2])
            cross = dot_tn(both[:, NB : NB + 128], both[:, 128:NB])
            grams += [total[:, 0:128] + (total[:, 128:] + cross), block]
    keep = pltpu.make_async_copy(both, yout, ysem)
    keep.start()
    gl[...] = jnp.concatenate(grams, axis=0).reshape(8, 48, 128)

    copies = []
    for d in range(1, ndx):
        peer = lax.rem(dx + d, ndx)
        copies.append(remote(gl.at[peer], ra.at[dx], as_.at[d], ar_.at[d], (peer, dy)))
    for copy in copies:
        copy.wait()
    chunk = gl[dx]
    for d in range(1, ndx):
        chunk += ra[lax.rem(dx + d, ndx)]
    for p in range(16):
        sb[p] = chunk[3 * p : 3 * p + 3]
    copies = []
    for d in range(1, ndy):
        peer = lax.rem(dy + d, ndy)
        copies.append(remote(sb.at[peer], rb.at[dy], bs_.at[d], br_.at[d], (dx, peer)))
    for copy in copies:
        copy.wait()
    piece = sb[dy]
    for d in range(1, ndy):
        piece += rb[lax.rem(dy + d, ndy)]
    gb[dy] = piece
    copies = []
    for d in range(1, ndy):
        peer = lax.rem(dy + d, ndy)
        copies.append(remote(gb.at[dy], gb.at[dy], cs_.at[d], cr_.at[d], (dx, peer)))
    for copy in copies:
        copy.wait()
    for p in range(16):
        gf[dx, 3 * p : 3 * p + 3] = gb[p]
    copies = []
    for d in range(1, ndx):
        peer = lax.rem(dx + d, ndx)
        copies.append(remote(gf.at[dx], gf.at[dx], ds_.at[d], dr_.at[d], (peer, dy)))
    for copy in copies:
        copy.wait()
    grams = gf[...].reshape(384, 128)
    gout[0:128, 0:128] = grams[0:128]
    gout[0:128, 128:NB] = grams[128:NB]
    gout[128:NB, 0:128] = jnp.zeros((128, 128), F32)
    gout[128:NB, 128:NB] = grams[NB:384]
    keep.wait()


def split3(x):
    a = x.astype(BF16)
    rest = x - a.astype(F32)
    b = rest.astype(BF16)
    return a, b, (rest - b.astype(F32)).astype(BF16)


def factor_inverse(g, work, ones):
    ones[...] = jnp.ones((8, 128), F32)
    one = ones[...]
    rows = lax.broadcasted_iota(jnp.int32, (8, 128), 0)
    lanes = lax.broadcasted_iota(jnp.int32, (8, 128), 1)
    scales = []
    for o in range(8):
        base = 32 * o
        source = g if o == 0 else work
        tiles = [
            [source[base + 8 * t : base + 8 * t + 8, 128 * h : 128 * h + 128] for h in range(2)]
            for t in range(4)
        ]
        factors = []
        half = base // 128
        for s in range(4):
            first = base + 8 * s - 128 * half
            inside = jnp.logical_and(lanes >= first, lanes < first + 8)
            columns = []
            for q in range(s, 4):
                tile = tiles[q][half]
                columns.append(
                    [
                        jnp.broadcast_to(tile[:, first + j : first + j + 1], (8, 128)) * one
                        for j in range(8)
                    ]
                )
                fresh = jnp.where(lanes == rows + first, 1.0, 0.0) if q == s else 0.0
                tiles[q][half] = jnp.where(inside, fresh, tile)
            scale = jnp.ones((8, 128), F32)
            factor = jnp.ones((8, 128), F32)
            for k in range(8):
                lead = [jnp.broadcast_to(columns[0][j][k : k + 1, :], (8, 128)) for j in range(k, 8)]
                inv = 1.0 / lead[0]
                scale = jnp.where(rows == k, lead[0], scale)
                factor = jnp.where(rows == k, inv, factor)
                pivot = [jnp.broadcast_to(tiles[s][h][k : k + 1, :], (8, 128)) * inv for h in range(2)]
                ready = [v * inv for v in lead]
                for q in range(s, 4):
                    if q == s and k == 7:
                        continue
                    column = columns[q - s][k]
                    if q == s:
                        column = jnp.where(rows > k, column, 0.0)
                    for j in range(k + 1, 8):
                        if q == s:
                            change = (column * lead[j - k]) * inv
                        else:
                            change = column * ready[j - k]
                        columns[q - s][j] = columns[q - s][j] - change
                    for h in range(2):
                        tiles[q][h] = tiles[q][h] - column * pivot[h]
            scales.append(lax.rsqrt(scale))
            factors.append(factor)
        for t in range(4):
            for h in range(2):
                work[base + 8 * t : base + 8 * t + 8, 128 * h : 128 * h + 128] = tiles[t][h]
        if o < 7:
            u = jnp.concatenate([jnp.concatenate(tiles[t], axis=1) for t in range(4)], axis=0)
            f = jnp.concatenate([jnp.concatenate([v, v], axis=1) for v in factors], axis=0)
            r = lax.broadcasted_iota(jnp.int32, (32, NB), 0) + base
            c = lax.broadcasted_iota(jnp.int32, (32, NB), 1)
            v = jnp.where(jnp.logical_and(c > r, c < base + 32), 0.0, u * f)
            start = 128 * ((base + 32) // 128)
            u1, u2, u3 = split3(u[:, start:])
            v1, v2, v3 = split3(v)
            left = jnp.concatenate([u1, u1, u1, u2, u2, u3], axis=0)
            right = jnp.concatenate([v1, v2, v3, v1, v2, v1], axis=0)
            change = lax.dot_general(
                left, right, (((0,), (0,)), ((), ())), preferred_element_type=F32
            )
            rest = slice(base + 32, NB)
            old = (g if o == 0 else work)[rest, :]
            cc = lax.broadcasted_iota(jnp.int32, old.shape, 1)
            old = jnp.where(jnp.logical_and(cc >= base, cc < base + 32), 0.0, old)
            work[rest, :] = old - change[base + 32 - start :, :]
    for t in range(32):
        for h in range(2):
            tile = work[8 * t : 8 * t + 8, 128 * h : 128 * h + 128] * scales[t]
            work[8 * t : 8 * t + 8, 128 * h : 128 * h + 128] = jnp.where(
                lanes + 128 * h <= rows + 8 * t, tile, 0.0
            )


def basis_kernel(scale, y, g, out, ybuf, stage, work, ones, weights, yin, osem):
    load = pltpu.make_async_copy(y, ybuf, yin)
    load.start()
    factor_inverse(g, work, ones)
    w = work[...].T * scale
    top = w.astype(BF16)
    weights[0:NB] = top
    weights[NB : 2 * NB] = top
    weights[2 * NB :] = (w - top.astype(F32)).astype(BF16)
    load.wait()
    copies = []
    for start, count in ((0, 4), (4, 4), (8, 4), (12, 2)):
        rows = slice(208 * start, 208 * (start + count))
        left = jnp.concatenate([ybuf[rows, :], ybuf[rows, 0:NB]], axis=1)
        q = dot_nn(left, weights[...]).reshape(count, 13, 16, NB)
        planes = slice(start, start + count)
        stage[planes] = q[:, :, 0:14, :]
        copy = pltpu.make_async_copy(stage.at[planes], out.at[planes], osem.at[start])
        copy.start()
        copies.append(copy)
    for copy in copies:
        copy.wait()


def solution(mesh):
    ndx, ndy = mesh.shape["dx"], mesh.shape["dy"]
    vmem = pl.BlockSpec(memory_space=pltpu.VMEM)
    anywhere = pl.BlockSpec(memory_space=pl.ANY)
    scale = math.sqrt(14 * 14 * 13 * ndx * ndy)

    def shards(orbitals, elem_mats, conn):
        dma = pltpu.SemaphoreType.DMA
        y, g = pl.pallas_call(
            lambda *refs: filter_kernel(ndx, ndy, *refs),
            out_shape=(
                jax.ShapeDtypeStruct((2912, 2 * NB), BF16),
                jax.ShapeDtypeStruct((NB, NB), F32),
            ),
            in_specs=[anywhere, anywhere, vmem],
            out_specs=(anywhere, vmem),
            scratch_shapes=[
                pltpu.VMEM((14, 13, 14, NB), BF16),
                pltpu.VMEM((8, 512, 512), BF16),
                pltpu.VMEM((8, 448, 448), BF16),
                pltpu.VMEM((2, 448, 128), jnp.int32),
                pltpu.VMEM((448, 512), BF16),
                pltpu.VMEM((512, 448), BF16),
                pltpu.VMEM((2, 3120, 128), F32),
                pltpu.VMEM((2, 3120, 128), F32),
                pltpu.VMEM((2, 3120, 128), F32),
                pltpu.VMEM((2912, 2 * NB), BF16),
                pltpu.VMEM((2, 13, 14, 128), BF16),
                pltpu.VMEM((2, 182, 128), BF16),
                pltpu.VMEM((2, 13, 128), BF16),
                pltpu.VMEM((2, 182, 128), BF16),
                pltpu.VMEM((2, 13, 128), BF16),
                pltpu.VMEM((3, 2, 13, 16, 128), BF16),
                pltpu.VMEM((2, 2, 13, 16, 128), BF16),
                pltpu.VMEM((3, 2, 195, 128), BF16),
                pltpu.VMEM((2, 2, 195, 128), BF16),
                pltpu.VMEM((3, 4, 2, 13, 128), BF16),
                pltpu.VMEM((2, 2, 13, 16, 128), BF16),
                pltpu.VMEM((3, 2, 13, 16, 128), BF16),
                pltpu.VMEM((2, 2, 195, 128), BF16),
                pltpu.VMEM((3, 2, 195, 128), BF16),
                pltpu.VMEM((3, 4, 2, 13, 128), BF16),
                pltpu.VMEM((8, 48, 128), F32),
                pltpu.VMEM((8, 48, 128), F32),
                pltpu.VMEM((16, 3, 128), F32),
                pltpu.VMEM((16, 3, 128), F32),
                pltpu.VMEM((16, 3, 128), F32),
                pltpu.VMEM((8, 48, 128), F32),
                dma,
                dma((8,)),
                dma,
                dma((2, 3)),
                dma((2, 3)),
                dma((3, 2, 8)),
                dma((3, 2, 8)),
                dma((8,)),
                dma((8,)),
                dma((16,)),
                dma((16,)),
                dma((16,)),
                dma((16,)),
                dma((8,)),
                dma((8,)),
            ],
            compiler_params=pltpu.CompilerParams(collective_id=0, has_side_effects=True),
            name="filter",
        )(jnp.swapaxes(orbitals, 1, 2), elem_mats, conn)
        filtered = pl.pallas_call(
            lambda *refs: basis_kernel(scale, *refs),
            out_shape=jax.ShapeDtypeStruct((14, 13, 14, NB), F32),
            in_specs=[anywhere, vmem],
            out_specs=anywhere,
            scratch_shapes=[
                pltpu.VMEM((2912, 2 * NB), BF16),
                pltpu.VMEM((14, 13, 14, NB), F32),
                pltpu.VMEM((NB, NB), F32),
                pltpu.VMEM((8, 128), F32),
                pltpu.VMEM((3 * NB, NB), BF16),
                dma,
                dma((14,)),
            ],
            name="basis",
        )(y, g)
        return jnp.swapaxes(filtered, 1, 2)

    in_specs = (
        P("dx", "dy", None, None),
        P("dx", "dy", None, None, None),
        P("dx", "dy", None, None),
    )
    out_specs = P("dx", "dy", None, None)
    return jax.shard_map(shards, mesh=mesh, in_specs=in_specs, out_specs=out_specs, check_vma=False)
```

```python
import math

import jax
import jax.numpy as jnp
from jax import lax
from jax.experimental import pallas as pl
from jax.experimental.pallas import tpu as pltpu
from jax.sharding import PartitionSpec as P

MESH = pl.DeviceIdType.MESH
F32 = jnp.float32
BF16 = jnp.bfloat16
NB = 256


def dot_nn(a, b, precision=None):
    return lax.dot_general(
        a, b, (((1,), (0,)), ((), ())), precision=precision, preferred_element_type=F32
    )


def dot_nt(a, b, precision=None):
    return lax.dot_general(
        a, b, (((1,), (1,)), ((), ())), precision=precision, preferred_element_type=F32
    )


def dot_tn(a, b, precision=None):
    return lax.dot_general(
        a, b, (((0,), (0,)), ((), ())), precision=precision, preferred_element_type=F32
    )


def filter_kernel(
    ndx, ndy,
    orb, mats, conn,
    yout, gout,
    obuf, abuf, ap, rmap, st, tt, ya2, yb2, acc2, both,
    hx, hy, hc, shy, shc, sxl, sxh, syl, syh, scs, rxl, rxh, ryl, ryh, rcs,
    gl, ra, gb, gf,
    osem, msem, ysem, hss, hrs, ess, ers, as_, ar_, bs_, br_, cs_, cr_,
):
    dx = lax.axis_index("dx")
    dy = lax.axis_index("dy")
    xp, xm = lax.rem(dx + 1, ndx), lax.rem(dx + ndx - 1, ndx)
    yp, ym = lax.rem(dy + 1, ndy), lax.rem(dy + ndy - 1, ndy)
    ya, yb, acc = (ref.reshape(2, 15, 13, 16, 128) for ref in (ya2, yb2, acc2))

    barrier = pltpu.get_barrier_semaphore()
    partners = [(lax.rem(dx + d, ndx), dy) for d in range(1, ndx)]
    partners += [(dx, lax.rem(dy + d, ndy)) for d in range(1, ndy)]
    partners += [(xp, yp), (xp, ym), (xm, yp), (xm, ym)]
    for partner in partners:
        pl.semaphore_signal(barrier, inc=1, device_id=partner, device_id_type=MESH)

    first_load = pltpu.make_async_copy(orb, obuf, osem)
    first_load.start()
    loads = []
    for e in range(8):
        copy = pltpu.make_async_copy(mats.at[e // 4, e // 2 % 2, e % 2], abuf.at[e], msem.at[e])
        copy.start()
        loads.append(copy)

    grid = (8, 7, 8, 128)
    a_of, l_of, s_of = (lax.broadcasted_iota(jnp.int32, grid, d) for d in range(3))
    for ey in range(2):
        b_of = jnp.where(s_of < 7 - ey, s_of + 1 + ey, s_of - 7 + ey)
        rmap[ey] = (a_of * 225 + b_of * 15 + l_of).reshape(448, 128)

    def line(i, slot, count):
        return pl.ds(i * 208 + slot, 13 * count, stride=16)

    for h in range(2):
        ya2[h, 0:208, :] = jnp.zeros((208, 128), F32)
        ya2[h, line(1, 14, 14), :] = jnp.zeros((182, 128), F32)
        ya2[h, line(1, 15, 14), :] = jnp.zeros((182, 128), F32)
    first_load.wait()

    def fill(i, carry):
        plane = obuf[i].astype(F32)
        for h in range(2):
            ya[h, i + 1, :, 0:14, :] = plane[:, :, 128 * h : 128 * h + 128]
        return carry

    lax.fori_loop(0, 14, fill, 0)

    for h in range(2):
        shy[h] = ya2[h, line(1, 13, 14), :].astype(BF16)
        shc[h] = ya2[h, line(14, 13, 1), :].astype(BF16)

    def fold(c):
        ex, ey = c // 2, c % 2
        links = conn[ex, ey]
        for ez in range(2):
            e = c * 2 + ez
            loads[e].wait()
            row = links[ez : ez + 1] - ((7 * ex * 15 + 7 * ey) * 15 + 7 * ez + 1 - ez)
            for q in range(4):
                part = row[:, 128 * q : 128 * q + 128]
                st[:, 128 * q : 128 * q + 128] = jnp.where(rmap[ey] == part, 1.0, 0.0).astype(BF16)
            tt[...] = dot_nt(abuf[e], st[...]).astype(BF16)
            ap[e] = dot_nn(st[...], tt[...]).astype(BF16)

    def remote(src, dst, ssem, rsem, where):
        copy = pltpu.make_async_remote_copy(
            src_ref=src, dst_ref=dst, send_sem=ssem, recv_sem=rsem, device_id=where, device_id_type=MESH
        )
        copy.start()
        return copy

    x_low, x_high, y_low, y_high = dx > 0, dx < ndx - 1, dy > 0, dy < ndy - 1

    def toward(src, dst, ssem, rsem, sx, sy):
        where = (dx + sx, dy + sy)
        copy = pltpu.make_async_remote_copy(
            src_ref=src, dst_ref=dst, send_sem=ssem, recv_sem=rsem, device_id=where, device_id_type=MESH
        )
        ahead = [f for f in ({1: x_high, -1: x_low}.get(sx), {1: y_high, -1: y_low}.get(sy)) if f is not None]
        behind = [f for f in ({1: x_low, -1: x_high}.get(sx), {1: y_low, -1: y_high}.get(sy)) if f is not None]
        ahead = ahead[0] if len(ahead) == 1 else jnp.logical_and(*ahead)
        behind = behind[0] if len(behind) == 1 else jnp.logical_and(*behind)

        @pl.when(ahead)
        def _():
            copy.start()

        return copy, ahead, behind

    def wait(copies):
        for copy, ahead, behind in copies:

            @pl.when(behind)
            def _():
                copy.wait_recv()

            @pl.when(ahead)
            def _():
                copy.wait_send()

    fold(0)
    pl.semaphore_wait(barrier, len(partners))
    halo = []
    for h in range(2):
        half = obuf.at[13, :, :, 128 * h : 128 * h + 128]
        halo.append(
            [
                toward(shc.at[h], hc.at[h], hss.at[h, 2], hrs.at[h, 2], 1, 1),
                toward(shy.at[h], hy.at[h], hss.at[h, 1], hrs.at[h, 1], 0, 1),
                toward(half, hx.at[h], hss.at[h, 0], hrs.at[h, 0], 1, 0),
            ]
        )
    for c in range(1, 4):
        fold(c)

    sub = lax.broadcasted_iota(jnp.int32, (8, 7, 8, 128), 2)

    def apply(src, h):
        for ex in range(2):
            for ez in range(2):
                i0, l0 = 7 * ex, 6 * ez
                rows, layers = slice(i0, i0 + 8), slice(l0, l0 + 7)
                n0 = src[h, rows, layers, 0:8]
                n1 = src[h, rows, layers, 8:16]
                t0 = jnp.where(sub < 7, n0, n1).reshape(448, 128).astype(BF16)
                t1 = jnp.where(sub < 6, n1, n0).reshape(448, 128).astype(BF16)
                p0 = dot_nn(ap[4 * ex + ez], t0).reshape(8, 7, 8, 128)
                p1 = dot_nn(ap[4 * ex + 2 + ez], t1).reshape(8, 7, 8, 128)
                m0 = jnp.where(sub < 7, p0, 0.0) + jnp.where(sub < 6, 0.0, p1)
                m1 = jnp.where(sub < 6, p1, 0.0) + jnp.where(sub < 7, 0.0, p0)
                for part, tile in ((m0, slice(0, 8)), (m1, slice(8, 16))):
                    if ex:
                        first = part[:1, ez:] + acc[h, 7:8, l0 + ez : l0 + 7, tile]
                        rest = jnp.concatenate([first, part[1:, ez:]], axis=0)
                    else:
                        rest = part[:, ez:]
                    if ez:
                        joint = part[:, :1] + acc[h, rows, l0 : l0 + 1, tile]
                        rest = jnp.concatenate([joint, rest], axis=1)
                    acc[h, rows, layers, tile] = rest

    def exchange(t, h):
        copies = []

        def send(n, src, dst, sx, sy):
            copies.append(toward(src, dst, ess.at[t, h, n], ers.at[t, h, n], sx, sy))

        corners = [(0, 15, -1, -1), (14, 13, 1, 1), (0, 13, -1, 1), (14, 15, 1, -1)]
        count = 4 if t < 2 else 1
        for n, (i, slot, _, _) in enumerate(corners[:count]):
            scs[t, n, h] = acc2[h, line(i, slot, 1), :].astype(BF16)
        syl[t, h] = acc2[h, line(0, 15, 15), :].astype(BF16)
        if t < 2:
            syh[t, h] = acc2[h, line(0, 13, 15), :].astype(BF16)
        sxl[t, h] = acc[h, 0].astype(BF16)
        if t < 2:
            sxh[t, h] = acc[h, 14].astype(BF16)
        for n, (_, _, sx, sy) in enumerate(corners[:count]):
            send(4 + n, scs.at[t, n, h], rcs.at[t, n, h], sx, sy)
        send(0, syl.at[t, h], ryh.at[t, h], 0, -1)
        if t < 2:
            send(1, syh.at[t, h], ryl.at[t, h], 0, 1)
        send(2, sxl.at[t, h], rxh.at[t, h], -1, 0)
        if t < 2:
            send(3, sxh.at[t, h], rxl.at[t, h], 1, 0)
        return copies

    def gated(flag, value, coef):
        return jnp.where(flag, value.astype(F32), 0.0) * coef

    def faces(t, h, y, y2, coef):
        def bump(i, slot, count, value):
            y2[h, line(i, slot, count), :] += value

        y[h, 14] += gated(x_high, rxh[t, h], coef)
        bump(0, 13, 15, gated(y_high, ryh[t, h], coef))
        bump(14, 13, 1, gated(jnp.logical_and(x_high, y_high), rcs[t, 0, h], coef))
        if t < 2:
            y[h, 0] += rxl[t, h].astype(F32) * coef
            bump(0, 15, 15, ryl[t, h].astype(F32) * coef)
            bump(0, 15, 1, rcs[t, 1, h].astype(F32) * coef)
            bump(14, 15, 1, gated(x_high, rcs[t, 2, h], coef))
            bump(0, 13, 1, gated(y_high, rcs[t, 3, h], coef))
            y[h, 0] = jnp.where(x_low, y[h, 0], 0.0)
            edge = y2[h, line(0, 15, 15), :]
            y2[h, line(0, 15, 15), :] = jnp.where(y_low, edge, 0.0)

    stages = []
    for h in range(2):
        wait(halo[h])
        ya[h, 0, :, 0:14, :] = jnp.where(x_low, hx[h].astype(F32), 0.0)
        ya2[h, line(1, 15, 14), :] = jnp.where(y_low, hy[h].astype(F32), 0.0)
        ya2[h, line(0, 15, 1), :] = jnp.where(
            jnp.logical_and(x_low, y_low), hc[h].astype(F32), 0.0
        )
        apply(ya, h)
        stages.append(exchange(0, h))
    for h in range(2):
        yb2[h] = 0.25 * acc2[h] - 0.375 * ya2[h]
    for h in range(2):
        wait(stages[h])
        faces(0, h, yb, yb2, 0.25)
        apply(yb, h)
        stages[h] = exchange(1, h)
    for h in range(2):
        ya2[h] = 0.5 * acc2[h] - 0.75 * yb2[h] - ya2[h]
    for h in range(2):
        wait(stages[h])
        faces(1, h, ya, ya2, 0.5)
        apply(ya, h)
        stages[h] = exchange(2, h)
    for h in range(2):
        yb2[h] = 0.5 * acc2[h] - 0.75 * ya2[h] - yb2[h]

    def pair(h):
        high = both[:, 128 * h : 128 * h + 128]
        low = both[:, NB + 128 * h : NB + 128 * h + 128]
        return high, low, jnp.concatenate([high, low], axis=1)

    def diagonal(h):
        high, _, pairs = pair(h)
        total = dot_tn(high, pairs)
        cross = total[:, 128:]
        return total[:, 0:128] + (cross + cross.T)

    for h in range(2):
        wait(stages[h])
        faces(2, h, yb, yb2, 0.5)
        yb2[h, line(0, 15, 15), :] = jnp.zeros((195, 128), F32)
        y = yb2[h, 208:3120, :]
        top = y.astype(BF16)
        both[:, 128 * h : 128 * h + 128] = top
        both[:, NB + 128 * h : NB + 128 * h + 128] = (y - top.astype(F32)).astype(BF16)
        block = diagonal(h)
        if h == 0:
            grams = [block]
        else:
            total = dot_tn(both[:, 0:128], pair(1)[2])
            cross = dot_tn(both[:, NB : NB + 128], both[:, 128:NB])
            grams += [total[:, 0:128] + (total[:, 128:] + cross), block]
    keep = pltpu.make_async_copy(both, yout, ysem)
    keep.start()
    gl[...] = jnp.concatenate(grams, axis=0).reshape(16, 24, 128)

    copies = []
    for d in range(1, ndy):
        peer = lax.rem(dy + d, ndy)
        copies.append(remote(gl.at[peer], ra.at[dy], as_.at[d], ar_.at[d], (dx, peer)))
    for copy in copies:
        copy.wait()
    chunk = gl[dy]
    for d in range(1, ndy):
        chunk += ra[lax.rem(dy + d, ndy)]
    gb[dx] = chunk
    copies = []
    for d in range(1, ndx):
        peer = lax.rem(dx + d, ndx)
        copies.append(remote(gb.at[dx], gb.at[dx], bs_.at[d], br_.at[d], (peer, dy)))
    for copy in copies:
        copy.wait()
    chunk = gb[0]
    for p in range(1, ndx):
        chunk += gb[p]
    gf[dy] = chunk
    copies = []
    for d in range(1, ndy):
        peer = lax.rem(dy + d, ndy)
        copies.append(remote(gf.at[dy], gf.at[dy], cs_.at[d], cr_.at[d], (dx, peer)))
    for copy in copies:
        copy.wait()
    grams = gf[...].reshape(384, 128)
    gout[0:128, 0:128] = grams[0:128]
    gout[0:128, 128:NB] = grams[128:NB]
    gout[128:NB, 0:128] = jnp.zeros((128, 128), F32)
    gout[128:NB, 128:NB] = grams[NB:384]
    keep.wait()


def split3(x):
    a = x.astype(BF16)
    rest = x - a.astype(F32)
    b = rest.astype(BF16)
    return a, b, (rest - b.astype(F32)).astype(BF16)


def factor_inverse(g, work, ones):
    ones[...] = jnp.ones((8, 128), F32)
    one = ones[...]
    rows = lax.broadcasted_iota(jnp.int32, (8, 128), 0)
    lanes = lax.broadcasted_iota(jnp.int32, (8, 128), 1)
    scales = []
    for o in range(8):
        base = 32 * o
        source = g if o == 0 else work
        tiles = [
            [source[base + 8 * t : base + 8 * t + 8, 128 * h : 128 * h + 128] for h in range(2)]
            for t in range(4)
        ]
        factors = []
        half = base // 128
        for s in range(4):
            first = base + 8 * s - 128 * half
            inside = jnp.logical_and(lanes >= first, lanes < first + 8)
            columns = []
            for q in range(s, 4):
                tile = tiles[q][half]
                columns.append(
                    [
                        jnp.broadcast_to(tile[:, first + j : first + j + 1], (8, 128)) * one
                        for j in range(8)
                    ]
                )
                fresh = jnp.where(lanes == rows + first, 1.0, 0.0) if q == s else 0.0
                tiles[q][half] = jnp.where(inside, fresh, tile)
            scale = jnp.ones((8, 128), F32)
            factor = jnp.ones((8, 128), F32)
            for k in range(8):
                lead = [jnp.broadcast_to(columns[0][j][k : k + 1, :], (8, 128)) for j in range(k, 8)]
                inv = 1.0 / lead[0]
                scale = jnp.where(rows == k, lead[0], scale)
                factor = jnp.where(rows == k, inv, factor)
                pivot = [jnp.broadcast_to(tiles[s][h][k : k + 1, :], (8, 128)) * inv for h in range(2)]
                ready = [v * inv for v in lead]
                for q in range(s, 4):
                    if q == s and k == 7:
                        continue
                    column = columns[q - s][k]
                    if q == s:
                        column = jnp.where(rows > k, column, 0.0)
                    for j in range(k + 1, 8):
                        if q == s:
                            change = (column * lead[j - k]) * inv
                        else:
                            change = column * ready[j - k]
                        columns[q - s][j] = columns[q - s][j] - change
                    for h in range(2):
                        tiles[q][h] = tiles[q][h] - column * pivot[h]
            scales.append(lax.rsqrt(scale))
            factors.append(factor)
        for t in range(4):
            for h in range(2):
                work[base + 8 * t : base + 8 * t + 8, 128 * h : 128 * h + 128] = tiles[t][h]
        if o < 7:
            u = jnp.concatenate([jnp.concatenate(tiles[t], axis=1) for t in range(4)], axis=0)
            f = jnp.concatenate([jnp.concatenate([v, v], axis=1) for v in factors], axis=0)
            r = lax.broadcasted_iota(jnp.int32, (32, NB), 0) + base
            c = lax.broadcasted_iota(jnp.int32, (32, NB), 1)
            v = jnp.where(jnp.logical_and(c > r, c < base + 32), 0.0, u * f)
            start = 128 * ((base + 32) // 128)
            u1, u2, u3 = split3(u[:, start:])
            v1, v2, v3 = split3(v)
            left = jnp.concatenate([u1, u1, u1, u2, u2, u3], axis=0)
            right = jnp.concatenate([v1, v2, v3, v1, v2, v1], axis=0)
            change = lax.dot_general(
                left, right, (((0,), (0,)), ((), ())), preferred_element_type=F32
            )
            rest = slice(base + 32, NB)
            old = (g if o == 0 else work)[rest, :]
            cc = lax.broadcasted_iota(jnp.int32, old.shape, 1)
            old = jnp.where(jnp.logical_and(cc >= base, cc < base + 32), 0.0, old)
            work[rest, :] = old - change[base + 32 - start :, :]
    for t in range(32):
        for h in range(2):
            tile = work[8 * t : 8 * t + 8, 128 * h : 128 * h + 128] * scales[t]
            work[8 * t : 8 * t + 8, 128 * h : 128 * h + 128] = jnp.where(
                lanes + 128 * h <= rows + 8 * t, tile, 0.0
            )


def basis_kernel(scale, y, g, out, ybuf, stage, work, ones, weights, yin, osem):
    load = pltpu.make_async_copy(y, ybuf, yin)
    load.start()
    factor_inverse(g, work, ones)
    w = work[...].T * scale
    top = w.astype(BF16)
    weights[0:NB] = top
    weights[NB : 2 * NB] = top
    weights[2 * NB :] = (w - top.astype(F32)).astype(BF16)
    load.wait()
    copies = []
    for start, count in ((0, 4), (4, 4), (8, 4), (12, 2)):
        rows = slice(208 * start, 208 * (start + count))
        left = jnp.concatenate([ybuf[rows, :], ybuf[rows, 0:NB]], axis=1)
        q = dot_nn(left, weights[...]).reshape(count, 13, 16, NB)
        planes = slice(start, start + count)
        stage[planes] = q[:, :, 0:14, :]
        copy = pltpu.make_async_copy(stage.at[planes], out.at[planes], osem.at[start])
        copy.start()
        copies.append(copy)
    for copy in copies:
        copy.wait()


def solution(mesh):
    ndx, ndy = mesh.shape["dx"], mesh.shape["dy"]
    vmem = pl.BlockSpec(memory_space=pltpu.VMEM)
    anywhere = pl.BlockSpec(memory_space=pl.ANY)
    scale = math.sqrt(14 * 14 * 13 * ndx * ndy)

    def shards(orbitals, elem_mats, conn):
        dma = pltpu.SemaphoreType.DMA
        y, g = pl.pallas_call(
            lambda *refs: filter_kernel(ndx, ndy, *refs),
            out_shape=(
                jax.ShapeDtypeStruct((2912, 2 * NB), BF16),
                jax.ShapeDtypeStruct((NB, NB), F32),
            ),
            in_specs=[anywhere, anywhere, vmem],
            out_specs=(anywhere, vmem),
            scratch_shapes=[
                pltpu.VMEM((14, 13, 14, NB), BF16),
                pltpu.VMEM((8, 512, 512), BF16),
                pltpu.VMEM((8, 448, 448), BF16),
                pltpu.VMEM((2, 448, 128), jnp.int32),
                pltpu.VMEM((448, 512), BF16),
                pltpu.VMEM((512, 448), BF16),
                pltpu.VMEM((2, 3120, 128), F32),
                pltpu.VMEM((2, 3120, 128), F32),
                pltpu.VMEM((2, 3120, 128), F32),
                pltpu.VMEM((2912, 2 * NB), BF16),
                pltpu.VMEM((2, 13, 14, 128), BF16),
                pltpu.VMEM((2, 182, 128), BF16),
                pltpu.VMEM((2, 13, 128), BF16),
                pltpu.VMEM((2, 182, 128), BF16),
                pltpu.VMEM((2, 13, 128), BF16),
                pltpu.VMEM((3, 2, 13, 16, 128), BF16),
                pltpu.VMEM((2, 2, 13, 16, 128), BF16),
                pltpu.VMEM((3, 2, 195, 128), BF16),
                pltpu.VMEM((2, 2, 195, 128), BF16),
                pltpu.VMEM((3, 4, 2, 13, 128), BF16),
                pltpu.VMEM((2, 2, 13, 16, 128), BF16),
                pltpu.VMEM((3, 2, 13, 16, 128), BF16),
                pltpu.VMEM((2, 2, 195, 128), BF16),
                pltpu.VMEM((3, 2, 195, 128), BF16),
                pltpu.VMEM((3, 4, 2, 13, 128), BF16),
                pltpu.VMEM((16, 24, 128), F32),
                pltpu.VMEM((16, 24, 128), F32),
                pltpu.VMEM((8, 24, 128), F32),
                pltpu.VMEM((16, 24, 128), F32),
                dma,
                dma((8,)),
                dma,
                dma((2, 3)),
                dma((2, 3)),
                dma((3, 2, 8)),
                dma((3, 2, 8)),
                dma((16,)),
                dma((16,)),
                dma((8,)),
                dma((8,)),
                dma((16,)),
                dma((16,)),
            ],
            compiler_params=pltpu.CompilerParams(collective_id=0, has_side_effects=True),
            name="filter",
        )(jnp.swapaxes(orbitals, 1, 2), elem_mats, conn)
        filtered = pl.pallas_call(
            lambda *refs: basis_kernel(scale, *refs),
            out_shape=jax.ShapeDtypeStruct((14, 13, 14, NB), F32),
            in_specs=[anywhere, vmem],
            out_specs=anywhere,
            scratch_shapes=[
                pltpu.VMEM((2912, 2 * NB), BF16),
                pltpu.VMEM((14, 13, 14, NB), F32),
                pltpu.VMEM((NB, NB), F32),
                pltpu.VMEM((8, 128), F32),
                pltpu.VMEM((3 * NB, NB), BF16),
                dma,
                dma((14,)),
            ],
            name="basis",
        )(y, g)
        return jnp.swapaxes(filtered, 1, 2)

    in_specs = (
        P("dx", "dy", None, None),
        P("dx", "dy", None, None, None),
        P("dx", "dy", None, None),
    )
    out_specs = P("dx", "dy", None, None)
    return jax.shard_map(shards, mesh=mesh, in_specs=in_specs, out_specs=out_specs, check_vma=False)
```

```python
import math

import jax
import jax.numpy as jnp
from jax import lax
from jax.experimental import pallas as pl
from jax.experimental.pallas import tpu as pltpu
from jax.sharding import PartitionSpec as P

MESH = pl.DeviceIdType.MESH
F32 = jnp.float32
BF16 = jnp.bfloat16
NB = 256


def dot_nn(a, b, precision=None):
    return lax.dot_general(
        a, b, (((1,), (0,)), ((), ())), precision=precision, preferred_element_type=F32
    )


def dot_nt(a, b, precision=None):
    return lax.dot_general(
        a, b, (((1,), (1,)), ((), ())), precision=precision, preferred_element_type=F32
    )


def dot_tn(a, b, precision=None):
    return lax.dot_general(
        a, b, (((0,), (0,)), ((), ())), precision=precision, preferred_element_type=F32
    )


def filter_kernel(
    ndx, ndy,
    orb, mats, links_in,
    yout, gout,
    obuf, conn, abuf, ap, rmap, st, tt, ya2, yb2, acc2, both, rim, edge, gram,
    hx, hy, hc, shy, shc, sxl, sxh, syl, syh, scs, rxl, rxh, ryl, ryh, rcs,
    gl, ra, gb, gf,
    osem, csem, msem, ysem, hss, hrs, ess, ers, as_, ar_, bs_, br_, cs_, cr_,
):
    dx = lax.axis_index("dx")
    dy = lax.axis_index("dy")
    xp, xm = lax.rem(dx + 1, ndx), lax.rem(dx + ndx - 1, ndx)
    yp, ym = lax.rem(dy + 1, ndy), lax.rem(dy + ndy - 1, ndy)
    ya, yb, acc = (ref.reshape(2, 15, 13, 16, 128) for ref in (ya2, yb2, acc2))

    barrier = pltpu.get_barrier_semaphore()
    partners = [(lax.rem(dx + d, ndx), dy) for d in range(1, ndx)]
    partners += [(dx, lax.rem(dy + d, ndy)) for d in range(1, ndy)]
    partners += [(xp, yp), (xp, ym), (xm, yp), (xm, ym)]
    for partner in partners:
        pl.semaphore_signal(barrier, inc=1, device_id=partner, device_id_type=MESH)

    first_load = pltpu.make_async_copy(orb, obuf, osem)
    first_load.start()
    link_load = pltpu.make_async_copy(links_in, conn, csem)
    link_load.start()
    loads = []
    for e in range(8):
        copy = pltpu.make_async_copy(mats.at[e // 4, e // 2 % 2, e % 2], abuf.at[e], msem.at[e])
        copy.start()
        loads.append(copy)

    grid = (8, 7, 8, 128)
    a_of, l_of, s_of = (lax.broadcasted_iota(jnp.int32, grid, d) for d in range(3))
    for ey in range(2):
        b_of = jnp.where(s_of < 7 - ey, s_of + 1 + ey, s_of - 7 + ey)
        rmap[ey] = (a_of * 225 + b_of * 15 + l_of).reshape(448, 128)

    def line(i, slot, count):
        return pl.ds(i * 208 + slot, 13 * count, stride=16)

    for h in range(2):
        ya2[h, 0:208, :] = jnp.zeros((208, 128), F32)
        ya2[h, line(1, 14, 14), :] = jnp.zeros((182, 128), F32)
        ya2[h, line(1, 15, 14), :] = jnp.zeros((182, 128), F32)
    first_load.wait()

    def fill(i, carry):
        plane = obuf[i].astype(F32)
        for h in range(2):
            ya[h, i + 1, :, 0:14, :] = plane[:, :, 128 * h : 128 * h + 128]
        return carry

    lax.fori_loop(0, 14, fill, 0)

    for h in range(2):
        shy[h] = ya2[h, line(1, 13, 14), :].astype(BF16)
        shc[h] = ya2[h, line(14, 13, 1), :].astype(BF16)

    def fold(c):
        ex, ey = c // 2, c % 2
        links = conn[ex, ey]
        for ez in range(2):
            e = c * 2 + ez
            loads[e].wait()
            row = links[ez : ez + 1] - ((7 * ex * 15 + 7 * ey) * 15 + 7 * ez + 1 - ez)
            for q in range(4):
                part = row[:, 128 * q : 128 * q + 128]
                st[:, 128 * q : 128 * q + 128] = jnp.where(rmap[ey] == part, 1.0, 0.0).astype(BF16)
            tt[...] = dot_nt(abuf[e], st[...]).astype(BF16)
            ap[e] = dot_nn(st[...], tt[...]).astype(BF16)

    def remote(src, dst, ssem, rsem, where):
        copy = pltpu.make_async_remote_copy(
            src_ref=src, dst_ref=dst, send_sem=ssem, recv_sem=rsem, device_id=where, device_id_type=MESH
        )
        copy.start()
        return copy

    x_low, x_high, y_low, y_high = dx > 0, dx < ndx - 1, dy > 0, dy < ndy - 1

    def toward(src, dst, ssem, rsem, sx, sy):
        where = (dx + sx, dy + sy)
        copy = pltpu.make_async_remote_copy(
            src_ref=src, dst_ref=dst, send_sem=ssem, recv_sem=rsem, device_id=where, device_id_type=MESH
        )
        ahead = [f for f in ({1: x_high, -1: x_low}.get(sx), {1: y_high, -1: y_low}.get(sy)) if f is not None]
        behind = [f for f in ({1: x_low, -1: x_high}.get(sx), {1: y_low, -1: y_high}.get(sy)) if f is not None]
        ahead = ahead[0] if len(ahead) == 1 else jnp.logical_and(*ahead)
        behind = behind[0] if len(behind) == 1 else jnp.logical_and(*behind)

        @pl.when(ahead)
        def _():
            copy.start()

        return copy, (sx, sy), ahead, behind

    sent = {}

    def wait(copies):
        for copy, side, ahead, behind in copies:

            @pl.when(behind)
            def _():
                copy.wait_recv()

            sent.setdefault(side, (ahead, []))[1].append(copy)

    def drain():
        for ahead, copies in sent.values():

            @pl.when(ahead)
            def _():
                for copy in copies:
                    copy.wait_send()

    link_load.wait()
    fold(0)
    pl.semaphore_wait(barrier, len(partners))
    halo = []
    for h in range(2):
        half = obuf.at[13, :, :, 128 * h : 128 * h + 128]
        halo.append(
            [
                toward(shc.at[h], hc.at[h], hss.at[h, 2], hrs.at[h, 2], 1, 1),
                toward(shy.at[h], hy.at[h], hss.at[h, 1], hrs.at[h, 1], 0, 1),
                toward(half, hx.at[h], hss.at[h, 0], hrs.at[h, 0], 1, 0),
            ]
        )
    for c in range(1, 4):
        fold(c)

    sub = lax.broadcasted_iota(jnp.int32, (8, 7, 8, 128), 2)

    def apply(src, h):
        for ex in range(2):
            for ez in range(2):
                i0, l0 = 7 * ex, 6 * ez
                rows, layers = slice(i0, i0 + 8), slice(l0, l0 + 7)
                n0 = src[h, rows, layers, 0:8]
                n1 = src[h, rows, layers, 8:16]
                t0 = jnp.where(sub < 7, n0, n1).reshape(448, 128).astype(BF16)
                t1 = jnp.where(sub < 6, n1, n0).reshape(448, 128).astype(BF16)
                p0 = dot_nn(ap[4 * ex + ez], t0).reshape(8, 7, 8, 128)
                p1 = dot_nn(ap[4 * ex + 2 + ez], t1).reshape(8, 7, 8, 128)
                m0 = jnp.where(sub < 7, p0, 0.0) + jnp.where(sub < 6, 0.0, p1)
                m1 = jnp.where(sub < 6, p1, 0.0) + jnp.where(sub < 7, 0.0, p0)
                for part, tile in ((m0, slice(0, 8)), (m1, slice(8, 16))):
                    if ex:
                        first = part[:1, ez:] + acc[h, 7:8, l0 + ez : l0 + 7, tile]
                        rest = jnp.concatenate([first, part[1:, ez:]], axis=0)
                    else:
                        rest = part[:, ez:]
                    if ez:
                        joint = part[:, :1] + acc[h, rows, l0 : l0 + 1, tile]
                        rest = jnp.concatenate([joint, rest], axis=1)
                    acc[h, rows, layers, tile] = rest

    def exchange(t, h):
        copies = []

        def send(n, src, dst, sx, sy):
            copies.append(toward(src, dst, ess.at[t, h, n], ers.at[t, h, n], sx, sy))

        corners = [(0, 15, -1, -1), (14, 13, 1, 1), (0, 13, -1, 1), (14, 15, 1, -1)]
        count = 4 if t < 2 else 1
        for n, (i, slot, _, _) in enumerate(corners[:count]):
            scs[t, n, h] = acc2[h, line(i, slot, 1), :].astype(BF16)
        syl[t, h] = acc2[h, line(0, 15, 15), :].astype(BF16)
        if t < 2:
            syh[t, h] = acc2[h, line(0, 13, 15), :].astype(BF16)
        sxl[t, h] = acc[h, 0].astype(BF16)
        if t < 2:
            sxh[t, h] = acc[h, 14].astype(BF16)
        for n, (_, _, sx, sy) in enumerate(corners[:count]):
            send(4 + n, scs.at[t, n, h], rcs.at[t, n, h], sx, sy)
        send(0, syl.at[t, h], ryh.at[t, h], 0, -1)
        if t < 2:
            send(1, syh.at[t, h], ryl.at[t, h], 0, 1)
        send(2, sxl.at[t, h], rxh.at[t, h], -1, 0)
        if t < 2:
            send(3, sxh.at[t, h], rxl.at[t, h], 1, 0)
        return copies

    def gated(flag, value, coef):
        return jnp.where(flag, value.astype(F32), 0.0) * coef

    def faces(t, h, y, y2, coef):
        def bump(i, slot, count, value):
            y2[h, line(i, slot, count), :] += value

        y[h, 14] += gated(x_high, rxh[t, h], coef)
        bump(0, 13, 15, gated(y_high, ryh[t, h], coef))
        bump(14, 13, 1, gated(jnp.logical_and(x_high, y_high), rcs[t, 0, h], coef))
        if t < 2:
            y[h, 0] += rxl[t, h].astype(F32) * coef
            bump(0, 15, 15, ryl[t, h].astype(F32) * coef)
            bump(0, 15, 1, rcs[t, 1, h].astype(F32) * coef)
            bump(14, 15, 1, gated(x_high, rcs[t, 2, h], coef))
            bump(0, 13, 1, gated(y_high, rcs[t, 3, h], coef))
            y[h, 0] = jnp.where(x_low, y[h, 0], 0.0)
            kept = jnp.where(y_low, y2[h, line(0, 15, 15), :], 0.0)
            y2[h, line(0, 15, 15), :] = kept

    stages = []
    for h in range(2):
        wait(halo[h])
        ya[h, 0, :, 0:14, :] = jnp.where(x_low, hx[h].astype(F32), 0.0)
        ya2[h, line(1, 15, 14), :] = jnp.where(y_low, hy[h].astype(F32), 0.0)
        ya2[h, line(0, 15, 1), :] = jnp.where(
            jnp.logical_and(x_low, y_low), hc[h].astype(F32), 0.0
        )
        apply(ya, h)
        stages.append(exchange(0, h))
    for h in range(2):
        yb2[h] = 0.25 * acc2[h] - 0.375 * ya2[h]
    for h in range(2):
        wait(stages[h])
        faces(0, h, yb, yb2, 0.25)
        apply(yb, h)
        stages[h] = exchange(1, h)
    for h in range(2):
        ya2[h] = 0.5 * acc2[h] - 0.75 * yb2[h] - ya2[h]
    for h in range(2):
        wait(stages[h])
        faces(1, h, ya, ya2, 0.5)
        apply(ya, h)
        stages[h] = exchange(2, h)
    for h in range(2):
        yb2[h] = 0.5 * acc2[h] - 0.75 * ya2[h] - yb2[h]

    def parts(y):
        top = y.astype(BF16)
        return top, (y - top.astype(F32)).astype(BF16)

    def gram_of(ref):
        total = dot_tn(ref[:, 0:NB], ref[...])
        cross = total[:, NB:]
        return total[:, 0:NB] + (cross + cross.T)

    slot = lax.broadcasted_iota(jnp.int32, (169, 16, 128), 1)
    for h in range(2):
        inner = jnp.where(slot < 13, yb[h, 1:14].reshape(169, 16, 128), 0.0).reshape(2704, 128)
        top, low = parts(inner)
        both[0:2704, 128 * h : 128 * h + 128] = top
        both[0:2704, NB + 128 * h : NB + 128 * h + 128] = low
        rim[h, 368:384, :] = jnp.zeros((16, 128), F32)
    gram[...] = gram_of(both.at[0:2704])
    for h in range(2):
        wait(stages[h])
        faces(2, h, yb, yb2, 0.5)
        yb2[h, line(0, 15, 15), :] = jnp.zeros((195, 128), F32)
        rim[h, 0:208, :] = yb2[h, 2912:3120, :]
        rim[h, 208:377, :] = yb2[h, line(1, 13, 13), :]
        top, low = parts(rim[h])
        edge[:, 128 * h : 128 * h + 128] = top
        edge[:, NB + 128 * h : NB + 128 * h + 128] = low
    full = gram[...] + gram_of(edge)
    blocks = [full[0:128, 0:128], full[0:128, 128:NB], full[128:NB, 128:NB]]
    gl[...] = jnp.concatenate(blocks, axis=0).reshape(16, 24, 128)

    copies = []
    for d in range(1, ndy):
        peer = lax.rem(dy + d, ndy)
        copies.append(remote(gl.at[peer], ra.at[dy], as_.at[d], ar_.at[d], (dx, peer)))
    for h in range(2):
        top, low = parts(yb2[h, 208:3120, :])
        both[:, 128 * h : 128 * h + 128] = top
        both[:, NB + 128 * h : NB + 128 * h + 128] = low
    keep = pltpu.make_async_copy(both, yout, ysem)
    keep.start()
    drain()
    for copy in copies:
        copy.wait()
    chunk = gl[dy]
    for d in range(1, ndy):
        chunk += ra[lax.rem(dy + d, ndy)]
    gb[dx] = chunk
    copies = []
    for d in range(1, ndx):
        peer = lax.rem(dx + d, ndx)
        copies.append(remote(gb.at[dx], gb.at[dx], bs_.at[d], br_.at[d], (peer, dy)))
    for copy in copies:
        copy.wait()
    chunk = gb[0]
    for p in range(1, ndx):
        chunk += gb[p]
    gf[dy] = chunk
    copies = []
    for d in range(1, ndy):
        peer = lax.rem(dy + d, ndy)
        copies.append(remote(gf.at[dy], gf.at[dy], cs_.at[d], cr_.at[d], (dx, peer)))
    for copy in copies:
        copy.wait()
    grams = gf[...].reshape(384, 128)
    gout[0:128, 0:128] = grams[0:128]
    gout[0:128, 128:NB] = grams[128:NB]
    gout[128:NB, 0:128] = jnp.zeros((128, 128), F32)
    gout[128:NB, 128:NB] = grams[NB:384]
    keep.wait()


def split3(x):
    a = x.astype(BF16)
    rest = x - a.astype(F32)
    b = rest.astype(BF16)
    return a, b, (rest - b.astype(F32)).astype(BF16)


def factor_inverse(g, work, ones):
    ones[...] = jnp.ones((8, 128), F32)
    one = ones[...]
    rows = lax.broadcasted_iota(jnp.int32, (8, 128), 0)
    lanes = lax.broadcasted_iota(jnp.int32, (8, 128), 1)
    scales = []
    for o in range(8):
        base = 32 * o
        source = g if o == 0 else work
        tiles = [
            [source[base + 8 * t : base + 8 * t + 8, 128 * h : 128 * h + 128] for h in range(2)]
            for t in range(4)
        ]
        factors = []
        half = base // 128
        for s in range(4):
            first = base + 8 * s - 128 * half
            inside = jnp.logical_and(lanes >= first, lanes < first + 8)
            columns = []
            for q in range(s, 4):
                tile = tiles[q][half]
                columns.append(
                    [
                        jnp.broadcast_to(tile[:, first + j : first + j + 1], (8, 128)) * one
                        for j in range(8)
                    ]
                )
                fresh = jnp.where(lanes == rows + first, 1.0, 0.0) if q == s else 0.0
                tiles[q][half] = jnp.where(inside, fresh, tile)
            scale = jnp.ones((8, 128), F32)
            factor = jnp.ones((8, 128), F32)
            for k in range(8):
                lead = [jnp.broadcast_to(columns[0][j][k : k + 1, :], (8, 128)) for j in range(k, 8)]
                inv = 1.0 / lead[0]
                scale = jnp.where(rows == k, lead[0], scale)
                factor = jnp.where(rows == k, inv, factor)
                pivot = [jnp.broadcast_to(tiles[s][h][k : k + 1, :], (8, 128)) * inv for h in range(2)]
                ready = [v * inv for v in lead]
                for q in range(s, 4):
                    if q == s and k == 7:
                        continue
                    column = columns[q - s][k]
                    if q == s:
                        column = jnp.where(rows > k, column, 0.0)
                    for j in range(k + 1, 8):
                        if q == s:
                            change = (column * lead[j - k]) * inv
                        else:
                            change = column * ready[j - k]
                        columns[q - s][j] = columns[q - s][j] - change
                    for h in range(2):
                        tiles[q][h] = tiles[q][h] - column * pivot[h]
            scales.append(lax.rsqrt(scale))
            factors.append(factor)
        for t in range(4):
            for h in range(2):
                work[base + 8 * t : base + 8 * t + 8, 128 * h : 128 * h + 128] = tiles[t][h]
        if o < 7:
            u = jnp.concatenate([jnp.concatenate(tiles[t], axis=1) for t in range(4)], axis=0)
            f = jnp.concatenate([jnp.concatenate([v, v], axis=1) for v in factors], axis=0)
            r = lax.broadcasted_iota(jnp.int32, (32, NB), 0) + base
            c = lax.broadcasted_iota(jnp.int32, (32, NB), 1)
            v = jnp.where(jnp.logical_and(c > r, c < base + 32), 0.0, u * f)
            start = 128 * ((base + 32) // 128)
            u1, u2, u3 = split3(u[:, start:])
            v1, v2, v3 = split3(v)
            left = jnp.concatenate([u1, u1, u1, u2, u2, u3], axis=0)
            right = jnp.concatenate([v1, v2, v3, v1, v2, v1], axis=0)
            change = lax.dot_general(
                left, right, (((0,), (0,)), ((), ())), preferred_element_type=F32
            )
            rest = slice(base + 32, NB)
            old = (g if o == 0 else work)[rest, :]
            cc = lax.broadcasted_iota(jnp.int32, old.shape, 1)
            old = jnp.where(jnp.logical_and(cc >= base, cc < base + 32), 0.0, old)
            work[rest, :] = old - change[base + 32 - start :, :]
    for t in range(32):
        for h in range(2):
            tile = work[8 * t : 8 * t + 8, 128 * h : 128 * h + 128] * scales[t]
            work[8 * t : 8 * t + 8, 128 * h : 128 * h + 128] = jnp.where(
                lanes + 128 * h <= rows + 8 * t, tile, 0.0
            )


def basis_kernel(scale, y, g, out, ybuf, stage, work, ones, weights, yin, osem):
    load = pltpu.make_async_copy(y, ybuf, yin)
    load.start()
    factor_inverse(g, work, ones)
    w = work[...].T * scale
    top = w.astype(BF16)
    weights[0:NB] = top
    weights[NB : 2 * NB] = top
    weights[2 * NB :] = (w - top.astype(F32)).astype(BF16)
    load.wait()
    copies = []
    for start, count in ((0, 4), (4, 4), (8, 4), (12, 2)):
        rows = slice(208 * start, 208 * (start + count))
        left = jnp.concatenate([ybuf[rows, :], ybuf[rows, 0:NB]], axis=1)
        q = dot_nn(left, weights[...]).reshape(count, 13, 16, NB)
        planes = slice(start, start + count)
        stage[planes] = q[:, :, 0:14, :]
        copy = pltpu.make_async_copy(stage.at[planes], out.at[planes], osem.at[start])
        copy.start()
        copies.append(copy)
    for copy in copies:
        copy.wait()


def solution(mesh):
    ndx, ndy = mesh.shape["dx"], mesh.shape["dy"]
    vmem = pl.BlockSpec(memory_space=pltpu.VMEM)
    anywhere = pl.BlockSpec(memory_space=pl.ANY)
    scale = math.sqrt(14 * 14 * 13 * ndx * ndy)

    def shards(orbitals, elem_mats, conn):
        dma = pltpu.SemaphoreType.DMA
        y, g = pl.pallas_call(
            lambda *refs: filter_kernel(ndx, ndy, *refs),
            out_shape=(
                jax.ShapeDtypeStruct((2912, 2 * NB), BF16),
                jax.ShapeDtypeStruct((NB, NB), F32),
            ),
            in_specs=[anywhere, anywhere, anywhere],
            out_specs=(anywhere, vmem),
            scratch_shapes=[
                pltpu.VMEM((14, 13, 14, NB), BF16),
                pltpu.VMEM((2, 2, 2, 512), jnp.int32),
                pltpu.VMEM((8, 512, 512), BF16),
                pltpu.VMEM((8, 448, 448), BF16),
                pltpu.VMEM((2, 448, 128), jnp.int32),
                pltpu.VMEM((448, 512), BF16),
                pltpu.VMEM((512, 448), BF16),
                pltpu.VMEM((2, 3120, 128), F32),
                pltpu.VMEM((2, 3120, 128), F32),
                pltpu.VMEM((2, 3120, 128), F32),
                pltpu.VMEM((2912, 2 * NB), BF16),
                pltpu.VMEM((2, 384, 128), F32),
                pltpu.VMEM((384, 2 * NB), BF16),
                pltpu.VMEM((NB, NB), F32),
                pltpu.VMEM((2, 13, 14, 128), BF16),
                pltpu.VMEM((2, 182, 128), BF16),
                pltpu.VMEM((2, 13, 128), BF16),
                pltpu.VMEM((2, 182, 128), BF16),
                pltpu.VMEM((2, 13, 128), BF16),
                pltpu.VMEM((3, 2, 13, 16, 128), BF16),
                pltpu.VMEM((2, 2, 13, 16, 128), BF16),
                pltpu.VMEM((3, 2, 195, 128), BF16),
                pltpu.VMEM((2, 2, 195, 128), BF16),
                pltpu.VMEM((3, 4, 2, 13, 128), BF16),
                pltpu.VMEM((2, 2, 13, 16, 128), BF16),
                pltpu.VMEM((3, 2, 13, 16, 128), BF16),
                pltpu.VMEM((2, 2, 195, 128), BF16),
                pltpu.VMEM((3, 2, 195, 128), BF16),
                pltpu.VMEM((3, 4, 2, 13, 128), BF16),
                pltpu.VMEM((16, 24, 128), F32),
                pltpu.VMEM((16, 24, 128), F32),
                pltpu.VMEM((8, 24, 128), F32),
                pltpu.VMEM((16, 24, 128), F32),
                dma,
                dma,
                dma((8,)),
                dma,
                dma((2, 3)),
                dma((2, 3)),
                dma((3, 2, 8)),
                dma((3, 2, 8)),
                dma((16,)),
                dma((16,)),
                dma((8,)),
                dma((8,)),
                dma((16,)),
                dma((16,)),
            ],
            compiler_params=pltpu.CompilerParams(collective_id=0, has_side_effects=True),
            name="filter",
        )(jnp.swapaxes(orbitals, 1, 2), elem_mats, conn)
        filtered = pl.pallas_call(
            lambda *refs: basis_kernel(scale, *refs),
            out_shape=jax.ShapeDtypeStruct((14, 13, 14, NB), F32),
            in_specs=[anywhere, vmem],
            out_specs=anywhere,
            scratch_shapes=[
                pltpu.VMEM((2912, 2 * NB), BF16),
                pltpu.VMEM((14, 13, 14, NB), F32),
                pltpu.VMEM((NB, NB), F32),
                pltpu.VMEM((8, 128), F32),
                pltpu.VMEM((3 * NB, NB), BF16),
                dma,
                dma((14,)),
            ],
            name="basis",
        )(y, g)
        return jnp.swapaxes(filtered, 1, 2)

    in_specs = (
        P("dx", "dy", None, None),
        P("dx", "dy", None, None, None),
        P("dx", "dy", None, None),
    )
    out_specs = P("dx", "dy", None, None)
    return jax.shard_map(shards, mesh=mesh, in_specs=in_specs, out_specs=out_specs, check_vma=False)
```

```python
import math

import jax
import jax.numpy as jnp
from jax import lax
from jax.experimental import pallas as pl
from jax.experimental.pallas import tpu as pltpu
from jax.sharding import PartitionSpec as P

MESH = pl.DeviceIdType.MESH
F32 = jnp.float32
BF16 = jnp.bfloat16
NB = 256


def dot_nn(a, b, precision=None):
    return lax.dot_general(
        a, b, (((1,), (0,)), ((), ())), precision=precision, preferred_element_type=F32
    )


def dot_nt(a, b, precision=None):
    return lax.dot_general(
        a, b, (((1,), (1,)), ((), ())), precision=precision, preferred_element_type=F32
    )


def dot_tn(a, b, precision=None):
    return lax.dot_general(
        a, b, (((0,), (0,)), ((), ())), precision=precision, preferred_element_type=F32
    )


def filter_kernel(
    ndx, ndy,
    orb, mats, links_in,
    yout, gout,
    obuf, conn, abuf, ap, rmap, st, tt, ya2, yb2, acc2, both, rim, edge, gram,
    hx, hy, hc, shy, shc, sxl, sxh, syl, syh, scs, rxl, rxh, ryl, ryh, rcs,
    gl, ra, gb, gf,
    osem, csem, msem, ysem, hss, hrs, ess, ers, as_, ar_, bs_, br_, cs_, cr_,
):
    dx = lax.axis_index("dx")
    dy = lax.axis_index("dy")
    xp, xm = lax.rem(dx + 1, ndx), lax.rem(dx + ndx - 1, ndx)
    yp, ym = lax.rem(dy + 1, ndy), lax.rem(dy + ndy - 1, ndy)
    ya, yb, acc = (ref.reshape(2, 15, 13, 16, 128) for ref in (ya2, yb2, acc2))

    barrier = pltpu.get_barrier_semaphore()
    partners = [(lax.rem(dx + d, ndx), dy) for d in range(1, ndx)]
    partners += [(dx, lax.rem(dy + d, ndy)) for d in range(1, ndy)]
    partners += [(xp, yp), (xp, ym), (xm, yp), (xm, ym)]
    for partner in partners:
        pl.semaphore_signal(barrier, inc=1, device_id=partner, device_id_type=MESH)

    first_load = pltpu.make_async_copy(orb, obuf, osem)
    first_load.start()
    link_load = pltpu.make_async_copy(links_in, conn, csem)
    link_load.start()
    loads = []
    for e in range(8):
        copy = pltpu.make_async_copy(mats.at[e // 4, e // 2 % 2, e % 2], abuf.at[e], msem.at[e])
        copy.start()
        loads.append(copy)

    grid = (8, 7, 8, 128)
    a_of, l_of, s_of = (lax.broadcasted_iota(jnp.int32, grid, d) for d in range(3))
    for ey in range(2):
        b_of = jnp.where(s_of < 7 - ey, s_of + 1 + ey, s_of - 7 + ey)
        rmap[ey] = (a_of * 225 + b_of * 15 + l_of).reshape(448, 128)

    def line(i, slot, count):
        return pl.ds(i * 208 + slot, 13 * count, stride=16)

    for h in range(2):
        ya2[h, 0:208, :] = jnp.zeros((208, 128), F32)
        ya2[h, line(1, 14, 14), :] = jnp.zeros((182, 128), F32)
        ya2[h, line(1, 15, 14), :] = jnp.zeros((182, 128), F32)
    first_load.wait()

    def fill(i, carry):
        plane = obuf[i].astype(F32)
        for h in range(2):
            ya[h, i + 1, :, 0:14, :] = plane[:, :, 128 * h : 128 * h + 128]
        return carry

    lax.fori_loop(0, 14, fill, 0)

    for h in range(2):
        shy[h] = ya2[h, line(1, 13, 14), :].astype(BF16)
        shc[h] = ya2[h, line(14, 13, 1), :].astype(BF16)

    def fold(c):
        ex, ey = c // 2, c % 2
        links = conn[ex, ey]
        for ez in range(2):
            e = c * 2 + ez
            loads[e].wait()
            row = links[ez : ez + 1] - ((7 * ex * 15 + 7 * ey) * 15 + 7 * ez + 1 - ez)
            for q in range(4):
                part = row[:, 128 * q : 128 * q + 128]
                st[:, 128 * q : 128 * q + 128] = jnp.where(rmap[ey] == part, 1.0, 0.0).astype(BF16)
            tt[...] = dot_nt(abuf[e], st[...]).astype(BF16)
            ap[e] = dot_nn(st[...], tt[...]).astype(BF16)

    def remote(src, dst, ssem, rsem, where):
        copy = pltpu.make_async_remote_copy(
            src_ref=src, dst_ref=dst, send_sem=ssem, recv_sem=rsem, device_id=where, device_id_type=MESH
        )
        copy.start()
        return copy

    x_low, x_high, y_low, y_high = dx > 0, dx < ndx - 1, dy > 0, dy < ndy - 1

    def toward(src, dst, ssem, rsem, sx, sy):
        where = (dx + sx, dy + sy)
        copy = pltpu.make_async_remote_copy(
            src_ref=src, dst_ref=dst, send_sem=ssem, recv_sem=rsem, device_id=where, device_id_type=MESH
        )
        ahead = [f for f in ({1: x_high, -1: x_low}.get(sx), {1: y_high, -1: y_low}.get(sy)) if f is not None]
        behind = [f for f in ({1: x_low, -1: x_high}.get(sx), {1: y_low, -1: y_high}.get(sy)) if f is not None]
        ahead = ahead[0] if len(ahead) == 1 else jnp.logical_and(*ahead)
        behind = behind[0] if len(behind) == 1 else jnp.logical_and(*behind)

        @pl.when(ahead)
        def _():
            copy.start()

        return copy, (sx, sy), ahead, behind

    sent = {}

    def wait(copies):
        for copy, side, ahead, behind in copies:

            @pl.when(behind)
            def _():
                copy.wait_recv()

            sent.setdefault(side, (ahead, []))[1].append(copy)

    def drain():
        for ahead, copies in sent.values():

            @pl.when(ahead)
            def _():
                for copy in copies:
                    copy.wait_send()

    link_load.wait()
    fold(0)
    pl.semaphore_wait(barrier, len(partners))
    halo = []
    for h in range(2):
        half = obuf.at[13, :, :, 128 * h : 128 * h + 128]
        halo.append(
            [
                toward(shc.at[h], hc.at[h], hss.at[h, 2], hrs.at[h, 2], 1, 1),
                toward(shy.at[h], hy.at[h], hss.at[h, 1], hrs.at[h, 1], 0, 1),
                toward(half, hx.at[h], hss.at[h, 0], hrs.at[h, 0], 1, 0),
            ]
        )
    for c in range(1, 4):
        fold(c)

    sub = lax.broadcasted_iota(jnp.int32, (8, 7, 8, 128), 2)

    def apply(src, h):
        for ex in range(2):
            for ez in range(2):
                i0, l0 = 7 * ex, 6 * ez
                rows, layers = slice(i0, i0 + 8), slice(l0, l0 + 7)
                n0 = src[h, rows, layers, 0:8]
                n1 = src[h, rows, layers, 8:16]
                t0 = jnp.where(sub < 7, n0, n1).reshape(448, 128).astype(BF16)
                t1 = jnp.where(sub < 6, n1, n0).reshape(448, 128).astype(BF16)
                p0 = dot_nn(ap[4 * ex + ez], t0).reshape(8, 7, 8, 128)
                p1 = dot_nn(ap[4 * ex + 2 + ez], t1).reshape(8, 7, 8, 128)
                m0 = jnp.where(sub < 7, p0, 0.0) + jnp.where(sub < 6, 0.0, p1)
                m1 = jnp.where(sub < 6, p1, 0.0) + jnp.where(sub < 7, 0.0, p0)
                for part, tile in ((m0, slice(0, 8)), (m1, slice(8, 16))):
                    if ex:
                        first = part[:1, ez:] + acc[h, 7:8, l0 + ez : l0 + 7, tile]
                        rest = jnp.concatenate([first, part[1:, ez:]], axis=0)
                    else:
                        rest = part[:, ez:]
                    if ez:
                        joint = part[:, :1] + acc[h, rows, l0 : l0 + 1, tile]
                        rest = jnp.concatenate([joint, rest], axis=1)
                    acc[h, rows, layers, tile] = rest

    def exchange(t, h):
        copies = []

        def send(n, src, dst, sx, sy):
            copies.append(toward(src, dst, ess.at[t, h, n], ers.at[t, h, n], sx, sy))

        corners = [(0, 15, -1, -1), (14, 13, 1, 1), (0, 13, -1, 1), (14, 15, 1, -1)]
        count = 4 if t < 2 else 1
        for n, (i, slot, sx, sy) in enumerate(corners[:count]):
            scs[t, n, h] = acc2[h, line(i, slot, 1), :].astype(BF16)
        for n, (_, _, sx, sy) in enumerate(corners[:count]):
            send(4 + n, scs.at[t, n, h], rcs.at[t, n, h], sx, sy)
        syl[t, h] = acc2[h, line(0, 15, 15), :].astype(BF16)
        if t < 2:
            syh[t, h] = acc2[h, line(0, 13, 15), :].astype(BF16)
        send(0, syl.at[t, h], ryh.at[t, h], 0, -1)
        if t < 2:
            send(1, syh.at[t, h], ryl.at[t, h], 0, 1)
        sxl[t, h] = acc[h, 0].astype(BF16)
        if t < 2:
            sxh[t, h] = acc[h, 14].astype(BF16)
        send(2, sxl.at[t, h], rxh.at[t, h], -1, 0)
        if t < 2:
            send(3, sxh.at[t, h], rxl.at[t, h], 1, 0)
        return copies

    def gated(flag, value, coef):
        return jnp.where(flag, value.astype(F32), 0.0) * coef

    def faces(t, h, y, y2, coef):
        def bump(i, slot, count, value):
            y2[h, line(i, slot, count), :] += value

        y[h, 14] += gated(x_high, rxh[t, h], coef)
        bump(0, 13, 15, gated(y_high, ryh[t, h], coef))
        bump(14, 13, 1, gated(jnp.logical_and(x_high, y_high), rcs[t, 0, h], coef))
        if t < 2:
            y[h, 0] += rxl[t, h].astype(F32) * coef
            bump(0, 15, 15, ryl[t, h].astype(F32) * coef)
            bump(0, 15, 1, rcs[t, 1, h].astype(F32) * coef)
            bump(14, 15, 1, gated(x_high, rcs[t, 2, h], coef))
            bump(0, 13, 1, gated(y_high, rcs[t, 3, h], coef))
            y[h, 0] = jnp.where(x_low, y[h, 0], 0.0)
            kept = jnp.where(y_low, y2[h, line(0, 15, 15), :], 0.0)
            y2[h, line(0, 15, 15), :] = kept

    stages = []
    for h in range(2):
        wait(halo[h])
        ya[h, 0, :, 0:14, :] = jnp.where(x_low, hx[h].astype(F32), 0.0)
        ya2[h, line(1, 15, 14), :] = jnp.where(y_low, hy[h].astype(F32), 0.0)
        ya2[h, line(0, 15, 1), :] = jnp.where(
            jnp.logical_and(x_low, y_low), hc[h].astype(F32), 0.0
        )
        apply(ya, h)
        stages.append(exchange(0, h))
    for h in range(2):
        yb2[h] = 0.25 * acc2[h] - 0.375 * ya2[h]
    for h in range(2):
        wait(stages[h])
        faces(0, h, yb, yb2, 0.25)
        apply(yb, h)
        stages[h] = exchange(1, h)
    for h in range(2):
        ya2[h] = 0.5 * acc2[h] - 0.75 * yb2[h] - ya2[h]
    for h in range(2):
        wait(stages[h])
        faces(1, h, ya, ya2, 0.5)
        apply(ya, h)
        stages[h] = exchange(2, h)
    for h in range(2):
        yb2[h] = 0.5 * acc2[h] - 0.75 * ya2[h] - yb2[h]

    def parts(y):
        top = y.astype(BF16)
        return top, (y - top.astype(F32)).astype(BF16)

    def gram_of(ref):
        total = dot_tn(ref[:, 0:NB], ref[...])
        cross = total[:, NB:]
        return total[:, 0:NB] + (cross + cross.T)

    slot = lax.broadcasted_iota(jnp.int32, (169, 16, 128), 1)
    for h in range(2):
        inner = jnp.where(slot < 13, yb[h, 1:14].reshape(169, 16, 128), 0.0).reshape(2704, 128)
        top, low = parts(inner)
        both[0:2704, 128 * h : 128 * h + 128] = top
        both[0:2704, NB + 128 * h : NB + 128 * h + 128] = low
        rim[h, 368:384, :] = jnp.zeros((16, 128), F32)
    gram[...] = gram_of(both.at[0:2704])
    for h in range(2):
        wait(stages[h])
        faces(2, h, yb, yb2, 0.5)
        yb2[h, line(0, 15, 15), :] = jnp.zeros((195, 128), F32)
        rim[h, 0:208, :] = yb2[h, 2912:3120, :]
        rim[h, 208:377, :] = yb2[h, line(1, 13, 13), :]
        top, low = parts(rim[h])
        edge[:, 128 * h : 128 * h + 128] = top
        edge[:, NB + 128 * h : NB + 128 * h + 128] = low
    full = gram[...] + gram_of(edge)
    blocks = [full[0:128, 0:128], full[0:128, 128:NB], full[128:NB, 128:NB]]
    gl[...] = jnp.concatenate(blocks, axis=0).reshape(16, 24, 128)

    pending = []
    copies = []
    for d in range(1, ndy):
        peer = lax.rem(dy + d, ndy)
        copies.append(remote(gl.at[peer], ra.at[dy], as_.at[d], ar_.at[d], (dx, peer)))
    for h in range(2):
        top, low = parts(yb2[h, 208:3120, :])
        both[:, 128 * h : 128 * h + 128] = top
        both[:, NB + 128 * h : NB + 128 * h + 128] = low
    keep = pltpu.make_async_copy(both, yout, ysem)
    keep.start()
    drain()
    for copy in copies:
        copy.wait_recv()
    pending += copies
    chunk = gl[dy]
    for d in range(1, ndy):
        chunk += ra[lax.rem(dy + d, ndy)]
    gb[dx] = chunk
    copies = []
    for d in range(1, ndx):
        peer = lax.rem(dx + d, ndx)
        copies.append(remote(gb.at[dx], gb.at[dx], bs_.at[d], br_.at[d], (peer, dy)))
    for copy in copies:
        copy.wait_recv()
    pending += copies
    chunk = gb[0]
    for p in range(1, ndx):
        chunk += gb[p]
    gf[dy] = chunk
    copies = []
    for d in range(1, ndy):
        peer = lax.rem(dy + d, ndy)
        copies.append(remote(gf.at[dy], gf.at[dy], cs_.at[d], cr_.at[d], (dx, peer)))
    for copy in copies:
        copy.wait_recv()
    pending += copies
    grams = gf[...].reshape(384, 128)
    gout[0:128, 0:128] = grams[0:128]
    gout[0:128, 128:NB] = grams[128:NB]
    gout[128:NB, 0:128] = jnp.zeros((128, 128), F32)
    gout[128:NB, 128:NB] = grams[NB:384]
    for copy in pending:
        copy.wait_send()
    keep.wait()


def split3(x):
    a = x.astype(BF16)
    rest = x - a.astype(F32)
    b = rest.astype(BF16)
    return a, b, (rest - b.astype(F32)).astype(BF16)


def factor_inverse(g, work, ones):
    ones[...] = jnp.ones((8, 128), F32)
    one = ones[...]
    rows = lax.broadcasted_iota(jnp.int32, (8, 128), 0)
    lanes = lax.broadcasted_iota(jnp.int32, (8, 128), 1)
    scales = []
    for o in range(8):
        base = 32 * o
        source = g if o == 0 else work
        tiles = [
            [source[base + 8 * t : base + 8 * t + 8, 128 * h : 128 * h + 128] for h in range(2)]
            for t in range(4)
        ]
        factors = []
        half = base // 128
        for s in range(4):
            first = base + 8 * s - 128 * half
            inside = jnp.logical_and(lanes >= first, lanes < first + 8)
            columns = []
            for q in range(s, 4):
                tile = tiles[q][half]
                columns.append(
                    [
                        jnp.broadcast_to(tile[:, first + j : first + j + 1], (8, 128)) * one
                        for j in range(8)
                    ]
                )
                fresh = jnp.where(lanes == rows + first, 1.0, 0.0) if q == s else 0.0
                tiles[q][half] = jnp.where(inside, fresh, tile)
            scale = jnp.ones((8, 128), F32)
            factor = jnp.ones((8, 128), F32)
            for k in range(8):
                lead = [jnp.broadcast_to(columns[0][j][k : k + 1, :], (8, 128)) for j in range(k, 8)]
                inv = 1.0 / lead[0]
                scale = jnp.where(rows == k, lead[0], scale)
                factor = jnp.where(rows == k, inv, factor)
                pivot = [jnp.broadcast_to(tiles[s][h][k : k + 1, :], (8, 128)) * inv for h in range(2)]
                ready = [v * inv for v in lead]
                for q in range(s, 4):
                    if q == s and k == 7:
                        continue
                    column = columns[q - s][k]
                    if q == s:
                        column = jnp.where(rows > k, column, 0.0)
                    for j in range(k + 1, 8):
                        if q == s:
                            change = (column * lead[j - k]) * inv
                        else:
                            change = column * ready[j - k]
                        columns[q - s][j] = columns[q - s][j] - change
                    for h in range(2):
                        tiles[q][h] = tiles[q][h] - column * pivot[h]
            scales.append(lax.rsqrt(scale))
            factors.append(factor)
        for t in range(4):
            for h in range(2):
                work[base + 8 * t : base + 8 * t + 8, 128 * h : 128 * h + 128] = tiles[t][h]
        if o < 7:
            u = jnp.concatenate([jnp.concatenate(tiles[t], axis=1) for t in range(4)], axis=0)
            f = jnp.concatenate([jnp.concatenate([v, v], axis=1) for v in factors], axis=0)
            r = lax.broadcasted_iota(jnp.int32, (32, NB), 0) + base
            c = lax.broadcasted_iota(jnp.int32, (32, NB), 1)
            v = jnp.where(jnp.logical_and(c > r, c < base + 32), 0.0, u * f)
            start = 128 * ((base + 32) // 128)
            u1, u2, u3 = split3(u[:, start:])
            v1, v2, v3 = split3(v)
            left = jnp.concatenate([u1, u1, u1, u2, u2, u3], axis=0)
            right = jnp.concatenate([v1, v2, v3, v1, v2, v1], axis=0)
            change = lax.dot_general(
                left, right, (((0,), (0,)), ((), ())), preferred_element_type=F32
            )
            rest = slice(base + 32, NB)
            old = (g if o == 0 else work)[rest, :]
            cc = lax.broadcasted_iota(jnp.int32, old.shape, 1)
            old = jnp.where(jnp.logical_and(cc >= base, cc < base + 32), 0.0, old)
            work[rest, :] = old - change[base + 32 - start :, :]
    for t in range(32):
        for h in range(2):
            tile = work[8 * t : 8 * t + 8, 128 * h : 128 * h + 128] * scales[t]
            work[8 * t : 8 * t + 8, 128 * h : 128 * h + 128] = jnp.where(
                lanes + 128 * h <= rows + 8 * t, tile, 0.0
            )


def basis_kernel(scale, y, g, out, ybuf, stage, work, ones, weights, yin, osem):
    load = pltpu.make_async_copy(y, ybuf, yin)
    load.start()
    factor_inverse(g, work, ones)
    w = work[...].T * scale
    top = w.astype(BF16)
    weights[0:NB] = top
    weights[NB : 2 * NB] = top
    weights[2 * NB :] = (w - top.astype(F32)).astype(BF16)
    load.wait()
    copies = []
    for start, count in ((0, 2), (2, 4), (6, 4), (10, 3), (13, 1)):
        rows = slice(208 * start, 208 * (start + count))
        left = jnp.concatenate([ybuf[rows, :], ybuf[rows, 0:NB]], axis=1)
        q = dot_nn(left, weights[...]).reshape(count, 13, 16, NB)
        planes = slice(start, start + count)
        stage[planes] = q[:, :, 0:14, :]
        copy = pltpu.make_async_copy(stage.at[planes], out.at[planes], osem.at[start])
        copy.start()
        copies.append(copy)
    for copy in copies:
        copy.wait()


def solution(mesh):
    ndx, ndy = mesh.shape["dx"], mesh.shape["dy"]
    vmem = pl.BlockSpec(memory_space=pltpu.VMEM)
    anywhere = pl.BlockSpec(memory_space=pl.ANY)
    scale = math.sqrt(14 * 14 * 13 * ndx * ndy)

    def shards(orbitals, elem_mats, conn):
        dma = pltpu.SemaphoreType.DMA
        y, g = pl.pallas_call(
            lambda *refs: filter_kernel(ndx, ndy, *refs),
            out_shape=(
                jax.ShapeDtypeStruct((2912, 2 * NB), BF16),
                jax.ShapeDtypeStruct((NB, NB), F32),
            ),
            in_specs=[anywhere, anywhere, anywhere],
            out_specs=(anywhere, vmem),
            scratch_shapes=[
                pltpu.VMEM((14, 13, 14, NB), BF16),
                pltpu.VMEM((2, 2, 2, 512), jnp.int32),
                pltpu.VMEM((8, 512, 512), BF16),
                pltpu.VMEM((8, 448, 448), BF16),
                pltpu.VMEM((2, 448, 128), jnp.int32),
                pltpu.VMEM((448, 512), BF16),
                pltpu.VMEM((512, 448), BF16),
                pltpu.VMEM((2, 3120, 128), F32),
                pltpu.VMEM((2, 3120, 128), F32),
                pltpu.VMEM((2, 3120, 128), F32),
                pltpu.VMEM((2912, 2 * NB), BF16),
                pltpu.VMEM((2, 384, 128), F32),
                pltpu.VMEM((384, 2 * NB), BF16),
                pltpu.VMEM((NB, NB), F32),
                pltpu.VMEM((2, 13, 14, 128), BF16),
                pltpu.VMEM((2, 182, 128), BF16),
                pltpu.VMEM((2, 13, 128), BF16),
                pltpu.VMEM((2, 182, 128), BF16),
                pltpu.VMEM((2, 13, 128), BF16),
                pltpu.VMEM((3, 2, 13, 16, 128), BF16),
                pltpu.VMEM((2, 2, 13, 16, 128), BF16),
                pltpu.VMEM((3, 2, 195, 128), BF16),
                pltpu.VMEM((2, 2, 195, 128), BF16),
                pltpu.VMEM((3, 4, 2, 13, 128), BF16),
                pltpu.VMEM((2, 2, 13, 16, 128), BF16),
                pltpu.VMEM((3, 2, 13, 16, 128), BF16),
                pltpu.VMEM((2, 2, 195, 128), BF16),
                pltpu.VMEM((3, 2, 195, 128), BF16),
                pltpu.VMEM((3, 4, 2, 13, 128), BF16),
                pltpu.VMEM((16, 24, 128), F32),
                pltpu.VMEM((16, 24, 128), F32),
                pltpu.VMEM((8, 24, 128), F32),
                pltpu.VMEM((16, 24, 128), F32),
                dma,
                dma,
                dma((8,)),
                dma,
                dma((2, 3)),
                dma((2, 3)),
                dma((3, 2, 8)),
                dma((3, 2, 8)),
                dma((16,)),
                dma((16,)),
                dma((8,)),
                dma((8,)),
                dma((16,)),
                dma((16,)),
            ],
            compiler_params=pltpu.CompilerParams(collective_id=0, has_side_effects=True),
            name="filter",
        )(jnp.swapaxes(orbitals, 1, 2), elem_mats, conn)
        filtered = pl.pallas_call(
            lambda *refs: basis_kernel(scale, *refs),
            out_shape=jax.ShapeDtypeStruct((14, 13, 14, NB), F32),
            in_specs=[anywhere, vmem],
            out_specs=anywhere,
            scratch_shapes=[
                pltpu.VMEM((2912, 2 * NB), BF16),
                pltpu.VMEM((14, 13, 14, NB), F32),
                pltpu.VMEM((NB, NB), F32),
                pltpu.VMEM((8, 128), F32),
                pltpu.VMEM((3 * NB, NB), BF16),
                dma,
                dma((14,)),
            ],
            name="basis",
        )(y, g)
        return jnp.swapaxes(filtered, 1, 2)

    in_specs = (
        P("dx", "dy", None, None),
        P("dx", "dy", None, None, None),
        P("dx", "dy", None, None),
    )
    out_specs = P("dx", "dy", None, None)
    return jax.shard_map(shards, mesh=mesh, in_specs=in_specs, out_specs=out_specs, check_vma=False)
```
